32 devices in a mesh: quad: 2 (over x), py: 4 (over y, core), pz: 4 (over z).
Axes of the slice: x: 2, y: 2, z: 4, core: 2. Of those that a mesh axis runs over, the one named last changes fastest.
Arguments:
- source_real: float32 [4, 16, 64, 512], P(None, None, 'py', 'pz'), may hold values from -6 to 6
- source_imag: float32 [4, 16, 64, 512], P(None, None, 'py', 'pz'), may hold values from -2 to 2
- potential: float32 [16, 64, 512], P(None, 'py', 'pz'), may hold values from 0 to 2
- center: float32 [1], replicated, may hold values from 4.5 to 6
- radius: float32 [1], replicated, may hold values from 1 to 2
Outputs:
- moments: float32 [4, 2, 4, 16, 64, 512], P(None, None, None, 'quad', 'py', 'pz')
The draws below stay inside these ranges and needn't reach their ends.
All inputs are finite; a program needn't handle non-finite values.
Results may differ from the reference program's by a relative error of at most 0.0003.
Values sent between devices are 32-bit elements; how exact they have to be, the bound alone decides.
No kernel may reach another device: no remote copies, remote signals or barrier semaphores. Data moves between devices by JAX's collectives and lax.ppermute only.
A program may use at most 256 MiB of HBM per device.

```python
import math
import jax
import jax.numpy as jnp

CX = 16
SRC = 4
QPTS = 8
MOMS = 4
NY = 64
NZ = 512


def levels(own_key, shape, pieces, least, largest):
    def one(axis_at, blocks):
        heights = jax.random.uniform(jax.random.fold_in(jax.random.fold_in(own_key, 6), axis_at), (blocks,), jnp.float32, least / len(pieces), largest / len(pieces))
        return jnp.repeat(jnp.exp(heights), shape[axis_at] // blocks).reshape((-1,) + (1,) * (len(shape) - axis_at - 1))

    level = one(*pieces[0])
    for cut in pieces[1:]:
        level = level * one(*cut)
    return level


def normal_values(stream_key, dims, width, most, cuts=(), kind=jnp.bfloat16):
    entries = jax.random.normal(stream_key, dims, jnp.float32) * width
    if len(cuts) > 0:
        entries = levels(stream_key, dims, cuts, -0.22, 0.18) * entries
    return jnp.clip(entries, min=-most, max=most).astype(kind)


def setup_inputs(seed: int = 0) -> dict:
    seeds = jax.random.split(jax.random.key(seed), 6)
    source_real = normal_values(seeds[0], (SRC, CX, NY, NZ), 1.0, 6.0, ((2, 4), (3, 4)), jnp.float32)
    source_imag = normal_values(seeds[1], (SRC, CX, NY, NZ), 0.3, 2.0, ((2, 4), (3, 4)), jnp.float32)
    potential = jnp.clip(2.0 * jax.random.uniform(seeds[2], (CX, NY, NZ), jnp.float32) ** levels(seeds[2], (CX, NY, NZ), ((1, 4), (2, 4)), -0.2, 0.2), 0.0, 2.0)
    center = jnp.clip(jax.random.uniform(seeds[3], (1,), jnp.float32, 4.5, 6.0), 4.5, 6.0)
    radius = jnp.clip(jax.random.uniform(seeds[4], (1,), jnp.float32, 1.0, 2.0), 1.0, 2.0)
    return dict(source_real=source_real, source_imag=source_imag, potential=potential, center=center, radius=radius)


stencil_weights = (-205.0 / 72.0, 8.0 / 5.0, -1.0 / 5.0, 8.0 / 315.0, -1.0 / 560.0)


def hamiltonian(field, potential):
    laplace = 3.0 * stencil_weights[0] * field
    for offset in range(1, 5):
        beside_all = jnp.roll(field, offset, -3) + jnp.roll(field, -offset, -3)
        beside_all = beside_all + jnp.roll(field, offset, -2) + jnp.roll(field, -offset, -2)
        beside_all = beside_all + jnp.roll(field, offset, -1) + jnp.roll(field, -offset, -1)
        laplace = laplace + stencil_weights[offset] * beside_all
    return -0.5 * laplace + potential * field


def complex_mul(left, right):
    return (left[0] * right[0] - left[1] * right[1], left[0] * right[1] + left[1] * right[0])


def complex_div(left, right):
    norm_sq = right[0] * right[0] + right[1] * right[1]
    return ((left[0] * right[0] + left[1] * right[1]) / norm_sq, (left[1] * right[0] - left[0] * right[1]) / norm_sq)


def bilinear(left, right):
    both = complex_mul(left, right)
    return (jnp.sum(both[0], axis=(-3, -2, -1)), jnp.sum(both[1], axis=(-3, -2, -1)))


def spread(value):
    return (value[0][..., None, None, None], value[1][..., None, None, None])


def reference(source_real, source_imag, potential, center, radius):
    source = (source_real, source_imag)
    applied = hamiltonian(jnp.stack(source), potential)
    hsource = (applied[0], applied[1])
    rho_first = bilinear(source, source)
    curv_first = bilinear(source, hsource)
    orders = jnp.arange(1, MOMS + 1).astype(jnp.float32)
    moment_re = jnp.zeros((MOMS,) + source_real.shape, jnp.float32)
    moment_im = jnp.zeros((MOMS,) + source_real.shape, jnp.float32)
    for point in range(QPTS):
        angle = 2.0 * math.pi * (point + 0.5) / QPTS
        shift = (center[0] + radius[0] * math.cos(angle), radius[0] * math.sin(angle))
        scaled = complex_mul(shift, rho_first)
        denom = (scaled[0] - curv_first[0], scaled[1] - curv_first[1])
        alpha_first = spread(complex_div(rho_first, denom))
        first_iterate = complex_mul(alpha_first, source)
        shifted = complex_mul(shift, source)
        image = (shifted[0] - hsource[0], shifted[1] - hsource[1])
        moved = complex_mul(alpha_first, image)
        residual = (source[0] - moved[0], source[1] - moved[1])
        rho_next = bilinear(residual, residual)
        beta = spread(complex_div(rho_next, rho_first))
        carried = complex_mul(beta, source)
        direction = (residual[0] + carried[0], residual[1] + carried[1])
        happ = hamiltonian(jnp.stack(direction), potential)
        shifted_dir = complex_mul(shift, direction)
        image_next = (shifted_dir[0] - happ[0], shifted_dir[1] - happ[1])
        alpha_next = spread(complex_div(rho_next, bilinear(direction, image_next)))
        step_part = complex_mul(alpha_next, direction)
        solution = (first_iterate[0] + step_part[0], first_iterate[1] + step_part[1])
        weight_re = (radius[0] / QPTS) * jnp.cos(orders * angle)
        weight_im = (radius[0] / QPTS) * jnp.sin(orders * angle)
        weight_re = weight_re[:, None, None, None, None]
        weight_im = weight_im[:, None, None, None, None]
        moment_re = moment_re + (weight_re * solution[0][None] - weight_im * solution[1][None])
        moment_im = moment_im + (weight_re * solution[1][None] + weight_im * solution[0][None])
    return jnp.stack([moment_re, moment_im], 1)
```

```python
import functools
import math

import jax
import jax.numpy as jnp
import numpy as np
from jax import lax
from jax.experimental import pallas as pl
from jax.experimental.pallas import tpu as pltpu
from jax.sharding import PartitionSpec as P

QPTS = 8
MOMS = 4
REACH = 4
LANES = 128

stencil_weights = (-205.0 / 72.0, 8.0 / 5.0, -1.0 / 5.0, 8.0 / 315.0, -1.0 / 560.0)
DIAG = -1.5 * stencil_weights[0]
SIDE = tuple(-0.5 * w for w in stencil_weights)
HIGHEST = lax.Precision.HIGHEST


def dot(left, right, dims):
    return lax.dot_general(
        left, right, (dims, ((), ())), precision=HIGHEST, preferred_element_type=jnp.float32
    )


def band(shape, offset, signs, scale=1.0):
    step = offset + lax.broadcasted_iota(jnp.int32, shape, 0) - lax.broadcasted_iota(jnp.int32, shape, 1)
    out = jnp.zeros(shape, jnp.float32)
    for k in range(1, REACH + 1):
        for sign in signs:
            out = jnp.where(step == sign * k, scale * SIDE[k], out)
    return out


def edge_select(width):
    row = lax.broadcasted_iota(jnp.int32, (2 * REACH, width), 0)
    col = lax.broadcasted_iota(jnp.int32, (2 * REACH, width), 1)
    want = jnp.where(row < REACH, row, width - 2 * REACH + row)
    return jnp.where(col == want, 1.0, 0.0)


def pack_kernel(re_ref, im_ref, ylo_ref, yhi_ref, zlo_ref, zhi_ref):
    srcs, cx, ny, nz = re_ref.shape
    pick = edge_select(nz)
    for part, ref in enumerate((re_ref, im_ref)):
        for s in range(srcs):
            f = part * srcs + s
            ylo_ref[f] = ref[s, :, 0:REACH, :]
            yhi_ref[f] = ref[s, :, ny - REACH : ny, :]
            edges = dot(pick, ref[s].reshape(cx * ny, nz), ((1,), (1,)))
            zlo_ref[f * REACH : (f + 1) * REACH, :] = edges[0:REACH]
            zhi_ref[f * REACH : (f + 1) * REACH, :] = edges[REACH : 2 * REACH]


def inner_kernel(center_ref, re_ref, im_ref, pot_ref, out_ref, pad_ref):
    srcs, cx, ny, nz = re_ref.shape
    shift = DIAG - center_ref[0]
    matrix = band((nz, nz), 0, (1, -1))
    zero = jnp.zeros((cx, 8, nz), jnp.float32)
    pad_ref[:, 0:8, :] = zero
    pad_ref[:, 8 + ny : 16 + ny, :] = zero
    for part, ref in enumerate((re_ref, im_ref)):

        def field(s, _, ref=ref, part=part):
            f = part * srcs + s
            own = ref[s]
            pad_ref[:, 8 : 8 + ny, :] = own
            out_ref[f] = dot(own.reshape(cx * ny, nz), matrix, ((1,), (0,))).reshape(cx, ny, nz)
            for x in range(cx):
                total = out_ref[f, x] + (pot_ref[x] + shift) * ref[s, x]
                for k in range(1, REACH + 1):
                    beside = ref[s, (x + k) % cx] + ref[s, (x - k) % cx]
                    beside = beside + pad_ref[x, 8 + k : 8 + k + ny, :]
                    beside = beside + pad_ref[x, 8 - k : 8 - k + ny, :]
                    total = total + SIDE[k] * beside
                out_ref[f, x] = total
            return 0

        lax.fori_loop(0, srcs, field, 0)


def border_kernel(inner_ref, ylo_ref, yhi_ref, zlo_ref, zhi_ref, out_ref, oy_ref, oz_ref, own_ref, pad_ref):
    fields, cx, ny, nz = inner_ref.shape
    below = band((REACH, nz), -REACH, (1, -1))
    above = band((REACH, nz), nz, (1, -1))
    pick = edge_select(nz)
    zero = jnp.zeros((cx, 16, nz), jnp.float32)
    pad_ref[0] = zero
    pad_ref[1] = zero

    def field(f, _):
        at = pl.multiple_of(f * REACH, REACH)
        fix = dot(zlo_ref[f], below, ((0,), (0,))) + dot(zhi_ref[f], above, ((0,), (0,)))
        out_ref[f] = inner_ref[f] + fix.reshape(cx, ny, nz)
        pad_ref[0, :, 8 - REACH : 8, :] = ylo_ref[f]
        pad_ref[1, :, 8 : 8 + REACH, :] = yhi_ref[f]
        for x in range(cx):
            low = out_ref[f, x, 0:8, :]
            high = out_ref[f, x, ny - 8 : ny, :]
            for k in range(1, REACH + 1):
                low = low + SIDE[k] * pad_ref[0, x, 8 - k : 16 - k, :]
                high = high + SIDE[k] * pad_ref[1, x, k : 8 + k, :]
            out_ref[f, x, 0:8, :] = low
            out_ref[f, x, ny - 8 : ny, :] = high
        oy_ref[f] = out_ref[f, :, 0:REACH, :]
        edges = dot(pick, out_ref[f].reshape(cx * ny, nz), ((1,), (1,)))
        oz_ref[f] = edges[0:REACH]
        own_ref[f] = edges[REACH : 2 * REACH]
        return 0

    lax.fori_loop(0, fields, field, 0)


def fold(value):
    return jnp.sum(value, axis=0, keepdims=True)


def sums_kernel(center_ref, re_ref, im_ref, pot_ref, h_ref, acc_ref, step_ref):
    srcs, cx, ny, nz = re_ref.shape
    shift = DIAG - center_ref[0]
    matrix = band((nz, nz), 0, (1,), 2.0)
    row = lax.broadcasted_iota(jnp.int32, (ny, nz), 0)
    inside = [row < ny - k for k in range(REACH + 1)]
    for s in range(srcs):
        for part in range(2):
            f = part * srcs + s
            step_ref[part] = dot(h_ref[f].reshape(cx * ny, nz), matrix, ((1,), (0,))).reshape(cx, ny, nz)
        total = [jnp.zeros((ny, nz), jnp.float32) for _ in range(8)]
        for x in range(cx):
            local = pot_ref[x] + shift
            br, bi = re_ref[s, x], im_ref[s, x]
            h, g = [], []
            for part in range(2):
                f = part * srcs + s
                own = h_ref[f, x]
                image = step_ref[part, x] + local * own
                for k in range(1, REACH + 1):
                    up = jnp.where(inside[k], pltpu.roll(own, ny - k, 0), 0.0)
                    image = image + (2.0 * SIDE[k]) * (h_ref[f, (x + k) % cx] + up)
                h.append(own)
                g.append(image)
            terms = (
                br * br - bi * bi,
                2.0 * (br * bi),
                br * h[0] - bi * h[1],
                br * h[1] + bi * h[0],
                h[0] * h[0] - h[1] * h[1],
                2.0 * (h[0] * h[1]),
                h[0] * g[0] - h[1] * g[1],
                h[0] * g[1] + h[1] * g[0],
            )
            total = [t + v for t, v in zip(total, terms)]
        for i in range(8):
            acc_ref[i * srcs + s : i * srcs + s + 1, :] = fold(total[i])


def finish_kernel(acc_ref, h_ref, own_ref, yhi_ref, zhi_ref, out_ref, pad_ref):
    fields, cx, ny, nz = h_ref.shape
    srcs = fields // 2
    i = lax.broadcasted_iota(jnp.int32, (REACH, REACH), 0)
    j = lax.broadcasted_iota(jnp.int32, (REACH, REACH), 1)
    mix = jnp.zeros((REACH, REACH), jnp.float32)
    for k in range(1, REACH + 1):
        mix = jnp.where(j - i + REACH == k, 2.0 * SIDE[k], mix)
    out_ref[...] = acc_ref[...]
    pad_ref[...] = jnp.zeros(pad_ref.shape, jnp.float32)
    for s in range(srcs):
        edge = [own_ref[part * srcs + s] for part in range(2)]
        far = [dot(mix, zhi_ref[part * srcs + s], ((1,), (0,))) for part in range(2)]
        both = (edge[0] * far[0] - edge[1] * far[1], edge[0] * far[1] + edge[1] * far[0])
        sides = []
        for c in range(2):
            flat = fold(both[c])
            width = flat.shape[1]
            sides.append(sum(flat[:, at : at + nz] for at in range(0, width, nz)))
        total = [jnp.zeros((8, nz), jnp.float32) for _ in range(2)]
        for part in range(2):
            pad_ref[part, :, 8 : 8 + REACH, :] = yhi_ref[part * srcs + s]
        for x in range(cx):
            h = [h_ref[part * srcs + s, x, ny - 8 : ny, :] for part in range(2)]
            g = []
            for part in range(2):
                image = (2.0 * SIDE[1]) * pad_ref[part, x, 1:9, :]
                for k in range(2, REACH + 1):
                    image = image + (2.0 * SIDE[k]) * pad_ref[part, x, k : 8 + k, :]
                g.append(image)
            total[0] = total[0] + (h[0] * g[0] - h[1] * g[1])
            total[1] = total[1] + (h[0] * g[1] + h[1] * g[0])
        for c in range(2):
            at = (6 + c) * srcs + s
            out_ref[at : at + 1, :] = out_ref[at : at + 1, :] + fold(total[c]) + sides[c]


def complex_mul(left, right):
    return (left[0] * right[0] - left[1] * right[1], left[0] * right[1] + left[1] * right[0])


def complex_div(left, right):
    norm_sq = right[0] * right[0] + right[1] * right[1]
    return (
        (left[0] * right[0] + left[1] * right[1]) / norm_sq,
        (left[1] * right[0] - left[0] * right[1]) / norm_sq,
    )


def phase_table():
    lane = np.arange(LANES)
    angle = 2.0 * math.pi * (lane % QPTS + 0.5) / QPTS
    rows = [np.cos(angle), np.sin(angle)]
    for k in range(1, MOMS + 1):
        rows.append(np.where(lane < QPTS, np.cos(k * angle), 0.0) / QPTS)
        rows.append(np.where(lane < QPTS, np.sin(k * angle), 0.0) / QPTS)
    while len(rows) % 8:
        rows.append(np.zeros(LANES))
    return np.stack(rows).astype(np.float32)


def output_kernel(quad_ref, radius_ref, tot_ref, table_ref, re_ref, im_ref, hr_ref, hi_ref, out_ref, coef_ref):
    srcs = tot_ref.shape[0] // 8
    s = pl.program_id(0)

    @pl.when(s == 0)
    def _():
        radius = radius_ref[0]
        summed = jnp.sum(tot_ref[...], axis=1, keepdims=True)
        wide = jnp.broadcast_to(summed, (8 * srcs, LANES))
        nu = [
            (wide[2 * k * srcs : (2 * k + 1) * srcs], wide[(2 * k + 1) * srcs : (2 * k + 2) * srcs])
            for k in range(4)
        ]
        shape = (srcs, LANES)
        zeta = (
            jnp.broadcast_to(radius * table_ref[0:1, :], shape),
            jnp.broadcast_to(radius * table_ref[1:2, :], shape),
        )
        scaled = complex_mul(zeta, nu[0])
        alpha_first = complex_div(nu[0], (scaled[0] - nu[1][0], scaled[1] - nu[1][1]))
        mean = complex_div(nu[1], nu[0])
        t = complex_mul(mean, nu[1])
        spread2 = (nu[2][0] - t[0], nu[2][1] - t[1])
        t = complex_mul(mean, (nu[2][0] + spread2[0], nu[2][1] + spread2[1]))
        spread3 = (nu[3][0] - t[0], nu[3][1] - t[1])
        square = complex_mul(alpha_first, alpha_first)
        rho_next = complex_mul(square, spread2)
        beta = complex_div(rho_next, nu[0])
        first = complex_mul(zeta, rho_next)
        second = complex_mul(square, spread3)
        third = complex_div(complex_mul(beta, rho_next), alpha_first)
        alpha_next = complex_div(
            rho_next, (first[0] - second[0] - third[0], first[1] - second[1] - third[1])
        )
        t = complex_mul(alpha_first, mean)
        carried = complex_mul(alpha_next, (beta[0] - t[0], beta[1] - t[1]))
        on_source = (alpha_first[0] + carried[0], alpha_first[1] + carried[1])
        on_image = complex_mul(alpha_next, alpha_first)
        for k in range(MOMS):
            weight = (
                jnp.broadcast_to(radius * table_ref[2 + 2 * k : 3 + 2 * k, :], shape),
                jnp.broadcast_to(radius * table_ref[3 + 2 * k : 4 + 2 * k, :], shape),
            )
            for n, value in enumerate((on_source, on_image)):
                both = complex_mul(weight, value)
                for c in range(2):
                    column = jnp.sum(both[c], axis=1, keepdims=True)
                    coef_ref[4 * k + 2 * n + c, 0:srcs, :] = jnp.broadcast_to(column, shape)

    planes = re_ref.shape[1]
    plane = re_ref.shape[2:]
    for k in range(MOMS):
        c = [jnp.broadcast_to(coef_ref[4 * k + n, pl.ds(s, 1), :], plane) for n in range(4)]
        for x in range(planes):
            br, bi, hr, hi = re_ref[0, x], im_ref[0, x], hr_ref[0, x], hi_ref[0, x]
            out_ref[k, 0, 0, x] = c[0] * br - c[1] * bi + (c[2] * hr - c[3] * hi)
            out_ref[k, 1, 0, x] = c[0] * bi + c[1] * br + (c[2] * hi + c[3] * hr)


def ring(count, step):
    return [(i, (i + step) % count) for i in range(count)]


def total_over(value, axis):
    count = lax.axis_size(axis)
    if count & (count - 1):
        return lax.psum(value, axis)
    bit = 1
    while bit < count:
        value = value + lax.ppermute(value, axis, [(i, i ^ bit) for i in range(count)])
        bit *= 2
    return value


VMEM = pl.BlockSpec(memory_space=pltpu.VMEM)
SMEM = pl.BlockSpec(memory_space=pltpu.SMEM)


def shaped(*dims):
    return jax.ShapeDtypeStruct(dims, jnp.float32)


def cost(flops, nbytes):
    return pl.CostEstimate(flops=flops, bytes_accessed=nbytes, transcendentals=0)


def per_device(source_real, source_imag, potential, center, radius):
    srcs, cx, ny, nz = source_real.shape
    fields = 2 * srcs
    cells = cx * ny * nz
    py, pz, quads = lax.axis_size("py"), lax.axis_size("pz"), lax.axis_size("quad")

    ylo, yhi, zlo, zhi = pl.pallas_call(
        pack_kernel,
        out_shape=(
            shaped(fields, cx, REACH, nz),
            shaped(fields, cx, REACH, nz),
            shaped(fields * REACH, cx * ny),
            shaped(fields * REACH, cx * ny),
        ),
        in_specs=[VMEM] * 2,
        out_specs=(VMEM,) * 4,
        name="pack",
    )(source_real, source_imag)
    y_above = lax.ppermute(ylo, "py", ring(py, -1))
    y_below = lax.ppermute(yhi, "py", ring(py, 1))
    z_above = lax.ppermute(zlo, "pz", ring(pz, -1)).reshape(fields, REACH, cx * ny)
    z_below = lax.ppermute(zhi, "pz", ring(pz, 1)).reshape(fields, REACH, cx * ny)

    inner = pl.pallas_call(
        inner_kernel,
        out_shape=shaped(fields, cx, ny, nz),
        in_specs=[SMEM] + [VMEM] * 3,
        out_specs=VMEM,
        scratch_shapes=[pltpu.VMEM((cx, ny + 16, nz), jnp.float32)],
        cost_estimate=cost(fields * cells * 60, fields * cells * 12),
        name="inner",
    )(center, source_real, source_imag, potential)

    image, h_ylo, h_zlo, h_own = pl.pallas_call(
        border_kernel,
        out_shape=(
            shaped(fields, cx, ny, nz),
            shaped(fields, cx, REACH, nz),
            shaped(fields, REACH, cx * ny),
            shaped(fields, REACH, cx * ny),
        ),
        in_specs=[VMEM] * 5,
        out_specs=(VMEM,) * 4,
        scratch_shapes=[pltpu.VMEM((2, cx, 16, nz), jnp.float32)],
        name="border",
    )(inner, y_below, y_above, z_below, z_above)
    h_yabove = lax.ppermute(h_ylo, "py", ring(py, -1))
    h_zabove = lax.ppermute(h_zlo, "pz", ring(pz, -1))

    partial = pl.pallas_call(
        sums_kernel,
        out_shape=shaped(8 * srcs, nz),
        in_specs=[SMEM] + [VMEM] * 4,
        out_specs=VMEM,
        scratch_shapes=[pltpu.VMEM((2, cx, ny, nz), jnp.float32)],
        cost_estimate=cost(fields * cells * 60, fields * cells * 12),
        name="sums",
    )(center, source_real, source_imag, potential, image)

    partial = pl.pallas_call(
        finish_kernel,
        out_shape=shaped(8 * srcs, nz),
        in_specs=[VMEM] * 5,
        out_specs=VMEM,
        scratch_shapes=[pltpu.VMEM((2, cx, 16, nz), jnp.float32)],
        name="finish",
    )(partial, image, h_own, h_yabove, h_zabove)

    total = total_over(total_over(partial, "py"), "pz")

    planes = cx // quads
    quad = lax.axis_index("quad").reshape(1)
    table = jnp.asarray(phase_table())
    own = lambda shift: pl.BlockSpec((1, planes, ny, nz), lambda s, q: (s + shift, q[0], 0, 0))
    return pl.pallas_call(
        output_kernel,
        out_shape=shaped(MOMS, 2, srcs, planes, ny, nz),
        grid_spec=pltpu.PrefetchScalarGridSpec(
            num_scalar_prefetch=1,
            grid=(srcs,),
            in_specs=[
                SMEM,
                pl.BlockSpec(total.shape, lambda s, q: (0, 0)),
                pl.BlockSpec(table.shape, lambda s, q: (0, 0)),
                own(0),
                own(0),
                own(0),
                own(srcs),
            ],
            out_specs=pl.BlockSpec((MOMS, 2, 1, planes, ny, nz), lambda s, q: (0, 0, s, 0, 0, 0)),
            scratch_shapes=[pltpu.VMEM((4 * MOMS, 8, LANES), jnp.float32)],
        ),
        compiler_params=pltpu.CompilerParams(dimension_semantics=("arbitrary",)),
        name="output",
    )(quad, radius, total, table, source_real, source_imag, image, image)


def solution(mesh):
    in_specs = (P(None, None, "py", "pz"), P(None, None, "py", "pz"), P(None, "py", "pz"), P(), P())
    out_specs = P(None, None, None, "quad", "py", "pz")
    return jax.shard_map(
        per_device, mesh=mesh, in_specs=in_specs, out_specs=out_specs, check_vma=False
    )
```

```python
import functools
import math

import jax
import jax.numpy as jnp
import numpy as np
from jax import lax
from jax.experimental import pallas as pl
from jax.experimental.pallas import tpu as pltpu
from jax.sharding import PartitionSpec as P

QPTS = 8
MOMS = 4
REACH = 4
LANES = 128

stencil_weights = (-205.0 / 72.0, 8.0 / 5.0, -1.0 / 5.0, 8.0 / 315.0, -1.0 / 560.0)
DIAG = -1.5 * stencil_weights[0]
SIDE = tuple(-0.5 * w for w in stencil_weights)
HIGHEST = lax.Precision.HIGHEST


def dot(left, right, dims):
    return lax.dot_general(
        left, right, (dims, ((), ())), precision=HIGHEST, preferred_element_type=jnp.float32
    )


def band(shape, offset, signs, scale=1.0):
    step = offset + lax.broadcasted_iota(jnp.int32, shape, 0) - lax.broadcasted_iota(jnp.int32, shape, 1)
    out = jnp.zeros(shape, jnp.float32)
    for k in range(1, REACH + 1):
        for sign in signs:
            out = jnp.where(step == sign * k, scale * SIDE[k], out)
    return out


def split(value):
    high = value.astype(jnp.bfloat16)
    return high, (value - high.astype(jnp.float32)).astype(jnp.bfloat16)


def dot_split(left, right):
    return mul(left[0], right[0]) + (mul(left[0], right[1]) + mul(left[1], right[0]))


def mul(left, right):
    return lax.dot_general(left, right, (((1,), (0,)), ((), ())), preferred_element_type=jnp.float32)


def gather_edges(gathered, f, value):
    lane = lax.broadcasted_iota(jnp.int32, value.shape, 1)
    moved = pltpu.roll(value, 2 * REACH * f + REACH, 1)
    return jnp.where(lane // (2 * REACH) == f, moved, gathered)


def store_edges(gathered, fields, low_ref, high_ref):
    turned = gathered.T
    for f in range(fields):
        at = 2 * REACH * f
        high_ref[f * REACH : (f + 1) * REACH, :] = turned[at : at + REACH]
        low_ref[f * REACH : (f + 1) * REACH, :] = turned[at + REACH : at + 2 * REACH]


def load_kernel(
    re_hbm, im_hbm, pot_hbm, b_ref, pot_ref, ylo_ref, yhi_ref, zlo_ref, zhi_ref, edge_ref, sems
):
    fields, cx, ny, nz = b_ref.shape
    srcs = fields // 2
    copies = [
        pltpu.make_async_copy(hbm.at[s], b_ref.at[part * srcs + s], sems.at[part * srcs + s])
        for part, hbm in enumerate((re_hbm, im_hbm))
        for s in range(srcs)
    ]
    copies.append(pltpu.make_async_copy(pot_hbm, pot_ref, sems.at[fields]))
    for copy in copies:
        copy.start()
    edge_ref[...] = jnp.zeros(edge_ref.shape, jnp.float32)
    for f in range(fields):
        copies[f].wait()
        ylo_ref[f] = b_ref[f, :, 0:REACH, :]
        yhi_ref[f] = b_ref[f, :, ny - REACH : ny, :]
        edge_ref[...] = gather_edges(edge_ref[...], f, b_ref[f].reshape(cx * ny, nz))
    store_edges(edge_ref[...], fields, zlo_ref, zhi_ref)
    copies[fields].wait()


def inner_kernel(center_ref, b_ref, pot_ref, out_ref, pad_ref):
    fields, cx, ny, nz = b_ref.shape
    shift = DIAG - center_ref[0]
    matrix = split(band((nz, nz), 0, (1, -1)))
    zero = jnp.zeros((cx, 8, nz), jnp.float32)
    pad_ref[:, 0:8, :] = zero
    pad_ref[:, 8 + ny : 16 + ny, :] = zero

    def field(f, _):
        own = b_ref[f]
        pad_ref[:, 8 : 8 + ny, :] = own
        out_ref[f] = dot_split(split(own.reshape(cx * ny, nz)), matrix).reshape(cx, ny, nz)
        for x in range(cx):
            total = out_ref[f, x] + (pot_ref[x] + shift) * b_ref[f, x]
            for k in range(1, REACH + 1):
                beside = b_ref[f, (x + k) % cx] + b_ref[f, (x - k) % cx]
                beside = beside + pad_ref[x, 8 + k : 8 + k + ny, :]
                beside = beside + pad_ref[x, 8 - k : 8 - k + ny, :]
                total = total + SIDE[k] * beside
            out_ref[f, x] = total
        return 0

    lax.fori_loop(0, fields, field, 0)


def border_kernel(
    inner_ref, ylo_ref, yhi_ref, zlo_ref, zhi_ref, out_ref, oy_ref, oz_ref, own_ref, pad_ref, edge_ref
):
    fields, cx, ny, nz = inner_ref.shape
    rows = fields * REACH
    turned = split(jnp.concatenate([zlo_ref[...], zhi_ref[...]], axis=0).T)
    row = lax.broadcasted_iota(jnp.int32, (2 * rows, nz), 0)
    col = lax.broadcasted_iota(jnp.int32, (2 * rows, nz), 1)
    step = jnp.where(row < rows, row % REACH - REACH, nz + row % REACH) - col
    base = jnp.zeros((2 * rows, nz), jnp.float32)
    for k in range(1, REACH + 1):
        base = jnp.where(jnp.abs(step) == k, SIDE[k], base)
    owner = (row % rows) // REACH
    for f in range(fields):
        weights = split(jnp.where(owner == f, base, 0.0))
        out_ref[f] = dot_split(turned, weights).reshape(cx, ny, nz)
    zero = jnp.zeros((cx, 16, nz), jnp.float32)
    pad_ref[0] = zero
    pad_ref[1] = zero

    def field(f, _):
        pad_ref[0, :, 8 - REACH : 8, :] = ylo_ref[f]
        pad_ref[1, :, 8 : 8 + REACH, :] = yhi_ref[f]
        for x in range(cx):
            low = out_ref[f, x, 0:8, :] + inner_ref[f, x, 0:8, :]
            high = out_ref[f, x, ny - 8 : ny, :] + inner_ref[f, x, ny - 8 : ny, :]
            for k in range(1, REACH + 1):
                low = low + SIDE[k] * pad_ref[0, x, 8 - k : 16 - k, :]
                high = high + SIDE[k] * pad_ref[1, x, k : 8 + k, :]
            out_ref[f, x, 0:8, :] = low
            out_ref[f, x, ny - 8 : ny, :] = high
            if ny > 16:
                out_ref[f, x, 8 : ny - 8, :] = out_ref[f, x, 8 : ny - 8, :] + inner_ref[f, x, 8 : ny - 8, :]
        oy_ref[f] = out_ref[f, :, 0:REACH, :]
        return 0

    lax.fori_loop(0, fields, field, 0)
    gathered = jnp.zeros((cx * ny, nz), jnp.float32)
    for f in range(fields):
        gathered = gather_edges(gathered, f, out_ref[f].reshape(cx * ny, nz))
    store_edges(gathered, fields, oz_ref, own_ref)


def fold(value):
    return jnp.sum(value, axis=0, keepdims=True)


def sums_kernel(center_ref, b_ref, pot_ref, h_ref, acc_ref, step_ref):
    fields, cx, ny, nz = b_ref.shape
    srcs = fields // 2
    shift = DIAG - center_ref[0]
    matrix = split(band((nz, nz), 0, (1,), 2.0))
    row = lax.broadcasted_iota(jnp.int32, (ny, nz), 0)
    inside = [row < ny - k for k in range(REACH + 1)]
    for s in range(srcs):
        for part in range(2):
            f = part * srcs + s
            step_ref[part] = dot_split(split(h_ref[f].reshape(cx * ny, nz)), matrix).reshape(cx, ny, nz)
        total = [jnp.zeros((ny, nz), jnp.float32) for _ in range(8)]
        for x in range(cx):
            local = pot_ref[x] + shift
            br, bi = b_ref[s, x], b_ref[srcs + s, x]
            h, g = [], []
            for part in range(2):
                f = part * srcs + s
                own = h_ref[f, x]
                image = step_ref[part, x] + local * own
                for k in range(1, REACH + 1):
                    up = jnp.where(inside[k], pltpu.roll(own, ny - k, 0), 0.0)
                    image = image + (2.0 * SIDE[k]) * (h_ref[f, (x + k) % cx] + up)
                h.append(own)
                g.append(image)
            terms = (
                br * br - bi * bi,
                2.0 * (br * bi),
                br * h[0] - bi * h[1],
                br * h[1] + bi * h[0],
                h[0] * h[0] - h[1] * h[1],
                2.0 * (h[0] * h[1]),
                h[0] * g[0] - h[1] * g[1],
                h[0] * g[1] + h[1] * g[0],
            )
            total = [t + v for t, v in zip(total, terms)]
        for i in range(8):
            acc_ref[i * srcs + s : i * srcs + s + 1, :] = fold(total[i])


def finish_kernel(acc_ref, h_ref, own_ref, yhi_ref, zhi_ref, out_ref, pad_ref):
    fields, cx, ny, nz = h_ref.shape
    srcs = fields // 2
    i = lax.broadcasted_iota(jnp.int32, (REACH, REACH), 0)
    j = lax.broadcasted_iota(jnp.int32, (REACH, REACH), 1)
    mix = jnp.zeros((REACH, REACH), jnp.float32)
    for k in range(1, REACH + 1):
        mix = jnp.where(j - i + REACH == k, 2.0 * SIDE[k], mix)
    out_ref[...] = acc_ref[...]
    pad_ref[...] = jnp.zeros(pad_ref.shape, jnp.float32)
    for s in range(srcs):
        at = [(part * srcs + s) * REACH for part in range(2)]
        edge = [own_ref[n : n + REACH, :] for n in at]
        far = [dot(mix, zhi_ref[n : n + REACH, :], ((1,), (0,))) for n in at]
        both = (edge[0] * far[0] - edge[1] * far[1], edge[0] * far[1] + edge[1] * far[0])
        sides = []
        for c in range(2):
            flat = fold(both[c])
            width = flat.shape[1]
            sides.append(sum(flat[:, at : at + nz] for at in range(0, width, nz)))
        total = [jnp.zeros((8, nz), jnp.float32) for _ in range(2)]
        for part in range(2):
            pad_ref[part, :, 8 : 8 + REACH, :] = yhi_ref[part * srcs + s]
        for x in range(cx):
            h = [h_ref[part * srcs + s, x, ny - 8 : ny, :] for part in range(2)]
            g = []
            for part in range(2):
                image = (2.0 * SIDE[1]) * pad_ref[part, x, 1:9, :]
                for k in range(2, REACH + 1):
                    image = image + (2.0 * SIDE[k]) * pad_ref[part, x, k : 8 + k, :]
                g.append(image)
            total[0] = total[0] + (h[0] * g[0] - h[1] * g[1])
            total[1] = total[1] + (h[0] * g[1] + h[1] * g[0])
        for c in range(2):
            at = (6 + c) * srcs + s
            out_ref[at : at + 1, :] = out_ref[at : at + 1, :] + fold(total[c]) + sides[c]


def complex_mul(left, right):
    return (left[0] * right[0] - left[1] * right[1], left[0] * right[1] + left[1] * right[0])


def complex_div(left, right):
    norm_sq = right[0] * right[0] + right[1] * right[1]
    return (
        (left[0] * right[0] + left[1] * right[1]) / norm_sq,
        (left[1] * right[0] - left[0] * right[1]) / norm_sq,
    )


def phase_table():
    lane = np.arange(LANES)
    angle = 2.0 * math.pi * (lane % QPTS + 0.5) / QPTS
    rows = [np.cos(angle), np.sin(angle)]
    for k in range(1, MOMS + 1):
        rows.append(np.where(lane < QPTS, np.cos(k * angle), 0.0) / QPTS)
        rows.append(np.where(lane < QPTS, np.sin(k * angle), 0.0) / QPTS)
    while len(rows) % 8:
        rows.append(np.zeros(LANES))
    return np.stack(rows).astype(np.float32)


def output_kernel(quad_ref, radius_ref, tot_ref, table_ref, re_ref, im_ref, hr_ref, hi_ref, out_ref, coef_ref):
    srcs = tot_ref.shape[0] // 8
    s = pl.program_id(0)

    @pl.when(s == 0)
    def _():
        radius = radius_ref[0]
        summed = jnp.sum(tot_ref[...], axis=1, keepdims=True)
        wide = jnp.broadcast_to(summed, (8 * srcs, LANES))
        nu = [
            (wide[2 * k * srcs : (2 * k + 1) * srcs], wide[(2 * k + 1) * srcs : (2 * k + 2) * srcs])
            for k in range(4)
        ]
        shape = (srcs, LANES)
        zeta = (
            jnp.broadcast_to(radius * table_ref[0:1, :], shape),
            jnp.broadcast_to(radius * table_ref[1:2, :], shape),
        )
        scaled = complex_mul(zeta, nu[0])
        alpha_first = complex_div(nu[0], (scaled[0] - nu[1][0], scaled[1] - nu[1][1]))
        mean = complex_div(nu[1], nu[0])
        t = complex_mul(mean, nu[1])
        spread2 = (nu[2][0] - t[0], nu[2][1] - t[1])
        t = complex_mul(mean, (nu[2][0] + spread2[0], nu[2][1] + spread2[1]))
        spread3 = (nu[3][0] - t[0], nu[3][1] - t[1])
        square = complex_mul(alpha_first, alpha_first)
        rho_next = complex_mul(square, spread2)
        beta = complex_div(rho_next, nu[0])
        first = complex_mul(zeta, rho_next)
        second = complex_mul(square, spread3)
        third = complex_div(complex_mul(beta, rho_next), alpha_first)
        alpha_next = complex_div(
            rho_next, (first[0] - second[0] - third[0], first[1] - second[1] - third[1])
        )
        t = complex_mul(alpha_first, mean)
        carried = complex_mul(alpha_next, (beta[0] - t[0], beta[1] - t[1]))
        on_source = (alpha_first[0] + carried[0], alpha_first[1] + carried[1])
        on_image = complex_mul(alpha_next, alpha_first)
        for k in range(MOMS):
            weight = (
                jnp.broadcast_to(radius * table_ref[2 + 2 * k : 3 + 2 * k, :], shape),
                jnp.broadcast_to(radius * table_ref[3 + 2 * k : 4 + 2 * k, :], shape),
            )
            for n, value in enumerate((on_source, on_image)):
                both = complex_mul(weight, value)
                for c in range(2):
                    column = jnp.sum(both[c], axis=1, keepdims=True)
                    coef_ref[4 * k + 2 * n + c, 0:srcs, :] = jnp.broadcast_to(column, shape)

    planes = re_ref.shape[1]
    plane = re_ref.shape[2:]
    for k in range(MOMS):
        c = [jnp.broadcast_to(coef_ref[4 * k + n, pl.ds(s, 1), :], plane) for n in range(4)]
        for x in range(planes):
            br, bi, hr, hi = re_ref[0, x], im_ref[0, x], hr_ref[0, x], hi_ref[0, x]
            out_ref[k, 0, 0, x] = c[0] * br - c[1] * bi + (c[2] * hr - c[3] * hi)
            out_ref[k, 1, 0, x] = c[0] * bi + c[1] * br + (c[2] * hi + c[3] * hr)


def ring(count, step):
    return [(i, (i + step) % count) for i in range(count)]


def total_over(value, axis):
    count = lax.axis_size(axis)
    if count & (count - 1):
        return lax.psum(value, axis)
    bit = 1
    while bit < count:
        value = value + lax.ppermute(value, axis, [(i, i ^ bit) for i in range(count)])
        bit *= 2
    return value


HBM = pl.BlockSpec(memory_space=pltpu.HBM)
VMEM = pl.BlockSpec(memory_space=pltpu.VMEM)
SMEM = pl.BlockSpec(memory_space=pltpu.SMEM)


def shaped(*dims):
    return jax.ShapeDtypeStruct(dims, jnp.float32)


def small(mib):
    return pltpu.CompilerParams(vmem_limit_bytes=mib << 20)


def cost(flops, nbytes):
    return pl.CostEstimate(flops=flops, bytes_accessed=nbytes, transcendentals=0)


def per_device(source_real, source_imag, potential, center, radius):
    srcs, cx, ny, nz = source_real.shape
    fields = 2 * srcs
    cells = cx * ny * nz
    py, pz, quads = lax.axis_size("py"), lax.axis_size("pz"), lax.axis_size("quad")

    whole = shaped(fields, cx, ny, nz)
    thin = shaped(fields, cx, REACH, nz)
    flat = shaped(fields * REACH, cx * ny)
    b, pot, ylo, yhi, zlo, zhi = pl.pallas_call(
        load_kernel,
        out_shape=(whole, shaped(cx, ny, nz), thin, thin, flat, flat),
        in_specs=[HBM] * 3,
        out_specs=(VMEM,) * 6,
        scratch_shapes=[
            pltpu.VMEM((cx * ny, nz), jnp.float32),
            pltpu.SemaphoreType.DMA((fields + 1,)),
        ],
        compiler_params=small(8),
        name="load",
    )(*(pltpu.with_memory_space_constraint(a, pltpu.HBM) for a in (source_real, source_imag, potential)))
    y_above = lax.ppermute(ylo, "py", ring(py, -1))
    y_below = lax.ppermute(yhi, "py", ring(py, 1))
    z_above = lax.ppermute(zlo, "pz", ring(pz, -1))
    z_below = lax.ppermute(zhi, "pz", ring(pz, 1))

    inner = pl.pallas_call(
        inner_kernel,
        out_shape=whole,
        in_specs=[SMEM] + [VMEM] * 2,
        out_specs=VMEM,
        scratch_shapes=[pltpu.VMEM((cx, ny + 16, nz), jnp.float32)],
        compiler_params=small(12),
        cost_estimate=cost(fields * cells * 60, fields * cells * 12),
        name="inner",
    )(center, b, pot)

    image, h_ylo, h_zlo, h_own = pl.pallas_call(
        border_kernel,
        out_shape=(whole, thin, flat, flat),
        in_specs=[VMEM] * 5,
        out_specs=(VMEM,) * 4,
        scratch_shapes=[
            pltpu.VMEM((2, cx, 16, nz), jnp.float32),
            pltpu.VMEM((cx * ny, nz), jnp.float32),
        ],
        compiler_params=small(12),
        name="border",
    )(inner, y_below, y_above, z_below, z_above)
    h_yabove = lax.ppermute(h_ylo, "py", ring(py, -1))
    h_zabove = lax.ppermute(h_zlo, "pz", ring(pz, -1))

    partial = pl.pallas_call(
        sums_kernel,
        out_shape=shaped(8 * srcs, nz),
        in_specs=[SMEM] + [VMEM] * 3,
        out_specs=VMEM,
        scratch_shapes=[pltpu.VMEM((2, cx, ny, nz), jnp.float32)],
        compiler_params=small(12),
        cost_estimate=cost(fields * cells * 60, fields * cells * 12),
        name="sums",
    )(center, b, pot, image)

    partial = pl.pallas_call(
        finish_kernel,
        out_shape=shaped(8 * srcs, nz),
        in_specs=[VMEM] * 5,
        out_specs=VMEM,
        scratch_shapes=[pltpu.VMEM((2, cx, 16, nz), jnp.float32)],
        compiler_params=small(12),
        name="finish",
    )(partial, image, h_own, h_yabove, h_zabove)

    total = total_over(total_over(partial, "py"), "pz")

    planes = cx // quads
    quad = lax.axis_index("quad").reshape(1)
    table = jnp.asarray(phase_table())
    own = lambda shift: pl.BlockSpec((1, planes, ny, nz), lambda s, q: (s + shift, q[0], 0, 0))
    return pl.pallas_call(
        output_kernel,
        out_shape=shaped(MOMS, 2, srcs, planes, ny, nz),
        grid_spec=pltpu.PrefetchScalarGridSpec(
            num_scalar_prefetch=1,
            grid=(srcs,),
            in_specs=[
                SMEM,
                pl.BlockSpec(total.shape, lambda s, q: (0, 0)),
                pl.BlockSpec(table.shape, lambda s, q: (0, 0)),
                own(0),
                own(srcs),
                own(0),
                own(srcs),
            ],
            out_specs=pl.BlockSpec((MOMS, 2, 1, planes, ny, nz), lambda s, q: (0, 0, s, 0, 0, 0)),
            scratch_shapes=[pltpu.VMEM((4 * MOMS, 8, LANES), jnp.float32)],
        ),
        compiler_params=small(12),
        name="output",
    )(quad, radius, total, table, b, b, image, image)


def solution(mesh):
    in_specs = (P(None, None, "py", "pz"), P(None, None, "py", "pz"), P(None, "py", "pz"), P(), P())
    out_specs = P(None, None, None, "quad", "py", "pz")
    return jax.shard_map(
        per_device, mesh=mesh, in_specs=in_specs, out_specs=out_specs, check_vma=False
    )
```

```python
import functools
import math

import jax
import jax.numpy as jnp
import numpy as np
from jax import lax
from jax.experimental import pallas as pl
from jax.experimental.pallas import tpu as pltpu
from jax.sharding import PartitionSpec as P

QPTS = 8
MOMS = 4
REACH = 4
LANES = 128

stencil_weights = (-205.0 / 72.0, 8.0 / 5.0, -1.0 / 5.0, 8.0 / 315.0, -1.0 / 560.0)
DIAG = -1.5 * stencil_weights[0]
MIDDLE = 5.25
SIDE = tuple(-0.5 * w for w in stencil_weights)
HIGHEST = lax.Precision.HIGHEST


def dot(left, right, dims):
    return lax.dot_general(
        left, right, (dims, ((), ())), precision=HIGHEST, preferred_element_type=jnp.float32
    )


def band(shape, offset, signs, scale=1.0):
    step = offset + lax.broadcasted_iota(jnp.int32, shape, 0) - lax.broadcasted_iota(jnp.int32, shape, 1)
    out = jnp.zeros(shape, jnp.float32)
    for k in range(1, REACH + 1):
        for sign in signs:
            out = jnp.where(step == sign * k, scale * SIDE[k], out)
    return out


def split(value):
    high = value.astype(jnp.bfloat16)
    return high, (value - high.astype(jnp.float32)).astype(jnp.bfloat16)


def dot_split(left, right):
    rows = jnp.concatenate([left[0], left[1], left[0]], axis=1)
    cols = jnp.concatenate([right[0], right[0], right[1]], axis=0)
    return lax.dot_general(rows, cols, (((1,), (0,)), ((), ())), preferred_element_type=jnp.float32)


def gather_edges(gathered, f, value):
    lane = lax.broadcasted_iota(jnp.int32, value.shape, 1)
    moved = pltpu.roll(value, 2 * REACH * f + REACH, 1)
    return jnp.where(lane // (2 * REACH) == f, moved, gathered)


def store_edges(gathered, fields, low_ref, high_ref):
    turned = gathered.T
    for f in range(fields):
        at = 2 * REACH * f
        high_ref[f * REACH : (f + 1) * REACH, :] = turned[at : at + REACH]
        low_ref[f * REACH : (f + 1) * REACH, :] = turned[at + REACH : at + 2 * REACH]


def load_kernel(re_hbm, im_hbm, pot_hbm, b_ref, pot_ref, ylo_ref, yhi_ref, zlo_ref, zhi_ref, edge_ref, sems):
    fields, cx, ny, nz = b_ref.shape
    srcs = fields // 2
    copies = [
        pltpu.make_async_copy(hbm.at[s], b_ref.at[part * srcs + s], sems.at[part * srcs + s])
        for part, hbm in enumerate((re_hbm, im_hbm))
        for s in range(srcs)
    ]
    copies.append(pltpu.make_async_copy(pot_hbm, pot_ref, sems.at[fields]))
    for copy in copies:
        copy.start()
    edge_ref[...] = jnp.zeros(edge_ref.shape, jnp.float32)
    for f in range(fields):
        copies[f].wait()
        ylo_ref[f] = b_ref[f, :, 0:REACH, :]
        yhi_ref[f] = b_ref[f, :, ny - REACH : ny, :]
        edge_ref[...] = gather_edges(edge_ref[...], f, b_ref[f].reshape(cx * ny, nz))
    copies[fields].wait()
    pot_ref[...] = pot_ref[...] + (DIAG - MIDDLE)
    store_edges(edge_ref[...], fields, zlo_ref, zhi_ref)


def phase_table():
    lane = np.arange(LANES)
    angle = 2.0 * math.pi * (lane % QPTS + 0.5) / QPTS
    rows = [np.cos(angle), np.sin(angle)]
    for k in range(1, MOMS + 1):
        rows.append(np.where(lane < QPTS, np.cos(k * angle), 0.0) / QPTS)
        rows.append(np.where(lane < QPTS, np.sin(k * angle), 0.0) / QPTS)
    rows += [np.zeros(LANES)] * (-len(rows) % 8)
    return np.stack(rows).astype(np.float32)


def inner_kernel(b_ref, pot_ref, out_ref, pad_ref):
    fields, cx, ny, nz = b_ref.shape
    matrix = split(band((nz, nz), 0, (1, -1)))
    zero = jnp.zeros((cx, 8, nz), jnp.float32)
    pad_ref[:, 0:8, :] = zero
    pad_ref[:, 8 + ny : 16 + ny, :] = zero

    for f in range(fields):
        out_ref[f] = dot_split(split(b_ref[f].reshape(cx * ny, nz)), matrix).reshape(cx, ny, nz)

    def field(f, _):
        pad_ref[:, 8 : 8 + ny, :] = b_ref[f]
        for x in range(cx):
            total = out_ref[f, x] + pot_ref[x] * b_ref[f, x]
            for k in range(1, REACH + 1):
                beside = b_ref[f, (x + k) % cx] + b_ref[f, (x - k) % cx]
                beside = beside + pad_ref[x, 8 + k : 8 + k + ny, :]
                beside = beside + pad_ref[x, 8 - k : 8 - k + ny, :]
                total = total + SIDE[k] * beside
            out_ref[f, x] = total
        return 0

    lax.fori_loop(0, fields, field, 0)


def border_kernel(
    inner_ref, ylo_ref, yhi_ref, zlo_ref, zhi_ref, out_ref, oy_ref, oz_ref, own_ref, pad_ref, edge_ref
):
    fields, cx, ny, nz = inner_ref.shape
    rows = fields * REACH
    turned = split(jnp.concatenate([zlo_ref[...], zhi_ref[...]], axis=0).T)
    row = lax.broadcasted_iota(jnp.int32, (2 * rows, nz), 0)
    col = lax.broadcasted_iota(jnp.int32, (2 * rows, nz), 1)
    step = jnp.where(row < rows, row % REACH - REACH, nz + row % REACH) - col
    base = jnp.zeros((2 * rows, nz), jnp.float32)
    for k in range(1, REACH + 1):
        base = jnp.where(jnp.abs(step) == k, SIDE[k], base)
    owner = (row % rows) // REACH
    for f in range(fields):
        weights = split(jnp.where(owner == f, base, 0.0))
        out_ref[f] = dot_split(turned, weights).reshape(cx, ny, nz)
    zero = jnp.zeros((cx, 16, nz), jnp.float32)
    pad_ref[0] = zero
    pad_ref[1] = zero

    def field(f, _):
        pad_ref[0, :, 8 - REACH : 8, :] = ylo_ref[f]
        pad_ref[1, :, 8 : 8 + REACH, :] = yhi_ref[f]
        for x in range(cx):
            low = out_ref[f, x, 0:8, :] + inner_ref[f, x, 0:8, :]
            high = out_ref[f, x, ny - 8 : ny, :] + inner_ref[f, x, ny - 8 : ny, :]
            for k in range(1, REACH + 1):
                low = low + SIDE[k] * pad_ref[0, x, 8 - k : 16 - k, :]
                high = high + SIDE[k] * pad_ref[1, x, k : 8 + k, :]
            out_ref[f, x, 0:8, :] = low
            out_ref[f, x, ny - 8 : ny, :] = high
            if ny > 16:
                out_ref[f, x, 8 : ny - 8, :] = out_ref[f, x, 8 : ny - 8, :] + inner_ref[f, x, 8 : ny - 8, :]
        oy_ref[f] = out_ref[f, :, 0:REACH, :]
        return 0

    lax.fori_loop(0, fields, field, 0)
    gathered = jnp.zeros((cx * ny, nz), jnp.float32)
    for f in range(fields):
        gathered = gather_edges(gathered, f, out_ref[f].reshape(cx * ny, nz))
    store_edges(gathered, fields, oz_ref, own_ref)


def fold(value):
    return jnp.sum(value, axis=0, keepdims=True)


def sums_kernel(b_ref, pot_ref, h_ref, acc_ref, step_ref):
    fields, cx, ny, nz = b_ref.shape
    srcs = fields // 2
    matrix = split(band((nz, nz), 0, (1,), 2.0))
    row = lax.broadcasted_iota(jnp.int32, (ny, nz), 0)
    inside = [row < ny - k for k in range(REACH + 1)]
    for s in range(srcs):
        for part in range(2):
            f = part * srcs + s
            step_ref[part] = dot_split(split(h_ref[f].reshape(cx * ny, nz)), matrix).reshape(cx, ny, nz)
        total = [jnp.zeros((ny, nz), jnp.float32) for _ in range(8)]
        for x in range(cx):
            local = pot_ref[x]
            br, bi = b_ref[s, x], b_ref[srcs + s, x]
            h, g = [], []
            for part in range(2):
                f = part * srcs + s
                own = h_ref[f, x]
                image = step_ref[part, x] + local * own
                for k in range(1, REACH + 1):
                    up = jnp.where(inside[k], pltpu.roll(own, ny - k, 0), 0.0)
                    image = image + (2.0 * SIDE[k]) * (h_ref[f, (x + k) % cx] + up)
                h.append(own)
                g.append(image)
            terms = (
                br * br - bi * bi,
                2.0 * (br * bi),
                br * h[0] - bi * h[1],
                br * h[1] + bi * h[0],
                h[0] * h[0] - h[1] * h[1],
                2.0 * (h[0] * h[1]),
                h[0] * g[0] - h[1] * g[1],
                h[0] * g[1] + h[1] * g[0],
            )
            total = [t + v for t, v in zip(total, terms)]
        for i in range(8):
            acc_ref[i * srcs + s : i * srcs + s + 1, :] = fold(total[i])


def finish_kernel(sums_ref, h_ref, own_ref, yhi_ref, zhi_ref, out_ref, pad_ref, acc_ref):
    fields, cx, ny, nz = h_ref.shape
    srcs = fields // 2
    acc_ref[...] = sums_ref[...]
    i = lax.broadcasted_iota(jnp.int32, (REACH, REACH), 0)
    j = lax.broadcasted_iota(jnp.int32, (REACH, REACH), 1)
    mix = jnp.zeros((REACH, REACH), jnp.float32)
    for k in range(1, REACH + 1):
        mix = jnp.where(j - i + REACH == k, 2.0 * SIDE[k], mix)
    pad_ref[...] = jnp.zeros(pad_ref.shape, jnp.float32)
    for s in range(srcs):
        at = [(part * srcs + s) * REACH for part in range(2)]
        edge = [own_ref[n : n + REACH, :] for n in at]
        far = [dot(mix, zhi_ref[n : n + REACH, :], ((1,), (0,))) for n in at]
        both = (edge[0] * far[0] - edge[1] * far[1], edge[0] * far[1] + edge[1] * far[0])
        sides = []
        for c in range(2):
            flat = fold(both[c])
            width = flat.shape[1]
            sides.append(sum(flat[:, at : at + nz] for at in range(0, width, nz)))
        total = [jnp.zeros((8, nz), jnp.float32) for _ in range(2)]
        for part in range(2):
            pad_ref[part, :, 8 : 8 + REACH, :] = yhi_ref[part * srcs + s]
        for x in range(cx):
            h = [h_ref[part * srcs + s, x, ny - 8 : ny, :] for part in range(2)]
            g = []
            for part in range(2):
                image = (2.0 * SIDE[1]) * pad_ref[part, x, 1:9, :]
                for k in range(2, REACH + 1):
                    image = image + (2.0 * SIDE[k]) * pad_ref[part, x, k : 8 + k, :]
                g.append(image)
            total[0] = total[0] + (h[0] * g[0] - h[1] * g[1])
            total[1] = total[1] + (h[0] * g[1] + h[1] * g[0])
        for c in range(2):
            at = (6 + c) * srcs + s
            acc_ref[at : at + 1, :] = acc_ref[at : at + 1, :] + fold(total[c]) + sides[c]
    out_ref[...] = squeeze_rows(acc_ref[...])


def complex_mul(left, right):
    return (left[0] * right[0] - left[1] * right[1], left[0] * right[1] + left[1] * right[0])


def complex_div(left, right):
    norm_sq = right[0] * right[0] + right[1] * right[1]
    return (
        (left[0] * right[0] + left[1] * right[1]) / norm_sq,
        (left[1] * right[0] - left[0] * right[1]) / norm_sq,
    )


def squeeze_rows(value):
    rows, width = value.shape
    part = width // 4
    lane = lax.broadcasted_iota(jnp.int32, (rows // 4, width), 1) // part
    value = value + pltpu.roll(value, 2 * part, 1)
    value = value + pltpu.roll(value, part, 1)
    out = value[0 : rows // 4]
    for g in range(1, 4):
        out = jnp.where(lane == g, value[g * rows // 4 : (g + 1) * rows // 4], out)
    return out


def output_kernel(tot_ref, table_ref, b_ref, h_ref, out_hbm, coef_ref, buf_ref, sems):
    fields, cx, ny, nz = b_ref.shape
    srcs = fields // 2
    planes = buf_ref.shape[3]
    first = lax.axis_index("quad") * planes
    tot = tot_ref[...]
    lane = lax.broadcasted_iota(jnp.int32, tot.shape, 1) // (tot.shape[1] // 4)
    shape = (srcs, LANES)
    nu = []
    for k in range(4):
        column = jnp.sum(jnp.where(lane == k, tot, 0.0), axis=1, keepdims=True)
        wide = jnp.broadcast_to(column, (2 * srcs, LANES))
        nu.append((wide[0:srcs], wide[srcs : 2 * srcs]))
    zeta = (
        jnp.broadcast_to(table_ref[0:1, :], shape),
        jnp.broadcast_to(table_ref[1:2, :], shape),
    )
    scaled = complex_mul(zeta, nu[0])
    alpha_first = complex_div(nu[0], (scaled[0] - nu[1][0], scaled[1] - nu[1][1]))
    mean = complex_div(nu[1], nu[0])
    t = complex_mul(mean, nu[1])
    spread2 = (nu[2][0] - t[0], nu[2][1] - t[1])
    t = complex_mul(mean, (nu[2][0] + spread2[0], nu[2][1] + spread2[1]))
    spread3 = (nu[3][0] - t[0], nu[3][1] - t[1])
    square = complex_mul(alpha_first, alpha_first)
    rho_next = complex_mul(square, spread2)
    beta = complex_div(rho_next, nu[0])
    first_part = complex_mul(zeta, rho_next)
    second = complex_mul(square, spread3)
    third = complex_div(complex_mul(beta, rho_next), alpha_first)
    alpha_next = complex_div(
        rho_next, (first_part[0] - second[0] - third[0], first_part[1] - second[1] - third[1])
    )
    t = complex_mul(alpha_first, mean)
    carried = complex_mul(alpha_next, (beta[0] - t[0], beta[1] - t[1]))
    on_source = (alpha_first[0] + carried[0], alpha_first[1] + carried[1])
    on_image = complex_mul(alpha_next, alpha_first)
    for k in range(MOMS):
        weight = (
            jnp.broadcast_to(table_ref[2 + 2 * k : 3 + 2 * k, :], shape),
            jnp.broadcast_to(table_ref[3 + 2 * k : 4 + 2 * k, :], shape),
        )
        for n, value in enumerate((on_source, on_image)):
            both = complex_mul(weight, value)
            for c in range(2):
                column = jnp.sum(both[c], axis=1, keepdims=True)
                coef_ref[4 * k + 2 * n + c, 0:srcs, :] = jnp.broadcast_to(column, shape)

    copies = []
    for s in range(srcs):
        for k in range(MOMS):
            c = [
                jnp.broadcast_to(coef_ref[4 * k + n, s : s + 1, :], (ny, nz)) for n in range(4)
            ]
            for x in range(planes):
                br, bi = b_ref[s, first + x], b_ref[srcs + s, first + x]
                hr, hi = h_ref[s, first + x], h_ref[srcs + s, first + x]
                buf_ref[s, k, 0, x] = c[0] * br - c[1] * bi + (c[2] * hr - c[3] * hi)
                buf_ref[s, k, 1, x] = c[0] * bi + c[1] * br + (c[2] * hi + c[3] * hr)
        copy = pltpu.make_async_copy(buf_ref.at[s], out_hbm.at[:, :, s], sems.at[s])
        copy.start()
        copies.append(copy)
    for copy in copies:
        copy.wait()


def ring(count, step):
    return [(i, (i + step) % count) for i in range(count)]


def total_over(value, axis):
    count = lax.axis_size(axis)
    if count & (count - 1):
        return lax.psum(value, axis)
    bit = 1
    while bit < count:
        value = value + lax.ppermute(value, axis, [(i, i ^ bit) for i in range(count)])
        bit *= 2
    return value


ANY = pl.BlockSpec(memory_space=pl.ANY)
HBM = pl.BlockSpec(memory_space=pltpu.HBM)
VMEM = pl.BlockSpec(memory_space=pltpu.VMEM)
SMEM = pl.BlockSpec(memory_space=pltpu.SMEM)


def shaped(*dims):
    return jax.ShapeDtypeStruct(dims, jnp.float32)


def small(mib):
    return pltpu.CompilerParams(vmem_limit_bytes=mib << 20)


def cost(flops, nbytes):
    return pl.CostEstimate(flops=flops, bytes_accessed=nbytes, transcendentals=0)


def per_device(source_real, source_imag, potential, center, radius):
    srcs, cx, ny, nz = source_real.shape
    fields = 2 * srcs
    cells = cx * ny * nz
    py, pz, quads = lax.axis_size("py"), lax.axis_size("pz"), lax.axis_size("quad")

    whole = shaped(fields, cx, ny, nz)
    thin = shaped(fields, cx, REACH, nz)
    flat = shaped(fields * REACH, cx * ny)
    source_real, source_imag, potential = (
        pltpu.with_memory_space_constraint(a, pltpu.HBM)
        for a in (source_real, source_imag, potential)
    )
    b, pot, ylo, yhi, zlo, zhi = pl.pallas_call(
        load_kernel,
        out_shape=(whole, shaped(cx, ny, nz), thin, thin, flat, flat),
        in_specs=[HBM] * 3,
        out_specs=(VMEM,) * 6,
        scratch_shapes=[
            pltpu.VMEM((cx * ny, nz), jnp.float32),
            pltpu.SemaphoreType.DMA((fields + 1,)),
        ],
        compiler_params=small(8),
        name="load",
    )(source_real, source_imag, potential)
    y_above = lax.ppermute(ylo, "py", ring(py, -1))
    y_below = lax.ppermute(yhi, "py", ring(py, 1))
    z_above = lax.ppermute(zlo, "pz", ring(pz, -1))
    z_below = lax.ppermute(zhi, "pz", ring(pz, 1))

    inner = pl.pallas_call(
        inner_kernel,
        out_shape=whole,
        in_specs=[VMEM] * 2,
        out_specs=VMEM,
        scratch_shapes=[pltpu.VMEM((cx, ny + 16, nz), jnp.float32)],
        compiler_params=small(12),
        cost_estimate=cost(fields * cells * 60, fields * cells * 12),
        name="inner",
    )(b, pot)

    image, h_ylo, h_zlo, h_own = pl.pallas_call(
        border_kernel,
        out_shape=(whole, thin, flat, flat),
        in_specs=[VMEM] * 5,
        out_specs=(VMEM,) * 4,
        scratch_shapes=[
            pltpu.VMEM((2, cx, 16, nz), jnp.float32),
            pltpu.VMEM((cx * ny, nz), jnp.float32),
        ],
        compiler_params=small(12),
        name="border",
    )(inner, y_below, y_above, z_below, z_above)
    h_yabove = lax.ppermute(h_ylo, "py", ring(py, -1))
    h_zabove = lax.ppermute(h_zlo, "pz", ring(pz, -1))

    partial = pl.pallas_call(
        sums_kernel,
        out_shape=shaped(8 * srcs, nz),
        in_specs=[VMEM] * 3,
        out_specs=VMEM,
        scratch_shapes=[pltpu.VMEM((2, cx, ny, nz), jnp.float32)],
        compiler_params=small(12),
        cost_estimate=cost(fields * cells * 60, fields * cells * 12),
        name="sums",
    )(b, pot, image)

    partial = pl.pallas_call(
        finish_kernel,
        out_shape=shaped(2 * srcs, nz),
        in_specs=[VMEM] * 5,
        out_specs=VMEM,
        scratch_shapes=[
            pltpu.VMEM((2, cx, 16, nz), jnp.float32),
            pltpu.VMEM((8 * srcs, nz), jnp.float32),
        ],
        compiler_params=small(12),
        name="finish",
    )(partial, image, h_own, h_yabove, h_zabove)

    total = total_over(total_over(partial, "py"), "pz")

    planes = cx // quads
    table = jnp.asarray(phase_table())
    row = lax.broadcasted_iota(jnp.int32, table.shape, 0)
    table = radius * table + jnp.where(row == 0, center - MIDDLE, 0.0)
    return pl.pallas_call(
        output_kernel,
        out_shape=shaped(MOMS, 2, srcs, planes, ny, nz),
        in_specs=[VMEM] * 4,
        out_specs=HBM,
        scratch_shapes=[
            pltpu.VMEM((4 * MOMS, 8, LANES), jnp.float32),
            pltpu.VMEM((srcs, MOMS, 2, planes, ny, nz), jnp.float32),
            pltpu.SemaphoreType.DMA((srcs,)),
        ],
        compiler_params=small(12),
        name="output",
    )(total, table, b, image)


def solution(mesh):
    in_specs = (P(None, None, "py", "pz"), P(None, None, "py", "pz"), P(None, "py", "pz"), P(), P())
    out_specs = P(None, None, None, "quad", "py", "pz")
    return jax.shard_map(
        per_device, mesh=mesh, in_specs=in_specs, out_specs=out_specs, check_vma=False
    )
```

```python
import functools
import math

import jax
import jax.numpy as jnp
import numpy as np
from jax import lax
from jax.experimental import pallas as pl
from jax.experimental.pallas import tpu as pltpu
from jax.sharding import PartitionSpec as P

QPTS = 8
MOMS = 4
REACH = 4
LANES = 128

stencil_weights = (-205.0 / 72.0, 8.0 / 5.0, -1.0 / 5.0, 8.0 / 315.0, -1.0 / 560.0)
DIAG = -1.5 * stencil_weights[0]
MIDDLE = 5.25
SIDE = tuple(-0.5 * w for w in stencil_weights)
HIGHEST = lax.Precision.HIGHEST


def dot(left, right, dims):
    return lax.dot_general(
        left, right, (dims, ((), ())), precision=HIGHEST, preferred_element_type=jnp.float32
    )


def band(shape, offset, signs, scale=1.0):
    step = offset + lax.broadcasted_iota(jnp.int32, shape, 0) - lax.broadcasted_iota(jnp.int32, shape, 1)
    out = jnp.zeros(shape, jnp.float32)
    for k in range(1, REACH + 1):
        for sign in signs:
            out = jnp.where(step == sign * k, scale * SIDE[k], out)
    return out


def split(value):
    high = value.astype(jnp.bfloat16)
    return high, (value - high.astype(jnp.float32)).astype(jnp.bfloat16)


def dot_split(left, right):
    rows = jnp.concatenate([left[0], left[1], left[0]], axis=1)
    cols = jnp.concatenate([right[0], right[0], right[1]], axis=0)
    return lax.dot_general(rows, cols, (((1,), (0,)), ((), ())), preferred_element_type=jnp.float32)


def gather_edges(gathered, f, value):
    lane = lax.broadcasted_iota(jnp.int32, value.shape, 1)
    moved = pltpu.roll(value, 4 * REACH * f + 2 * REACH, 1)
    return jnp.where(lane // (4 * REACH) == f, moved, gathered)


def beside(owned, cx):
    return [x % cx for x in range(-REACH, owned + REACH)]


def load_kernel(
    owned, re_hbm, im_hbm, pot_hbm, b_ref, pot_ref, up_ref, down_ref, zup_ref, zdown_ref, edge_ref, sems
):
    fields, cx, ny, nz = b_ref.shape
    srcs = fields // 2
    parts = cx // owned
    reach = up_ref.shape[0] // (fields * REACH)
    near = beside(owned, cx)
    first = lax.axis_index("quad")
    copies = []
    for f in range(fields + 1):
        source = pot_hbm if f == fields else (re_hbm, im_hbm)[f // srcs].at[f % srcs]
        target = pot_ref if f == fields else b_ref.at[f]
        group = []
        for j in range(parts):
            at = pl.multiple_of(lax.rem(first + j, parts) * owned, owned)
            group.append(
                pltpu.make_async_copy(
                    source.at[pl.ds(at, owned)], target.at[pl.ds(j * owned, owned)], sems.at[f, j]
                )
            )
        copies.append(group)
    for group in copies:
        for copy in group:
            copy.start()
    edge_ref[...] = jnp.zeros(edge_ref.shape, jnp.float32)
    far = fields * len(near)
    for f in range(fields):
        for copy in copies[f]:
            copy.wait()
        for x in range(reach):
            at = (f * reach + x) * REACH
            up_ref[at : at + REACH, :] = b_ref[f, x, ny - REACH : ny, :]
        for i, x in enumerate(near):
            at = (f * len(near) + i) * REACH
            down_ref[at : at + REACH, :] = b_ref[f, x, 0:REACH, :]
        for x in range(owned):
            at = (far + f * owned + x) * REACH
            down_ref[at : at + REACH, :] = b_ref[f, x, REACH : 2 * REACH, :]
        edge_ref[...] = gather_edges(edge_ref[...], f, b_ref[f].reshape(cx * ny, nz))
    for copy in copies[fields]:
        copy.wait()
    pot_ref[...] = pot_ref[...] + (DIAG - MIDDLE)
    for x in range(owned):
        at = (far + fields * owned + x) * REACH
        down_ref[at : at + REACH, :] = pot_ref[x, 0:REACH, :]
    turned = edge_ref[...].T
    rows = fields * REACH
    for f in range(fields):
        at = 4 * REACH * f
        low, high = f * REACH, (f + 1) * REACH
        zup_ref[rows + low : rows + high, :] = turned[at : at + REACH]
        zup_ref[low:high, :] = turned[at + REACH : at + 2 * REACH]
        zdown_ref[low:high, :] = turned[at + 2 * REACH : at + 3 * REACH]
        zdown_ref[rows + low : rows + high, :] = turned[at + 3 * REACH : at + 4 * REACH]
    turned = pltpu.roll(pot_ref[...].reshape(cx * ny, nz), 2 * REACH, 1).T
    zup_ref[2 * rows : 2 * rows + REACH, :] = turned[REACH : 2 * REACH]
    zup_ref[2 * rows + REACH : 2 * rows + 2 * REACH, :] = turned[0:REACH]
    zdown_ref[2 * rows : 2 * rows + 2 * REACH, :] = turned[2 * REACH : 4 * REACH]


def phase_table():
    lane = np.arange(LANES)
    angle = 2.0 * math.pi * (lane % QPTS + 0.5) / QPTS
    rows = [np.cos(angle), np.sin(angle)]
    for k in range(1, MOMS + 1):
        rows.append(np.where(lane < QPTS, np.cos(k * angle), 0.0) / QPTS)
        rows.append(np.where(lane < QPTS, np.sin(k * angle), 0.0) / QPTS)
    rows += [np.zeros(LANES)] * (-len(rows) % 8)
    return np.stack(rows).astype(np.float32)


def inner_kernel(b_ref, pot_ref, out_ref, pad_ref):
    fields, cx, ny, nz = b_ref.shape
    reach = out_ref.shape[1]
    matrix = split(band((nz, nz), 0, (1, -1)))
    zero = jnp.zeros((reach, 8, nz), jnp.float32)
    pad_ref[:, 0:8, :] = zero
    pad_ref[:, 8 + ny : 16 + ny, :] = zero
    for f in range(fields):
        own = b_ref[f, 0:reach].reshape(reach * ny, nz)
        out_ref[f] = dot_split(split(own), matrix).reshape(reach, ny, nz)

    def field(f, _):
        pad_ref[:, 8 : 8 + ny, :] = b_ref[f, 0:reach]
        for x in range(reach):
            total = out_ref[f, x] + pot_ref[x] * b_ref[f, x]
            for k in range(1, REACH + 1):
                sides = b_ref[f, (x + k) % cx] + b_ref[f, (x - k) % cx]
                sides = sides + pad_ref[x, 8 + k : 8 + k + ny, :]
                sides = sides + pad_ref[x, 8 - k : 8 - k + ny, :]
                total = total + SIDE[k] * sides
            out_ref[f, x] = total
        return 0

    lax.fori_loop(0, fields, field, 0)


def links(row_at, col_at, row_field, col_field):
    step = jnp.abs(row_at - col_at)
    out = jnp.zeros(step.shape, jnp.float32)
    for k in range(1, REACH + 1):
        out = jnp.where((step == k) & (row_field == col_field), SIDE[k], out)
    return out


def layer_of(index, starts, rows):
    layer = jnp.full(index.shape, 1 << 20, jnp.int32)
    for n, start in enumerate(starts):
        layer = jnp.where(index // rows == n, start + index % REACH, layer)
    return layer, index % rows // REACH


def border_kernel(owned, inner_ref, below_ref, above_ref, zbelow_ref, zabove_ref, out_ref, u_ref, pad_ref, edge_ref):
    fields, reach, ny, nz = inner_ref.shape
    rows = fields * REACH
    count = owned + 2 * REACH
    turned = jnp.concatenate([zbelow_ref[0:rows], zabove_ref[0:rows]], axis=0).T
    turned = split(turned[0 : reach * ny])
    shape = (2 * rows, nz)
    layer, owner = layer_of(lax.broadcasted_iota(jnp.int32, shape, 0), (-REACH, nz), rows)
    cell = lax.broadcasted_iota(jnp.int32, shape, 1)
    for f in range(fields):
        weights = split(links(layer, cell, owner, f))
        out_ref[f] = dot_split(turned, weights).reshape(reach, ny, nz)
    zero = jnp.zeros((reach, 16, nz), jnp.float32)
    pad_ref[0] = zero
    pad_ref[1] = zero
    edge_ref[...] = jnp.zeros(edge_ref.shape, jnp.float32)
    for f in range(fields):
        for x in range(reach):
            at = (f * reach + x) * REACH
            pad_ref[0, x, 8 - REACH : 8, :] = below_ref[at : at + REACH, :]
            at = (f * count + REACH + x) * REACH
            pad_ref[1, x, 8 : 8 + REACH, :] = above_ref[at : at + REACH, :]
        for x in range(reach):
            low = SIDE[1] * pad_ref[0, x, 7:15, :]
            high = SIDE[1] * pad_ref[1, x, 1:9, :]
            for k in range(2, REACH + 1):
                low = low + SIDE[k] * pad_ref[0, x, 8 - k : 16 - k, :]
                high = high + SIDE[k] * pad_ref[1, x, k : 8 + k, :]
            total = out_ref[f, x] + inner_ref[f, x]
            middle = [total[8 : ny - 8]] if ny > 16 else []
            first, last = total[0:8] + low, total[ny - 8 : ny] + high
            out_ref[f, x] = jnp.concatenate([first] + middle + [last], axis=0)
            if x < owned:
                u = jnp.concatenate([first + low] + middle + [last + 3.0 * high], axis=0)
                spot = pl.ds(x * ny, ny)
                edge_ref[spot, :] = gather_edges(edge_ref[spot, :], f, u)
    turned = edge_ref[...].T
    for f in range(fields):
        at = 4 * REACH * f
        low, high = f * REACH, (f + 1) * REACH
        u_ref[low:high, :] = turned[at + 2 * REACH : at + 3 * REACH]
        u_ref[rows + low : rows + high, :] = turned[at + REACH : at + 2 * REACH]


def fold(value):
    return jnp.sum(value, axis=0, keepdims=True)


def sums_kernel(
    owned,
    b_ref,
    pot_ref,
    h_ref,
    u_ref,
    above_ref,
    zup_ref,
    zdown_ref,
    zbelow_ref,
    zabove_ref,
    out_ref,
    acc_ref,
    step_ref,
    far_ref,
):
    fields, cx, ny, nz = b_ref.shape
    srcs = fields // 2
    count = owned + 2 * REACH
    matrix = split(band((nz, nz), 0, (1,), 2.0))
    row = lax.broadcasted_iota(jnp.int32, (ny, nz), 0)
    inside = [row < ny - k for k in range(REACH + 1)]
    for f in range(fields):
        own = h_ref[f, 0:owned].reshape(owned * ny, nz)
        step_ref[f] = dot_split(split(own), matrix).reshape(owned, ny, nz)

    matrix = split(band((nz, nz), 0, (1, -1)))
    for f in range(fields):
        at = (f * count + REACH) * REACH
        far_ref[f] = dot_split(split(above_ref[at : at + owned * REACH, :]), matrix)
    quad_row = lax.broadcasted_iota(jnp.int32, (8, nz), 0) % REACH
    early = lax.broadcasted_iota(jnp.int32, (8, nz), 0) < REACH

    def top(ref, f, x):
        return jnp.where(early, pltpu.roll(ref[f, x, ny - 8 : ny, :], REACH, 0), ref[f, x + 1, ny - 8 : ny, :])

    def shifted(lower, upper, k):
        if k == REACH:
            return lower
        return jnp.where(quad_row >= k, pltpu.roll(upper, k, 0), pltpu.roll(lower, REACH + k, 0))

    def raised(lower, upper, k):
        if k == REACH:
            return upper
        return jnp.where(quad_row < REACH - k, pltpu.roll(lower, 8 - k, 0), pltpu.roll(upper, REACH - k, 0))

    for s in range(srcs):
        total = [jnp.zeros((ny, nz), jnp.float32) for _ in range(8)]
        for x in range(owned):
            local = pot_ref[x]
            br, bi = b_ref[s, x], b_ref[srcs + s, x]
            h, g = [], []
            for part in range(2):
                f = part * srcs + s
                own = h_ref[f, x]
                image = step_ref[f, x] + local * own
                for k in range(1, REACH + 1):
                    up = jnp.where(inside[k], pltpu.roll(own, ny - k, 0), 0.0)
                    image = image + (2.0 * SIDE[k]) * (h_ref[f, (x + k) % cx] + up)
                h.append(own)
                g.append(image)
            terms = (
                br * br - bi * bi,
                2.0 * (br * bi),
                br * h[0] - bi * h[1],
                br * h[1] + bi * h[0],
                h[0] * h[0] - h[1] * h[1],
                2.0 * (h[0] * h[1]),
                h[0] * g[0] - h[1] * g[1],
                h[0] * g[1] + h[1] * g[0],
            )
            total = [t + v for t, v in zip(total, terms)]
        cross = [jnp.zeros((8, nz), jnp.float32) for _ in range(2)]
        for x in range(0, owned, 2):
            at = (fields * (count + owned) + x) * REACH
            local = above_ref[at : at + 8, :]
            left, right = [], []
            for part in range(2):
                f = part * srcs + s
                at = (f * count + REACH + x) * REACH
                near = above_ref[at : at + 8, :]
                start = (fields * count + f * owned + x) * REACH
                far = above_ref[start : start + 8, :]
                own, own_h = top(b_ref, f, x), top(h_ref, f, x)
                image = far_ref[f, x * REACH : x * REACH + 8, :] + local * near
                pull = SIDE[REACH] * own_h
                for k in range(1, REACH + 1):
                    sides = above_ref[at + k * REACH : at + k * REACH + 8, :]
                    sides = sides + above_ref[at - k * REACH : at - k * REACH + 8, :]
                    sides = sides + raised(near, far, k) + shifted(own, near, k)
                    image = image + SIDE[k] * sides
                    if k < REACH:
                        pull = pull + SIDE[k] * jnp.where(quad_row < k, pltpu.roll(own_h, REACH + k, 0), 0.0)
                left.append(pull)
                right.append(image)
            cross[0] = cross[0] + (left[0] * right[0] - left[1] * right[1])
            cross[1] = cross[1] + (left[0] * right[1] + left[1] * right[0])
        for i in range(8):
            value = fold(total[i])
            if i >= 6:
                value = value + 2.0 * fold(cross[i - 6])
            acc_ref[i * srcs + s : i * srcs + s + 1, :] = value

    rows = fields * REACH
    width = cx * ny
    low, high = zdown_ref[0:rows, :], zup_ref[0:rows, :]
    below, above = zbelow_ref[0:rows, :], zabove_ref[0:rows, :]
    outer = jnp.concatenate([below, above], axis=0)
    stack = jnp.concatenate(
        [low, high, below, zbelow_ref[rows : 2 * rows, :], above, zabove_ref[rows : 2 * rows, :], outer], axis=0
    )
    shape = (2 * rows, 8 * rows)
    row_at, row_field = layer_of(lax.broadcasted_iota(jnp.int32, shape, 0), (-REACH, nz), rows)
    col = lax.broadcasted_iota(jnp.int32, shape, 1)
    starts = (0, nz - REACH, -REACH, -2 * REACH, nz, nz + REACH)
    col_at, col_field = layer_of(col, starts, rows)
    mix = split(links(row_at, col_at, row_field, col_field))
    image = dot_split(mix, split(stack))
    local = jnp.concatenate(
        [zbelow_ref[2 * rows : 2 * rows + REACH, :]] * fields + [zabove_ref[2 * rows : 2 * rows + REACH, :]] * fields,
        axis=0,
    )
    image = image + local * outer
    lane = lax.broadcasted_iota(jnp.int32, (2 * rows, width), 1)
    y = lane % ny
    for k in range(1, REACH + 1):
        sides = pltpu.roll(outer, ny * k, 1) + pltpu.roll(outer, width - ny * k, 1)
        sides = sides + jnp.where(y >= k, pltpu.roll(outer, k, 1), 0.0)
        sides = sides + jnp.where(y < ny - k, pltpu.roll(outer, width - k, 1), 0.0)
        image = image + SIDE[k] * sides
    shape = (4 * rows, 4 * rows)
    row = lax.broadcasted_iota(jnp.int32, shape, 0)
    col = lax.broadcasted_iota(jnp.int32, shape, 1)
    row_at, row_field = layer_of(row % (2 * rows), (0, nz - REACH), rows)
    col_at, col_field = layer_of(col % (2 * rows), (-REACH, nz), rows)
    mix = jnp.where(row // (2 * rows) == col // (2 * rows), links(row_at, col_at, row_field, col_field), 0.0)
    reached = dot_split(split(mix), split(jnp.concatenate([image, outer], axis=0)))

    def around(value):
        out = jnp.zeros(value.shape, jnp.float32)
        for k in range(1, REACH + 1):
            sides = jnp.where(y >= ny - k, pltpu.roll(value, ny - k, 1), 0.0)
            sides = sides + jnp.where(y < k, pltpu.roll(value, width + k - ny, 1), 0.0)
            out = out + SIDE[k] * sides
        return out

    weight = jnp.where(lane < owned * ny, jnp.where(y >= ny // 2, 3.0, 1.0), 0.0)
    edges = around(jnp.concatenate([low, high], axis=0)) * weight
    turned = around(reached[2 * rows : 4 * rows])
    half = rows // 2

    def product(left, right):
        re = im = 0.0
        for at in (0, rows):
            lr, li = left[at : at + half], left[at + half : at + rows]
            rr, ri = right[at : at + half], right[at + half : at + rows]
            re = re + (lr * rr - li * ri)
            im = im + (lr * ri + li * rr)
        return re, im

    first = product(u_ref[...], reached[0 : 2 * rows])
    second = product(edges, turned)
    for c in range(2):
        both = first[c] + second[c]
        both = sum(both[:, at : at + nz] for at in range(0, width, nz))
        for s in range(srcs):
            at = (6 + c) * srcs + s
            acc_ref[at : at + 1, :] = acc_ref[at : at + 1, :] + fold(both[s * REACH : (s + 1) * REACH])

    column = jnp.sum(acc_ref[...], axis=1, keepdims=True)
    row = lax.broadcasted_iota(jnp.int32, acc_ref.shape, 0)
    lane = lax.broadcasted_iota(jnp.int32, acc_ref.shape, 1)
    out_ref[...] = jnp.broadcast_to(fold(jnp.where(row == lane, column, 0.0)), out_ref.shape)


def complex_mul(left, right):
    return (left[0] * right[0] - left[1] * right[1], left[0] * right[1] + left[1] * right[0])


def complex_div(left, right):
    norm_sq = right[0] * right[0] + right[1] * right[1]
    return (
        (left[0] * right[0] + left[1] * right[1]) / norm_sq,
        (left[1] * right[0] - left[0] * right[1]) / norm_sq,
    )


def output_kernel(tot_ref, table_ref, b_ref, h_ref, out_hbm, coef_ref, buf_ref, sems):
    fields, cx, ny, nz = b_ref.shape
    srcs = fields // 2
    planes = buf_ref.shape[3]
    shape = (srcs, LANES)
    wide = jnp.broadcast_to(fold(tot_ref[...]), (8 * srcs, LANES))
    row = lax.broadcasted_iota(jnp.int32, wide.shape, 0)
    lane = lax.broadcasted_iota(jnp.int32, wide.shape, 1)
    wide = jnp.broadcast_to(jnp.sum(jnp.where(row == lane, wide, 0.0), axis=1, keepdims=True), wide.shape)
    nu = [
        (wide[2 * k * srcs : (2 * k + 1) * srcs], wide[(2 * k + 1) * srcs : (2 * k + 2) * srcs])
        for k in range(4)
    ]
    zeta = (
        jnp.broadcast_to(table_ref[0:1, :], shape),
        jnp.broadcast_to(table_ref[1:2, :], shape),
    )
    scaled = complex_mul(zeta, nu[0])
    alpha_first = complex_div(nu[0], (scaled[0] - nu[1][0], scaled[1] - nu[1][1]))
    mean = complex_div(nu[1], nu[0])
    t = complex_mul(mean, nu[1])
    spread2 = (nu[2][0] - t[0], nu[2][1] - t[1])
    t = complex_mul(mean, (nu[2][0] + spread2[0], nu[2][1] + spread2[1]))
    spread3 = (nu[3][0] - t[0], nu[3][1] - t[1])
    square = complex_mul(alpha_first, alpha_first)
    rho_next = complex_mul(square, spread2)
    beta = complex_div(rho_next, nu[0])
    first_part = complex_mul(zeta, rho_next)
    second = complex_mul(square, spread3)
    third = complex_div(complex_mul(beta, rho_next), alpha_first)
    alpha_next = complex_div(
        rho_next, (first_part[0] - second[0] - third[0], first_part[1] - second[1] - third[1])
    )
    t = complex_mul(alpha_first, mean)
    carried = complex_mul(alpha_next, (beta[0] - t[0], beta[1] - t[1]))
    on_source = (alpha_first[0] + carried[0], alpha_first[1] + carried[1])
    on_image = complex_mul(alpha_next, alpha_first)
    for k in range(MOMS):
        weight = (
            jnp.broadcast_to(table_ref[2 + 2 * k : 3 + 2 * k, :], shape),
            jnp.broadcast_to(table_ref[3 + 2 * k : 4 + 2 * k, :], shape),
        )
        for n, value in enumerate((on_source, on_image)):
            both = complex_mul(weight, value)
            for c in range(2):
                column = jnp.sum(both[c], axis=1, keepdims=True)
                coef_ref[4 * k + 2 * n + c, 0:srcs, :] = jnp.broadcast_to(column, shape)

    copies = []
    for s in range(srcs):
        for k in range(MOMS):
            c = [
                jnp.broadcast_to(coef_ref[4 * k + n, s : s + 1, :], (ny, nz)) for n in range(4)
            ]
            for x in range(planes):
                br, bi = b_ref[s, x], b_ref[srcs + s, x]
                hr, hi = h_ref[s, x], h_ref[srcs + s, x]
                buf_ref[s, k, 0, x] = c[0] * br - c[1] * bi + (c[2] * hr - c[3] * hi)
                buf_ref[s, k, 1, x] = c[0] * bi + c[1] * br + (c[2] * hi + c[3] * hr)
        copy = pltpu.make_async_copy(buf_ref.at[s], out_hbm.at[:, :, s], sems.at[s])
        copy.start()
        copies.append(copy)
    for copy in copies:
        copy.wait()


def ring(count, step):
    return [(i, (i + step) % count) for i in range(count)]


ANY = pl.BlockSpec(memory_space=pl.ANY)
HBM = pl.BlockSpec(memory_space=pltpu.HBM)
VMEM = pl.BlockSpec(memory_space=pltpu.VMEM)
SMEM = pl.BlockSpec(memory_space=pltpu.SMEM)


def shaped(*dims):
    return jax.ShapeDtypeStruct(dims, jnp.float32)


def small(mib):
    return pltpu.CompilerParams(vmem_limit_bytes=mib << 20)


def cost(flops, nbytes):
    return pl.CostEstimate(flops=flops, bytes_accessed=nbytes, transcendentals=0)


def per_device(source_real, source_imag, potential, center, radius):
    srcs, cx, ny, nz = source_real.shape
    fields = 2 * srcs
    py, pz, quads = lax.axis_size("py"), lax.axis_size("pz"), lax.axis_size("quad")
    owned = cx // quads
    reach = min(cx, owned + REACH)
    count = owned + 2 * REACH
    cells = reach * ny * nz

    source_real, source_imag, potential = (
        pltpu.with_memory_space_constraint(a, pltpu.HBM)
        for a in (source_real, source_imag, potential)
    )
    part = shaped(fields, reach, ny, nz)
    flat = shaped(2 * fields * REACH + 2 * REACH, cx * ny)
    b, pot, up, down, zup, zdown = pl.pallas_call(
        functools.partial(load_kernel, owned),
        out_shape=(
            shaped(fields, cx, ny, nz),
            shaped(cx, ny, nz),
            shaped(fields * reach * REACH, nz),
            shaped((fields * (count + owned) + owned) * REACH, nz),
            flat,
            flat,
        ),
        in_specs=[HBM] * 3,
        out_specs=(VMEM,) * 6,
        scratch_shapes=[
            pltpu.VMEM((cx * ny, nz), jnp.float32),
            pltpu.SemaphoreType.DMA((fields + 1, quads)),
        ],
        compiler_params=small(8),
        name="load",
    )(source_real, source_imag, potential)
    above = lax.ppermute(down, "py", ring(py, -1))
    below = lax.ppermute(up, "py", ring(py, 1))
    zabove = lax.ppermute(zdown, "pz", ring(pz, -1))
    zbelow = lax.ppermute(zup, "pz", ring(pz, 1))

    inner = pl.pallas_call(
        inner_kernel,
        out_shape=part,
        in_specs=[VMEM] * 2,
        out_specs=VMEM,
        scratch_shapes=[pltpu.VMEM((reach, ny + 16, nz), jnp.float32)],
        compiler_params=small(12),
        cost_estimate=cost(fields * cells * 60, fields * cells * 12),
        name="inner",
    )(b, pot)

    image, u = pl.pallas_call(
        functools.partial(border_kernel, owned),
        out_shape=(part, shaped(2 * fields * REACH, cx * ny)),
        in_specs=[VMEM] * 5,
        out_specs=(VMEM,) * 2,
        scratch_shapes=[
            pltpu.VMEM((2, reach, 16, nz), jnp.float32),
            pltpu.VMEM((cx * ny, nz), jnp.float32),
        ],
        compiler_params=small(12),
        name="border",
    )(inner, below, above, zbelow, zabove)

    devices = quads * py * pz
    partial = pl.pallas_call(
        functools.partial(sums_kernel, owned),
        out_shape=shaped(devices, LANES),
        in_specs=[VMEM] * 9,
        out_specs=VMEM,
        scratch_shapes=[
            pltpu.VMEM((8 * srcs, nz), jnp.float32),
            pltpu.VMEM((fields, owned, ny, nz), jnp.float32),
            pltpu.VMEM((fields, owned * REACH, nz), jnp.float32),
        ],
        compiler_params=small(12),
        name="sums",
    )(b, pot, image, u, above, zup, zdown, zbelow, zabove)

    total = lax.all_to_all(partial, ("quad", "py", "pz"), 0, 0)

    table = jnp.asarray(phase_table())
    row = lax.broadcasted_iota(jnp.int32, table.shape, 0)
    table = radius * table + jnp.where(row == 0, center - MIDDLE, 0.0)
    return pl.pallas_call(
        output_kernel,
        out_shape=shaped(MOMS, 2, srcs, owned, ny, nz),
        in_specs=[VMEM] * 4,
        out_specs=HBM,
        scratch_shapes=[
            pltpu.VMEM((4 * MOMS, 8, LANES), jnp.float32),
            pltpu.VMEM((srcs, MOMS, 2, owned, ny, nz), jnp.float32),
            pltpu.SemaphoreType.DMA((srcs,)),
        ],
        compiler_params=small(12),
        name="output",
    )(total, table, b, image)


def solution(mesh):
    in_specs = (P(None, None, "py", "pz"), P(None, None, "py", "pz"), P(None, "py", "pz"), P(), P())
    out_specs = P(None, None, None, "quad", "py", "pz")
    return jax.shard_map(
        per_device, mesh=mesh, in_specs=in_specs, out_specs=out_specs, check_vma=False
    )
```

```python
import functools
import math

import jax
import jax.numpy as jnp
import numpy as np
from jax import lax
from jax.experimental import pallas as pl
from jax.experimental.pallas import tpu as pltpu
from jax.sharding import PartitionSpec as P

QPTS = 8
MOMS = 4
REACH = 4
LANES = 128

stencil_weights = (-205.0 / 72.0, 8.0 / 5.0, -1.0 / 5.0, 8.0 / 315.0, -1.0 / 560.0)
DIAG = -1.5 * stencil_weights[0]
MIDDLE = 5.25
SIDE = tuple(-0.5 * w for w in stencil_weights)
HIGHEST = lax.Precision.HIGHEST


def dot(left, right, dims):
    return lax.dot_general(
        left, right, (dims, ((), ())), precision=HIGHEST, preferred_element_type=jnp.float32
    )


def band(shape, offset, signs, scale=1.0):
    step = offset + lax.broadcasted_iota(jnp.int32, shape, 0) - lax.broadcasted_iota(jnp.int32, shape, 1)
    out = jnp.zeros(shape, jnp.float32)
    for k in range(1, REACH + 1):
        for sign in signs:
            out = jnp.where(step == sign * k, scale * SIDE[k], out)
    return out


def split(value):
    high = value.astype(jnp.bfloat16)
    return high, (value - high.astype(jnp.float32)).astype(jnp.bfloat16)


def wide_left(value):
    high, low = split(value)
    return jnp.concatenate([high, low, high], axis=1)


def wide_right(value):
    high, low = split(value)
    return jnp.concatenate([high, high, low], axis=0)


def mul(left, right):
    return lax.dot_general(left, right, (((1,), (0,)), ((), ())), preferred_element_type=jnp.float32)


def gather_edges(gathered, f, value):
    lane = lax.broadcasted_iota(jnp.int32, value.shape, 1)
    moved = pltpu.roll(value, 4 * REACH * f + 2 * REACH, 1)
    return jnp.where(lane // (4 * REACH) == f, moved, gathered)


def load_kernel(
    owned, re_hbm, im_hbm, pot_hbm, b_ref, pot_ref, up_ref, down_ref, zup_ref, zdown_ref, edge_ref, sems
):
    fields, cx, ny, nz = b_ref.shape
    srcs = fields // 2
    parts = cx // owned
    reach = up_ref.shape[0] // (fields * REACH)
    first = lax.axis_index("quad")
    copies = []
    for f in range(fields + 1):
        source = pot_hbm if f == fields else (re_hbm, im_hbm)[f // srcs].at[f % srcs]
        target = pot_ref if f == fields else b_ref.at[f]
        group = []
        for j in range(parts):
            at = pl.multiple_of(lax.rem(first + j, parts) * owned, owned)
            group.append(
                pltpu.make_async_copy(
                    source.at[pl.ds(at, owned)], target.at[pl.ds(j * owned, owned)], sems.at[f, j]
                )
            )
        copies.append(group)
    for group in copies:
        for copy in group:
            copy.start()
    edge_ref[...] = jnp.zeros(edge_ref.shape, jnp.float32)
    far = fields * reach
    for f in range(fields):
        for copy in copies[f]:
            copy.wait()
        for x in range(reach):
            at = (f * reach + x) * REACH
            up_ref[at : at + REACH, :] = b_ref[f, x, ny - REACH : ny, :]
            down_ref[at : at + REACH, :] = b_ref[f, x, 0:REACH, :]
        for x in range(owned):
            at = (far + f * owned + x) * REACH
            down_ref[at : at + REACH, :] = b_ref[f, x, REACH : 2 * REACH, :]
        edge_ref[...] = gather_edges(edge_ref[...], f, b_ref[f].reshape(cx * ny, nz))
    for copy in copies[fields]:
        copy.wait()
    pot_ref[...] = pot_ref[...] + (DIAG - MIDDLE)
    for x in range(owned):
        at = (far + fields * owned + x) * REACH
        down_ref[at : at + REACH, :] = pot_ref[x, 0:REACH, :]
    turned = pltpu.roll(pot_ref[...].reshape(cx * ny, nz), 2 * REACH, 1).T
    rows = fields * REACH
    after = rows + rows // 2
    zup_ref[after : after + REACH, :] = turned[REACH : 2 * REACH]
    zup_ref[after + REACH : after + 2 * REACH, :] = turned[0:REACH]
    zdown_ref[after : after + 2 * REACH, :] = turned[2 * REACH : 4 * REACH]
    turned = edge_ref[...].T
    for f in range(fields):
        at = 4 * REACH * f
        low, high = f * REACH, (f + 1) * REACH
        zup_ref[low:high, :] = turned[at + REACH : at + 2 * REACH]
        zdown_ref[low:high, :] = turned[at + 2 * REACH : at + 3 * REACH]
        side, spot = f // srcs * LANES, rows + f % srcs * REACH
        lanes = slice(side, side + LANES)
        zup_ref[spot : spot + REACH, lanes] = turned[at : at + REACH, 0:LANES]
        zdown_ref[spot : spot + REACH, lanes] = turned[at + 3 * REACH : at + 4 * REACH, 0:LANES]


def phase_table():
    lane = np.arange(LANES)
    angle = 2.0 * math.pi * (lane % QPTS + 0.5) / QPTS
    rows = [np.cos(angle), np.sin(angle)]
    for k in range(1, MOMS + 1):
        rows.append(np.where(lane < QPTS, np.cos(k * angle), 0.0) / QPTS)
        rows.append(np.where(lane < QPTS, np.sin(k * angle), 0.0) / QPTS)
    rows += [np.zeros(LANES)] * (-len(rows) % 8)
    return np.stack(rows).astype(np.float32)


def links(row_at, col_at, row_field, col_field):
    step = jnp.abs(row_at - col_at)
    out = jnp.zeros(step.shape, jnp.float32)
    for k in range(1, REACH + 1):
        out = jnp.where((step == k) & (row_field == col_field), SIDE[k], out)
    return out


def layer_of(index, starts, rows):
    layer = jnp.full(index.shape, 1 << 20, jnp.int32)
    for n, start in enumerate(starts):
        layer = jnp.where(index // rows == n, start + index % REACH, layer)
    return layer, index % rows // REACH


def around(value, ny):
    y = lax.broadcasted_iota(jnp.int32, value.shape, 1) % ny
    width = value.shape[1]
    out = jnp.zeros(value.shape, jnp.float32)
    for k in range(1, REACH + 1):
        sides = jnp.where(y >= ny - k, pltpu.roll(value, ny - k, 1), 0.0)
        sides = sides + jnp.where(y < k, pltpu.roll(value, width + k - ny, 1), 0.0)
        out = out + SIDE[k] * sides
    return out


def inner_kernel(
    owned,
    b_ref,
    pot_ref,
    zup_ref,
    zdown_ref,
    out_ref,
    both_ref,
    half_ref,
    beyond_ref,
    back_ref,
    fix_ref,
    edges_ref,
    pad_ref,
):
    fields, cx, ny, nz = b_ref.shape
    reach = out_ref.shape[1]
    rows = fields * REACH
    both_ref[...] = wide_right(band((nz, nz), 0, (1, -1)))
    half_ref[...] = wide_right(band((nz, nz), 0, (1,), 2.0))
    for f in range(fields):
        own = b_ref[f, 0:reach].reshape(reach * ny, nz)
        out_ref[f] = mul(wide_left(own), both_ref[...]).reshape(reach, ny, nz)
    zero = jnp.zeros((reach, 8, nz), jnp.float32)
    pad_ref[:, 0:8, :] = zero
    pad_ref[:, 8 + ny : 16 + ny, :] = zero

    def field(f, _):
        pad_ref[:, 8 : 8 + ny, :] = b_ref[f, 0:reach]
        for x in range(reach):
            total = out_ref[f, x] + pot_ref[x] * b_ref[f, x]
            for k in range(1, REACH + 1):
                sides = b_ref[f, (x + k) % cx] + b_ref[f, (x - k) % cx]
                sides = sides + pad_ref[x, 8 + k : 8 + k + ny, :]
                sides = sides + pad_ref[x, 8 - k : 8 - k + ny, :]
                total = total + SIDE[k] * sides
            out_ref[f, x] = total
        return 0

    lax.fori_loop(0, fields, field, 0)

    shape = (2 * rows, 8 * rows)
    row_at, row_field = layer_of(lax.broadcasted_iota(jnp.int32, shape, 0), (-REACH, nz), rows)
    starts = (0, nz - REACH, -REACH, -2 * REACH, nz, nz + REACH)
    col_at, col_field = layer_of(lax.broadcasted_iota(jnp.int32, shape, 1), starts, rows)
    beyond_ref[...] = wide_left(links(row_at, col_at, row_field, col_field))
    shape = (4 * rows, 4 * rows)
    row = lax.broadcasted_iota(jnp.int32, shape, 0)
    col = lax.broadcasted_iota(jnp.int32, shape, 1)
    row_at, row_field = layer_of(row % (2 * rows), (0, nz - REACH), rows)
    col_at, col_field = layer_of(col % (2 * rows), (-REACH, nz), rows)
    same = row // (2 * rows) == col // (2 * rows)
    back_ref[...] = wide_left(jnp.where(same, links(row_at, col_at, row_field, col_field), 0.0))
    shape = (2 * rows, nz)
    layer, owner = layer_of(lax.broadcasted_iota(jnp.int32, shape, 0), (-REACH, nz), rows)
    cell = lax.broadcasted_iota(jnp.int32, shape, 1)
    for f in range(fields):
        fix_ref[f] = wide_right(links(layer, cell, owner, f))
    lane = lax.broadcasted_iota(jnp.int32, (2 * rows, LANES), 1)
    weight = jnp.where(lane < owned * ny, jnp.where(lane % ny >= ny // 2, 3.0, 1.0), 0.0)
    edges = jnp.concatenate([zdown_ref[0:rows, 0:LANES], zup_ref[0:rows, 0:LANES]], axis=0)
    edges_ref[...] = around(edges, ny) * weight


def fold(value):
    return jnp.sum(value, axis=0, keepdims=True)


def product(left, right):
    return left[0] * right[0] - left[1] * right[1], left[0] * right[1] + left[1] * right[0]


def main_kernel(
    owned,
    b_ref,
    pot_ref,
    inner_ref,
    below_ref,
    above_ref,
    zup_ref,
    zdown_ref,
    zbelow_ref,
    zabove_ref,
    both_ref,
    half_ref,
    beyond_ref,
    back_ref,
    fix_ref,
    edges_ref,
    h_ref,
    out_ref,
    pad_ref,
    edge_ref,
    acc_ref,
    step_ref,
    far_ref,
    pull_ref,
):
    fields, reach, ny, nz = inner_ref.shape
    cx = b_ref.shape[1]
    srcs = fields // 2
    rows = fields * REACH
    after = rows + rows // 2

    outer = jnp.concatenate([zbelow_ref[0:rows], zabove_ref[0:rows]], axis=0)
    wide = wide_left(outer.T[0 : reach * ny])
    near = outer[:, 0:LANES]

    def second(ref):
        return [ref[rows:after, 0:LANES], ref[rows:after, LANES : 2 * LANES]]

    stack = jnp.concatenate(
        [zdown_ref[0:rows, 0:LANES], zup_ref[0:rows, 0:LANES], near[0:rows]]
        + second(zbelow_ref)
        + [near[rows : 2 * rows]]
        + second(zabove_ref)
        + [near],
        axis=0,
    )
    image = mul(beyond_ref[...], wide_right(stack))
    local = jnp.concatenate(
        [zbelow_ref[after : after + REACH, 0:LANES]] * fields
        + [zabove_ref[after : after + REACH, 0:LANES]] * fields,
        axis=0,
    )
    image = image + local * near
    y = lax.broadcasted_iota(jnp.int32, (2 * rows, LANES), 1) % ny
    width = cx * ny
    for k in range(1, REACH + 1):
        sides = pltpu.roll(outer, ny * k, 1) + pltpu.roll(outer, width - ny * k, 1)
        sides = sides[:, 0:LANES] + jnp.where(y >= k, pltpu.roll(near, k, 1), 0.0)
        sides = sides + jnp.where(y < ny - k, pltpu.roll(near, LANES - k, 1), 0.0)
        image = image + SIDE[k] * sides
    reached = mul(back_ref[...], wide_right(jnp.concatenate([image, near], axis=0)))
    turned = around(reached[2 * rows : 4 * rows], ny)

    for f in range(fields):
        h_ref[f] = mul(wide, fix_ref[f]).reshape(reach, ny, nz)
    zero = jnp.zeros((reach, 16, nz), jnp.float32)
    pad_ref[0] = zero
    pad_ref[1] = zero
    edge_ref[...] = jnp.zeros(edge_ref.shape, jnp.float32)
    for f in range(fields):
        for x in range(reach):
            at = (f * reach + x) * REACH
            pad_ref[0, x, 8 - REACH : 8, :] = below_ref[at : at + REACH, :]
            pad_ref[1, x, 8 : 8 + REACH, :] = above_ref[at : at + REACH, :]
        for x in range(reach):
            low = SIDE[1] * pad_ref[0, x, 7:15, :]
            high = SIDE[1] * pad_ref[1, x, 1:9, :]
            for k in range(2, REACH + 1):
                low = low + SIDE[k] * pad_ref[0, x, 8 - k : 16 - k, :]
                high = high + SIDE[k] * pad_ref[1, x, k : 8 + k, :]
            total = h_ref[f, x] + inner_ref[f, x]
            middle = [total[8 : ny - 8]] if ny > 16 else []
            first, last = total[0:8] + low, total[ny - 8 : ny] + high
            h_ref[f, x] = jnp.concatenate([first] + middle + [last], axis=0)
            if x < owned:
                u = jnp.concatenate([first + low] + middle + [last + 3.0 * high], axis=0)
                spot = pl.ds(x * ny, ny)
                edge_ref[spot, :] = gather_edges(edge_ref[spot, :], f, u)

    for f in range(fields):
        own = h_ref[f, 0:owned].reshape(owned * ny, nz)
        step_ref[f] = mul(wide_left(own), half_ref[...]).reshape(owned, ny, nz)
        at = f * reach * REACH
        far_ref[f] = mul(wide_left(above_ref[at : at + owned * REACH, :]), both_ref[...])

    quad_row = lax.broadcasted_iota(jnp.int32, (8, nz), 0) % REACH
    early = lax.broadcasted_iota(jnp.int32, (8, nz), 0) < REACH

    def top(ref, f, x):
        return jnp.where(early, pltpu.roll(ref[f, x, ny - 8 : ny, :], REACH, 0), ref[f, x + 1, ny - 8 : ny, :])

    def lowered(lower, upper, k):
        if k == REACH:
            return lower
        return jnp.where(quad_row >= k, pltpu.roll(upper, k, 0), pltpu.roll(lower, REACH + k, 0))

    def raised(lower, upper, k):
        if k == REACH:
            return upper
        return jnp.where(quad_row < REACH - k, pltpu.roll(lower, 8 - k, 0), pltpu.roll(upper, REACH - k, 0))

    for f in range(fields):
        for x in range(0, reach, 2):
            own = top(h_ref, f, x)
            pull = SIDE[REACH] * own
            for k in range(1, REACH):
                pull = pull + SIDE[k] * jnp.where(quad_row < k, pltpu.roll(own, REACH + k, 0), 0.0)
            at = (f * reach + x) * REACH
            pull_ref[at : at + 8, :] = pull

    row = lax.broadcasted_iota(jnp.int32, (ny, nz), 0)
    inside = [row < ny - k for k in range(REACH + 1)]
    for s in range(srcs):
        total = [jnp.zeros((ny, nz), jnp.float32) for _ in range(8)]
        for x in range(owned):
            local = pot_ref[x]
            b = (b_ref[s, x], b_ref[srcs + s, x])
            h, g = [], []
            for part in range(2):
                f = part * srcs + s
                own = h_ref[f, x]
                value = step_ref[f, x] + local * own
                for k in range(1, REACH + 1):
                    up = jnp.where(inside[k], pltpu.roll(own, ny - k, 0), 0.0)
                    value = value + (2.0 * SIDE[k]) * (h_ref[f, (x + k) % cx] + up)
                h.append(own)
                g.append(value)
            terms = product(b, b) + product(b, h) + product(h, h) + product(h, g)
            total = [t + v for t, v in zip(total, terms)]
        cross = [jnp.zeros((8, nz), jnp.float32) for _ in range(2)]
        for x in range(0, owned, 2):
            at = (fields * (reach + owned) + x) * REACH
            local = above_ref[at : at + 8, :]
            left, right, first, pulls = [], [], [], []
            for part in range(2):
                f = part * srcs + s
                at = (f * reach + x) * REACH
                own = top(b_ref, f, x)
                first_layers = above_ref[at : at + 8, :]
                start = (fields * reach + f * owned + x) * REACH
                more = above_ref[start : start + 8, :]
                value = far_ref[f, x * REACH : x * REACH + 8, :] + local * first_layers
                pull = 0.0
                for k in range(1, REACH + 1):
                    sides = above_ref[at + k * REACH : at + k * REACH + 8, :]
                    sides = sides + raised(first_layers, more, k) + lowered(own, first_layers, k)
                    value = value + SIDE[k] * sides
                    pull = pull + SIDE[k] * pull_ref[at + k * REACH : at + k * REACH + 8, :]
                left.append(pull_ref[at : at + 8, :])
                right.append(value)
                first.append(first_layers)
                pulls.append(pull)
            for c, (one, two) in enumerate(zip(product(left, right), product(first, pulls))):
                cross[c] = cross[c] + (one + two)
        for i in range(8):
            value = fold(total[i])
            if i >= 6:
                value = value + 2.0 * fold(cross[i - 6])
            acc_ref[i * srcs + s : i * srcs + s + 1, :] = value

    gathered = edge_ref[...].T
    part = rows // 2
    both = [0.0, 0.0]
    for side in range(2):
        at = (1 - side) * REACH + REACH
        u = jnp.concatenate(
            [gathered[4 * REACH * f + at : 4 * REACH * f + at + REACH] for f in range(fields)], axis=0
        )
        base = side * rows
        for left, right in ((u, reached), (edges_ref[base : base + rows], turned)):
            terms = product(
                (left[0:part], left[part:rows]), (right[base : base + part], right[base + part : base + rows])
            )
            both = [t + v for t, v in zip(both, terms)]
    for c in range(2):
        for s in range(srcs):
            at = (6 + c) * srcs + s
            acc_ref[at : at + 1, :] = acc_ref[at : at + 1, :] + fold(both[c][s * REACH : (s + 1) * REACH])

    column = jnp.sum(acc_ref[...], axis=1, keepdims=True)
    row = lax.broadcasted_iota(jnp.int32, acc_ref.shape, 0)
    lane = lax.broadcasted_iota(jnp.int32, acc_ref.shape, 1)
    out_ref[...] = jnp.broadcast_to(fold(jnp.where(row == lane, column, 0.0)), out_ref.shape)


def complex_mul(left, right):
    return (left[0] * right[0] - left[1] * right[1], left[0] * right[1] + left[1] * right[0])


def complex_div(left, right):
    norm_sq = right[0] * right[0] + right[1] * right[1]
    return (
        (left[0] * right[0] + left[1] * right[1]) / norm_sq,
        (left[1] * right[0] - left[0] * right[1]) / norm_sq,
    )


def output_kernel(tot_ref, table_ref, b_ref, h_ref, out_hbm, coef_ref, buf_ref, sems):
    fields, cx, ny, nz = b_ref.shape
    srcs = fields // 2
    planes = buf_ref.shape[3]
    shape = (srcs, LANES)
    wide = jnp.broadcast_to(fold(tot_ref[...]), (8 * srcs, LANES))
    row = lax.broadcasted_iota(jnp.int32, wide.shape, 0)
    lane = lax.broadcasted_iota(jnp.int32, wide.shape, 1)
    wide = jnp.broadcast_to(jnp.sum(jnp.where(row == lane, wide, 0.0), axis=1, keepdims=True), wide.shape)
    nu = [
        (wide[2 * k * srcs : (2 * k + 1) * srcs], wide[(2 * k + 1) * srcs : (2 * k + 2) * srcs])
        for k in range(4)
    ]
    zeta = (
        jnp.broadcast_to(table_ref[0:1, :], shape),
        jnp.broadcast_to(table_ref[1:2, :], shape),
    )
    scaled = complex_mul(zeta, nu[0])
    alpha_first = complex_div(nu[0], (scaled[0] - nu[1][0], scaled[1] - nu[1][1]))
    mean = complex_div(nu[1], nu[0])
    t = complex_mul(mean, nu[1])
    spread2 = (nu[2][0] - t[0], nu[2][1] - t[1])
    t = complex_mul(mean, (nu[2][0] + spread2[0], nu[2][1] + spread2[1]))
    spread3 = (nu[3][0] - t[0], nu[3][1] - t[1])
    square = complex_mul(alpha_first, alpha_first)
    rho_next = complex_mul(square, spread2)
    beta = complex_div(rho_next, nu[0])
    first_part = complex_mul(zeta, rho_next)
    second = complex_mul(square, spread3)
    third = complex_div(complex_mul(beta, rho_next), alpha_first)
    alpha_next = complex_div(
        rho_next, (first_part[0] - second[0] - third[0], first_part[1] - second[1] - third[1])
    )
    t = complex_mul(alpha_first, mean)
    carried = complex_mul(alpha_next, (beta[0] - t[0], beta[1] - t[1]))
    on_source = (alpha_first[0] + carried[0], alpha_first[1] + carried[1])
    on_image = complex_mul(alpha_next, alpha_first)
    for k in range(MOMS):
        weight = (
            jnp.broadcast_to(table_ref[2 + 2 * k : 3 + 2 * k, :], shape),
            jnp.broadcast_to(table_ref[3 + 2 * k : 4 + 2 * k, :], shape),
        )
        for n, value in enumerate((on_source, on_image)):
            both = complex_mul(weight, value)
            for c in range(2):
                column = jnp.sum(both[c], axis=1, keepdims=True)
                coef_ref[4 * k + 2 * n + c, 0:srcs, :] = jnp.broadcast_to(column, shape)

    copies = []
    for s in range(srcs):
        for k in range(MOMS):
            c = [
                jnp.broadcast_to(coef_ref[4 * k + n, s : s + 1, :], (ny, nz)) for n in range(4)
            ]
            for x in range(planes):
                br, bi = b_ref[s, x], b_ref[srcs + s, x]
                hr, hi = h_ref[s, x], h_ref[srcs + s, x]
                buf_ref[s, k, 0, x] = c[0] * br - c[1] * bi + (c[2] * hr - c[3] * hi)
                buf_ref[s, k, 1, x] = c[0] * bi + c[1] * br + (c[2] * hi + c[3] * hr)
        copy = pltpu.make_async_copy(buf_ref.at[s], out_hbm.at[:, :, s], sems.at[s])
        copy.start()
        copies.append(copy)
    for copy in copies:
        copy.wait()


def ring(count, step):
    return [(i, (i + step) % count) for i in range(count)]


ANY = pl.BlockSpec(memory_space=pl.ANY)
HBM = pl.BlockSpec(memory_space=pltpu.HBM)
VMEM = pl.BlockSpec(memory_space=pltpu.VMEM)
SMEM = pl.BlockSpec(memory_space=pltpu.SMEM)


def shaped(*dims):
    return jax.ShapeDtypeStruct(dims, jnp.float32)


def small(mib):
    return pltpu.CompilerParams(vmem_limit_bytes=mib << 20)


def cost(flops, nbytes):
    return pl.CostEstimate(flops=flops, bytes_accessed=nbytes, transcendentals=0)


def per_device(source_real, source_imag, potential, center, radius):
    srcs, cx, ny, nz = source_real.shape
    fields = 2 * srcs
    py, pz, quads = lax.axis_size("py"), lax.axis_size("pz"), lax.axis_size("quad")
    owned = cx // quads
    reach = min(cx, owned + REACH)
    cells = reach * ny * nz
    rows = fields * REACH

    source_real, source_imag, potential = (
        pltpu.with_memory_space_constraint(a, pltpu.HBM)
        for a in (source_real, source_imag, potential)
    )
    part = shaped(fields, reach, ny, nz)
    flat = shaped(rows + rows // 2 + 2 * REACH, cx * ny)
    b, pot, up, down, zup, zdown = pl.pallas_call(
        functools.partial(load_kernel, owned),
        out_shape=(
            shaped(fields, cx, ny, nz),
            shaped(cx, ny, nz),
            shaped(fields * reach * REACH, nz),
            shaped((fields * (reach + owned) + owned) * REACH, nz),
            flat,
            flat,
        ),
        in_specs=[HBM] * 3,
        out_specs=(VMEM,) * 6,
        scratch_shapes=[
            pltpu.VMEM((cx * ny, nz), jnp.float32),
            pltpu.SemaphoreType.DMA((fields + 1, quads)),
        ],
        compiler_params=small(8),
        name="load",
    )(source_real, source_imag, potential)
    above = lax.ppermute(down, "py", ring(py, -1))
    below = lax.ppermute(up, "py", ring(py, 1))
    zabove = lax.ppermute(zdown, "pz", ring(pz, -1))
    zbelow = lax.ppermute(zup, "pz", ring(pz, 1))

    half = lambda *dims: jax.ShapeDtypeStruct(dims, jnp.bfloat16)
    inner, *weights = pl.pallas_call(
        functools.partial(inner_kernel, owned),
        out_shape=(
            part,
            half(3 * nz, nz),
            half(3 * nz, nz),
            half(2 * rows, 24 * rows),
            half(4 * rows, 12 * rows),
            half(fields, 6 * rows, nz),
            shaped(2 * rows, LANES),
        ),
        in_specs=[VMEM] * 4,
        out_specs=(VMEM,) * 7,
        scratch_shapes=[pltpu.VMEM((reach, ny + 16, nz), jnp.float32)],
        compiler_params=small(12),
        cost_estimate=cost(fields * cells * 60, fields * cells * 12),
        name="inner",
    )(b, pot, zup, zdown)

    devices = quads * py * pz
    image, partial = pl.pallas_call(
        functools.partial(main_kernel, owned),
        out_shape=(part, shaped(devices, LANES)),
        in_specs=[VMEM] * 15,
        out_specs=(VMEM,) * 2,
        scratch_shapes=[
            pltpu.VMEM((2, reach, 16, nz), jnp.float32),
            pltpu.VMEM((LANES, nz), jnp.float32),
            pltpu.VMEM((8 * srcs, nz), jnp.float32),
            pltpu.VMEM((fields, owned, ny, nz), jnp.float32),
            pltpu.VMEM((fields, owned * REACH, nz), jnp.float32),
            pltpu.VMEM((fields * reach * REACH, nz), jnp.float32),
        ],
        compiler_params=small(12),
        name="main",
    )(b, pot, inner, below, above, zup, zdown, zbelow, zabove, *weights)

    total = lax.all_to_all(partial, ("quad", "py", "pz"), 0, 0)

    table = jnp.asarray(phase_table())
    row = lax.broadcasted_iota(jnp.int32, table.shape, 0)
    table = radius * table + jnp.where(row == 0, center - MIDDLE, 0.0)
    return pl.pallas_call(
        output_kernel,
        out_shape=shaped(MOMS, 2, srcs, owned, ny, nz),
        in_specs=[VMEM] * 4,
        out_specs=HBM,
        scratch_shapes=[
            pltpu.VMEM((4 * MOMS, 8, LANES), jnp.float32),
            pltpu.VMEM((srcs, MOMS, 2, owned, ny, nz), jnp.float32),
            pltpu.SemaphoreType.DMA((srcs,)),
        ],
        compiler_params=small(12),
        name="output",
    )(total, table, b, image)


def solution(mesh):
    in_specs = (P(None, None, "py", "pz"), P(None, None, "py", "pz"), P(None, "py", "pz"), P(), P())
    out_specs = P(None, None, None, "quad", "py", "pz")
    return jax.shard_map(
        per_device, mesh=mesh, in_specs=in_specs, out_specs=out_specs, check_vma=False
    )
```

```python
import functools
import math

import jax
import jax.numpy as jnp
import numpy as np
from jax import lax
from jax.experimental import pallas as pl
from jax.experimental.pallas import tpu as pltpu
from jax.sharding import PartitionSpec as P

QPTS = 8
MOMS = 4
REACH = 4
LANES = 128

stencil_weights = (-205.0 / 72.0, 8.0 / 5.0, -1.0 / 5.0, 8.0 / 315.0, -1.0 / 560.0)
DIAG = -1.5 * stencil_weights[0]
MIDDLE = 5.25
SIDE = tuple(-0.5 * w for w in stencil_weights)
HIGHEST = lax.Precision.HIGHEST


def dot(left, right, dims):
    return lax.dot_general(
        left, right, (dims, ((), ())), precision=HIGHEST, preferred_element_type=jnp.float32
    )


def band(shape, offset, signs, scale=1.0):
    step = offset + lax.broadcasted_iota(jnp.int32, shape, 0) - lax.broadcasted_iota(jnp.int32, shape, 1)
    out = jnp.zeros(shape, jnp.float32)
    for k in range(1, REACH + 1):
        for sign in signs:
            out = jnp.where(step == sign * k, scale * SIDE[k], out)
    return out


def split(value):
    high = value.astype(jnp.bfloat16)
    return high, (value - high.astype(jnp.float32)).astype(jnp.bfloat16)


def wide_left(value):
    high, low = split(value)
    return jnp.concatenate([high, low, high], axis=1)


def wide_right(value):
    high, low = split(value)
    return jnp.concatenate([high, high, low], axis=0)


def mul(left, right):
    return lax.dot_general(left, right, (((1,), (0,)), ((), ())), preferred_element_type=jnp.float32)


def gather_edges(gathered, f, value):
    lane = lax.broadcasted_iota(jnp.int32, value.shape, 1)
    moved = pltpu.roll(value, 4 * REACH * f + 2 * REACH, 1)
    return jnp.where(lane // (4 * REACH) == f, moved, gathered)


def load_kernel(
    owned, re_hbm, im_hbm, pot_hbm, b_ref, pot_ref, up_ref, down_ref, zup_ref, zdown_ref, pick_ref, sems
):
    fields, cx, ny, nz = b_ref.shape
    srcs = fields // 2
    parts = cx // owned
    reach = up_ref.shape[0] // (fields * REACH)
    first = lax.axis_index("quad")
    copies = []
    for f in range(fields + 1):
        source = pot_hbm if f == fields else (re_hbm, im_hbm)[f // srcs].at[f % srcs]
        target = pot_ref if f == fields else b_ref.at[f]
        group = []
        for j in range(parts):
            at = pl.multiple_of(lax.rem(first + j, parts) * owned, owned)
            group.append(
                pltpu.make_async_copy(
                    source.at[pl.ds(at, owned)], target.at[pl.ds(j * owned, owned)], sems.at[f, j]
                )
            )
        copies.append(group)
    for group in copies:
        for copy in group:
            copy.start()
    shape = (2 * nz, nz)
    layer = lax.broadcasted_iota(jnp.int32, shape, 0) % nz
    lane = lax.broadcasted_iota(jnp.int32, shape, 1)
    spot = lax.rem(layer + 2 * REACH, nz)
    for f in range(fields):
        chosen = (spot < 4 * REACH) & (lane == spot + 4 * REACH * f)
        pick_ref[f] = jnp.where(chosen, 1.0, 0.0).astype(jnp.bfloat16)
    far = fields * reach
    for f in range(fields):
        for copy in copies[f]:
            copy.wait()
        for x in range(reach):
            at = (f * reach + x) * REACH
            up_ref[at : at + REACH, :] = b_ref[f, x, ny - REACH : ny, :]
            down_ref[at : at + REACH, :] = b_ref[f, x, 0:REACH, :]
        for x in range(owned):
            at = (far + f * owned + x) * REACH
            down_ref[at : at + REACH, :] = b_ref[f, x, REACH : 2 * REACH, :]
    for copy in copies[fields]:
        copy.wait()
    pot_ref[...] = pot_ref[...] + (DIAG - MIDDLE)
    for x in range(owned):
        at = (far + fields * owned + x) * REACH
        down_ref[at : at + REACH, :] = pot_ref[x, 0:REACH, :]
    turned = pltpu.roll(pot_ref[...].reshape(cx * ny, nz), 2 * REACH, 1).T
    rows = fields * REACH
    after = rows + rows // 2
    zup_ref[after : after + REACH, :] = turned[REACH : 2 * REACH]
    zup_ref[after + REACH : after + 2 * REACH, :] = turned[0:REACH]
    zdown_ref[after : after + 2 * REACH, :] = turned[2 * REACH : 4 * REACH]
    pieces = [split(b_ref[f].reshape(cx * ny, nz)) for f in range(fields)]
    wide = jnp.concatenate([half for pair in pieces for half in pair], axis=1)
    turned = mul(wide, pick_ref[...].reshape(2 * fields * nz, nz)).T
    for f in range(fields):
        at = 4 * REACH * f
        low, high = f * REACH, (f + 1) * REACH
        zup_ref[low:high, :] = turned[at + REACH : at + 2 * REACH]
        zdown_ref[low:high, :] = turned[at + 2 * REACH : at + 3 * REACH]
        side, spot = f // srcs * LANES, rows + f % srcs * REACH
        lanes = slice(side, side + LANES)
        zup_ref[spot : spot + REACH, lanes] = turned[at : at + REACH, 0:LANES]
        zdown_ref[spot : spot + REACH, lanes] = turned[at + 3 * REACH : at + 4 * REACH, 0:LANES]


def phase_table():
    lane = np.arange(LANES)
    angle = 2.0 * math.pi * (lane % QPTS + 0.5) / QPTS
    rows = [np.cos(angle), np.sin(angle)]
    for k in range(1, MOMS + 1):
        rows.append(np.where(lane < QPTS, np.cos(k * angle), 0.0) / QPTS)
        rows.append(np.where(lane < QPTS, np.sin(k * angle), 0.0) / QPTS)
    rows += [np.zeros(LANES)] * (-len(rows) % 8)
    return np.stack(rows).astype(np.float32)


def links(row_at, col_at, row_field, col_field):
    step = jnp.abs(row_at - col_at)
    out = jnp.zeros(step.shape, jnp.float32)
    for k in range(1, REACH + 1):
        out = jnp.where((step == k) & (row_field == col_field), SIDE[k], out)
    return out


def layer_of(index, starts, rows):
    layer = jnp.full(index.shape, 1 << 20, jnp.int32)
    for n, start in enumerate(starts):
        layer = jnp.where(index // rows == n, start + index % REACH, layer)
    return layer, index % rows // REACH


def around(value, ny):
    y = lax.broadcasted_iota(jnp.int32, value.shape, 1) % ny
    width = value.shape[1]
    out = jnp.zeros(value.shape, jnp.float32)
    for k in range(1, REACH + 1):
        sides = jnp.where(y >= ny - k, pltpu.roll(value, ny - k, 1), 0.0)
        sides = sides + jnp.where(y < k, pltpu.roll(value, width + k - ny, 1), 0.0)
        out = out + SIDE[k] * sides
    return out


def inner_kernel(
    owned,
    b_ref,
    pot_ref,
    zup_ref,
    zdown_ref,
    out_ref,
    both_ref,
    half_ref,
    beyond_ref,
    back_ref,
    fix_ref,
    pairs_ref,
    edges_ref,
    base_ref,
    pad_ref,
):
    fields, cx, ny, nz = b_ref.shape
    srcs = fields // 2
    reach = out_ref.shape[1]
    rows = fields * REACH
    both_ref[...] = wide_right(band((nz, nz), 0, (1, -1)))
    half_ref[...] = wide_right(band((nz, nz), 0, (1,), 2.0))
    for f in range(fields):
        own = b_ref[f, 0:reach].reshape(reach * ny, nz)
        out_ref[f] = mul(wide_left(own), both_ref[...]).reshape(reach, ny, nz)
    zero = jnp.zeros((reach, 8, nz), jnp.float32)
    pad_ref[:, 0:8, :] = zero
    pad_ref[:, 8 + ny : 16 + ny, :] = zero

    def field(f, _):
        pad_ref[:, 8 : 8 + ny, :] = b_ref[f, 0:reach]
        for x in range(reach):
            total = out_ref[f, x] + pot_ref[x] * b_ref[f, x]
            for k in range(1, REACH + 1):
                sides = b_ref[f, (x + k) % cx] + b_ref[f, (x - k) % cx]
                sides = sides + pad_ref[x, 8 + k : 8 + k + ny, :]
                sides = sides + pad_ref[x, 8 - k : 8 - k + ny, :]
                total = total + SIDE[k] * sides
            out_ref[f, x] = total
        return 0

    lax.fori_loop(0, fields, field, 0)

    shape = (owned * ny, reach * ny)
    to = lax.broadcasted_iota(jnp.int32, shape, 0)
    of = lax.broadcasted_iota(jnp.int32, shape, 1)
    planes, row_steps = of // ny - to // ny, of % ny - to % ny
    pairs = jnp.zeros(shape, jnp.float32)
    for k in range(1, REACH + 1):
        hit = ((planes == k) & (row_steps == 0)) | ((planes == 0) & (row_steps == k))
        pairs = jnp.where(hit, 2.0 * SIDE[k], pairs)
    pairs_ref[...] = wide_left(pairs)

    shape = (2 * rows, 8 * rows)
    row_at, row_field = layer_of(lax.broadcasted_iota(jnp.int32, shape, 0), (-REACH, nz), rows)
    starts = (0, nz - REACH, -REACH, -2 * REACH, nz, nz + REACH)
    col_at, col_field = layer_of(lax.broadcasted_iota(jnp.int32, shape, 1), starts, rows)
    beyond_ref[...] = wide_left(links(row_at, col_at, row_field, col_field))
    shape = (4 * rows, 4 * rows)
    row = lax.broadcasted_iota(jnp.int32, shape, 0)
    col = lax.broadcasted_iota(jnp.int32, shape, 1)
    row_at, row_field = layer_of(row % (2 * rows), (0, nz - REACH), rows)
    col_at, col_field = layer_of(col % (2 * rows), (-REACH, nz), rows)
    same = row // (2 * rows) == col // (2 * rows)
    back_ref[...] = wide_left(jnp.where(same, links(row_at, col_at, row_field, col_field), 0.0))
    shape = (2 * rows, nz)
    layer, owner = layer_of(lax.broadcasted_iota(jnp.int32, shape, 0), (-REACH, nz), rows)
    cell = lax.broadcasted_iota(jnp.int32, shape, 1)
    for f in range(fields):
        fix_ref[f] = wide_right(links(layer, cell, owner, f))
    lane = lax.broadcasted_iota(jnp.int32, (2 * rows, LANES), 1)
    weight = jnp.where(lane < owned * ny, jnp.where(lane % ny >= ny // 2, 3.0, 1.0), 0.0)
    edges = jnp.concatenate([zdown_ref[0:rows, 0:LANES], zup_ref[0:rows, 0:LANES]], axis=0)
    edges_ref[...] = around(edges, ny) * weight
    for s in range(srcs):
        re = im = jnp.zeros((ny, nz), jnp.float32)
        for x in range(owned):
            br, bi = b_ref[s, x], b_ref[srcs + s, x]
            re = re + (br * br - bi * bi)
            im = im + br * bi
        base_ref[s : s + 1, :] = fold(re)
        base_ref[srcs + s : srcs + s + 1, :] = fold(2.0 * im)


def fold(value):
    return jnp.sum(value, axis=0, keepdims=True)


def product(left, right):
    return left[0] * right[0] - left[1] * right[1], left[0] * right[1] + left[1] * right[0]


def main_kernel(
    owned,
    b_ref,
    pot_ref,
    inner_ref,
    below_ref,
    above_ref,
    zup_ref,
    zdown_ref,
    zbelow_ref,
    zabove_ref,
    both_ref,
    half_ref,
    beyond_ref,
    back_ref,
    fix_ref,
    pairs_ref,
    edges_ref,
    base_ref,
    h_ref,
    out_ref,
    pad_ref,
    edge_ref,
    acc_ref,
    step_ref,
    far_ref,
    pull_ref,
):
    fields, reach, ny, nz = inner_ref.shape
    cx = b_ref.shape[1]
    srcs = fields // 2
    rows = fields * REACH
    after = rows + rows // 2

    outer = jnp.concatenate([zbelow_ref[0:rows], zabove_ref[0:rows]], axis=0)
    high = outer.astype(jnp.bfloat16).astype(jnp.float32)
    wide = jnp.concatenate([high, outer - high, high], axis=0).T[0 : reach * ny].astype(jnp.bfloat16)
    near = outer[:, 0:LANES]

    def second(ref):
        return [ref[rows:after, 0:LANES], ref[rows:after, LANES : 2 * LANES]]

    stack = jnp.concatenate(
        [zdown_ref[0:rows, 0:LANES], zup_ref[0:rows, 0:LANES], near[0:rows]]
        + second(zbelow_ref)
        + [near[rows : 2 * rows]]
        + second(zabove_ref)
        + [near],
        axis=0,
    )
    image = mul(beyond_ref[...], wide_right(stack))
    for f in range(fields):
        h_ref[f] = mul(wide, fix_ref[f]).reshape(reach, ny, nz)
    zero = jnp.zeros((reach, 16, nz), jnp.float32)
    pad_ref[0] = zero
    pad_ref[1] = zero
    edge_ref[...] = jnp.zeros(edge_ref.shape, jnp.float32)
    def border(f):
        for x in range(reach):
            at = (f * reach + x) * REACH
            pad_ref[0, x, 8 - REACH : 8, :] = below_ref[at : at + REACH, :]
            pad_ref[1, x, 8 : 8 + REACH, :] = above_ref[at : at + REACH, :]
        for x in range(reach):
            low = SIDE[1] * pad_ref[0, x, 7:15, :]
            high = SIDE[1] * pad_ref[1, x, 1:9, :]
            for k in range(2, REACH + 1):
                low = low + SIDE[k] * pad_ref[0, x, 8 - k : 16 - k, :]
                high = high + SIDE[k] * pad_ref[1, x, k : 8 + k, :]
            total = h_ref[f, x] + inner_ref[f, x]
            middle = [total[8 : ny - 8]] if ny > 16 else []
            first, last = total[0:8] + low, total[ny - 8 : ny] + high
            h_ref[f, x] = jnp.concatenate([first] + middle + [last], axis=0)
            if x < owned:
                u = jnp.concatenate([first + low] + middle + [last + 3.0 * high], axis=0)
                spot = pl.ds(x * ny, ny)
                edge_ref[spot, :] = gather_edges(edge_ref[spot, :], f, u)

    cuts = [fields * n // 4 for n in range(5)]
    for f in range(cuts[0], cuts[1]):
        border(f)
    local = jnp.concatenate(
        [zbelow_ref[after : after + REACH, 0:LANES]] * fields
        + [zabove_ref[after : after + REACH, 0:LANES]] * fields,
        axis=0,
    )
    image = image + local * near
    y = lax.broadcasted_iota(jnp.int32, (2 * rows, LANES), 1) % ny
    width = cx * ny
    for k in range(1, REACH + 1):
        sides = pltpu.roll(outer, ny * k, 1) + pltpu.roll(outer, width - ny * k, 1)
        sides = sides[:, 0:LANES] + jnp.where(y >= k, pltpu.roll(near, k, 1), 0.0)
        sides = sides + jnp.where(y < ny - k, pltpu.roll(near, LANES - k, 1), 0.0)
        image = image + SIDE[k] * sides
    for f in range(cuts[1], cuts[2]):
        border(f)
    reached = mul(back_ref[...], wide_right(jnp.concatenate([image, near], axis=0)))
    for f in range(cuts[2], cuts[3]):
        border(f)
    turned = around(reached[2 * rows : 4 * rows], ny)
    for f in range(cuts[3], cuts[4]):
        border(f)

    for s in range(srcs):
        values = [h_ref[f].reshape(reach * ny, nz) for f in (s, srcs + s)]
        along = mul(pairs_ref[...], jnp.concatenate([wide_right(v) for v in values], axis=1))
        for part in range(2):
            f = part * srcs + s
            own = values[part][0 : owned * ny]
            step = mul(wide_left(own), half_ref[...]) + along[:, part * nz : (part + 1) * nz]
            step_ref[f] = step.reshape(owned, ny, nz)
    for f in range(fields):
        at = f * reach * REACH
        far_ref[f] = mul(wide_left(above_ref[at : at + owned * REACH, :]), both_ref[...])

    quad_row = lax.broadcasted_iota(jnp.int32, (8, nz), 0) % REACH
    early = lax.broadcasted_iota(jnp.int32, (8, nz), 0) < REACH

    def top(ref, f, x):
        return jnp.where(early, pltpu.roll(ref[f, x, ny - 8 : ny, :], REACH, 0), ref[f, x + 1, ny - 8 : ny, :])

    def lowered(lower, upper, k):
        if k == REACH:
            return lower
        return jnp.where(quad_row >= k, pltpu.roll(upper, k, 0), pltpu.roll(lower, REACH + k, 0))

    def raised(lower, upper, k):
        if k == REACH:
            return upper
        return jnp.where(quad_row < REACH - k, pltpu.roll(lower, 8 - k, 0), pltpu.roll(upper, REACH - k, 0))

    for f in range(fields):
        for x in range(0, reach, 2):
            own = top(h_ref, f, x)
            pull = SIDE[REACH] * own
            for k in range(1, REACH):
                pull = pull + SIDE[k] * jnp.where(quad_row < k, pltpu.roll(own, REACH + k, 0), 0.0)
            at = (f * reach + x) * REACH
            pull_ref[at : at + 8, :] = pull

    for s in range(srcs):
        total = [jnp.zeros((ny, nz), jnp.float32) for _ in range(6)]
        for x in range(owned):
            local = pot_ref[x]
            b = (b_ref[s, x], b_ref[srcs + s, x])
            h = (h_ref[s, x], h_ref[srcs + s, x])
            g = [step_ref[part * srcs + s, x] + local * h[part] for part in range(2)]
            squares = (h[0] * h[0] - h[1] * h[1], h[0] * h[1])
            terms = product(b, h) + squares + product(h, g)
            total = [t + v for t, v in zip(total, terms)]
        cross = [jnp.zeros((8, nz), jnp.float32) for _ in range(2)]
        for x in range(0, owned, 2):
            at = (fields * (reach + owned) + x) * REACH
            local = above_ref[at : at + 8, :]
            left, right, first, pulls = [], [], [], []
            for part in range(2):
                f = part * srcs + s
                at = (f * reach + x) * REACH
                own = top(b_ref, f, x)
                first_layers = above_ref[at : at + 8, :]
                start = (fields * reach + f * owned + x) * REACH
                more = above_ref[start : start + 8, :]
                value = far_ref[f, x * REACH : x * REACH + 8, :] + local * first_layers
                pull = 0.0
                for k in range(1, REACH + 1):
                    sides = above_ref[at + k * REACH : at + k * REACH + 8, :]
                    sides = sides + raised(first_layers, more, k) + lowered(own, first_layers, k)
                    value = value + SIDE[k] * sides
                    pull = pull + SIDE[k] * pull_ref[at + k * REACH : at + k * REACH + 8, :]
                left.append(pull_ref[at : at + 8, :])
                right.append(value)
                first.append(first_layers)
                pulls.append(pull)
            for c, (one, two) in enumerate(zip(product(left, right), product(first, pulls))):
                cross[c] = cross[c] + (one + two)
        for i in range(2, 8):
            value = fold(total[i - 2])
            if i == 5:
                value = 2.0 * value
            if i >= 6:
                value = value + 2.0 * fold(cross[i - 6])
            acc_ref[i * srcs + s : i * srcs + s + 1, :] = value

    acc_ref[0 : 2 * srcs, :] = base_ref[...]
    gathered = edge_ref[...].T
    part = rows // 2
    both = [0.0, 0.0]
    for side in range(2):
        at = (1 - side) * REACH + REACH
        u = jnp.concatenate(
            [gathered[4 * REACH * f + at : 4 * REACH * f + at + REACH] for f in range(fields)], axis=0
        )
        base = side * rows
        for left, right in ((u, reached), (edges_ref[base : base + rows], turned)):
            terms = product(
                (left[0:part], left[part:rows]), (right[base : base + part], right[base + part : base + rows])
            )
            both = [t + v for t, v in zip(both, terms)]
    for c in range(2):
        for s in range(srcs):
            at = (6 + c) * srcs + s
            acc_ref[at : at + 1, :] = acc_ref[at : at + 1, :] + fold(both[c][s * REACH : (s + 1) * REACH])

    column = jnp.sum(acc_ref[...], axis=1, keepdims=True)
    row = lax.broadcasted_iota(jnp.int32, acc_ref.shape, 0)
    lane = lax.broadcasted_iota(jnp.int32, acc_ref.shape, 1)
    out_ref[...] = jnp.broadcast_to(fold(jnp.where(row == lane, column, 0.0)), out_ref.shape)


def complex_mul(left, right):
    return (left[0] * right[0] - left[1] * right[1], left[0] * right[1] + left[1] * right[0])


def complex_div(left, right):
    norm_sq = right[0] * right[0] + right[1] * right[1]
    return (
        (left[0] * right[0] + left[1] * right[1]) / norm_sq,
        (left[1] * right[0] - left[0] * right[1]) / norm_sq,
    )


def output_kernel(tot_ref, table_ref, b_ref, h_ref, out_hbm, coef_ref, buf_ref, sems):
    fields, cx, ny, nz = b_ref.shape
    srcs = fields // 2
    planes = buf_ref.shape[3]
    shape = (srcs, LANES)
    wide = jnp.broadcast_to(fold(tot_ref[...]), (8 * srcs, LANES))
    row = lax.broadcasted_iota(jnp.int32, wide.shape, 0)
    lane = lax.broadcasted_iota(jnp.int32, wide.shape, 1)
    wide = jnp.broadcast_to(jnp.sum(jnp.where(row == lane, wide, 0.0), axis=1, keepdims=True), wide.shape)
    nu = [
        (wide[2 * k * srcs : (2 * k + 1) * srcs], wide[(2 * k + 1) * srcs : (2 * k + 2) * srcs])
        for k in range(4)
    ]
    zeta = (
        jnp.broadcast_to(table_ref[0:1, :], shape),
        jnp.broadcast_to(table_ref[1:2, :], shape),
    )
    scaled = complex_mul(zeta, nu[0])
    alpha_first = complex_div(nu[0], (scaled[0] - nu[1][0], scaled[1] - nu[1][1]))
    mean = complex_div(nu[1], nu[0])
    t = complex_mul(mean, nu[1])
    spread2 = (nu[2][0] - t[0], nu[2][1] - t[1])
    t = complex_mul(mean, (nu[2][0] + spread2[0], nu[2][1] + spread2[1]))
    spread3 = (nu[3][0] - t[0], nu[3][1] - t[1])
    square = complex_mul(alpha_first, alpha_first)
    rho_next = complex_mul(square, spread2)
    beta = complex_div(rho_next, nu[0])
    first_part = complex_mul(zeta, rho_next)
    second = complex_mul(square, spread3)
    third = complex_div(complex_mul(beta, rho_next), alpha_first)
    alpha_next = complex_div(
        rho_next, (first_part[0] - second[0] - third[0], first_part[1] - second[1] - third[1])
    )
    t = complex_mul(alpha_first, mean)
    carried = complex_mul(alpha_next, (beta[0] - t[0], beta[1] - t[1]))
    on_source = (alpha_first[0] + carried[0], alpha_first[1] + carried[1])
    on_image = complex_mul(alpha_next, alpha_first)
    for k in range(MOMS):
        weight = (
            jnp.broadcast_to(table_ref[2 + 2 * k : 3 + 2 * k, :], shape),
            jnp.broadcast_to(table_ref[3 + 2 * k : 4 + 2 * k, :], shape),
        )
        for n, value in enumerate((on_source, on_image)):
            both = complex_mul(weight, value)
            for c in range(2):
                column = jnp.sum(both[c], axis=1, keepdims=True)
                coef_ref[4 * k + 2 * n + c, 0:srcs, :] = jnp.broadcast_to(column, shape)

    copies = []
    for s in range(srcs):
        for k in range(MOMS):
            c = [
                jnp.broadcast_to(coef_ref[4 * k + n, s : s + 1, :], (ny, nz)) for n in range(4)
            ]
            for x in range(planes):
                br, bi = b_ref[s, x], b_ref[srcs + s, x]
                hr, hi = h_ref[s, x], h_ref[srcs + s, x]
                buf_ref[s, k, 0, x] = c[0] * br - c[1] * bi + (c[2] * hr - c[3] * hi)
                buf_ref[s, k, 1, x] = c[0] * bi + c[1] * br + (c[2] * hi + c[3] * hr)
            copy = pltpu.make_async_copy(buf_ref.at[s, k], out_hbm.at[k, :, s], sems.at[s, k])
            copy.start()
            copies.append(copy)
    for copy in copies:
        copy.wait()


def ring(count, step):
    return [(i, (i + step) % count) for i in range(count)]


ANY = pl.BlockSpec(memory_space=pl.ANY)
HBM = pl.BlockSpec(memory_space=pltpu.HBM)
VMEM = pl.BlockSpec(memory_space=pltpu.VMEM)
SMEM = pl.BlockSpec(memory_space=pltpu.SMEM)


def shaped(*dims):
    return jax.ShapeDtypeStruct(dims, jnp.float32)


def small(mib):
    return pltpu.CompilerParams(vmem_limit_bytes=mib << 20)


def cost(flops, nbytes):
    return pl.CostEstimate(flops=flops, bytes_accessed=nbytes, transcendentals=0)


def per_device(source_real, source_imag, potential, center, radius):
    srcs, cx, ny, nz = source_real.shape
    fields = 2 * srcs
    py, pz, quads = lax.axis_size("py"), lax.axis_size("pz"), lax.axis_size("quad")
    owned = cx // quads
    reach = min(cx, owned + REACH)
    cells = reach * ny * nz
    rows = fields * REACH

    source_real, source_imag, potential = (
        pltpu.with_memory_space_constraint(a, pltpu.HBM)
        for a in (source_real, source_imag, potential)
    )
    part = shaped(fields, reach, ny, nz)
    flat = shaped(rows + rows // 2 + 2 * REACH, cx * ny)
    b, pot, up, down, zup, zdown = pl.pallas_call(
        functools.partial(load_kernel, owned),
        out_shape=(
            shaped(fields, cx, ny, nz),
            shaped(cx, ny, nz),
            shaped(fields * reach * REACH, nz),
            shaped((fields * (reach + owned) + owned) * REACH, nz),
            flat,
            flat,
        ),
        in_specs=[HBM] * 3,
        out_specs=(VMEM,) * 6,
        scratch_shapes=[
            pltpu.VMEM((fields, 2 * nz, nz), jnp.bfloat16),
            pltpu.SemaphoreType.DMA((fields + 1, quads)),
        ],
        compiler_params=small(8),
        name="load",
    )(source_real, source_imag, potential)
    above = lax.ppermute(down, "py", ring(py, -1))
    below = lax.ppermute(up, "py", ring(py, 1))
    zabove = lax.ppermute(zdown, "pz", ring(pz, -1))
    zbelow = lax.ppermute(zup, "pz", ring(pz, 1))

    half = lambda *dims: jax.ShapeDtypeStruct(dims, jnp.bfloat16)
    inner, *weights = pl.pallas_call(
        functools.partial(inner_kernel, owned),
        out_shape=(
            part,
            half(3 * nz, nz),
            half(3 * nz, nz),
            half(2 * rows, 24 * rows),
            half(4 * rows, 12 * rows),
            half(fields, 6 * rows, nz),
            half(owned * ny, 3 * reach * ny),
            shaped(2 * rows, LANES),
            shaped(2 * srcs, nz),
        ),
        in_specs=[VMEM] * 4,
        out_specs=(VMEM,) * 9,
        scratch_shapes=[pltpu.VMEM((reach, ny + 16, nz), jnp.float32)],
        compiler_params=small(12),
        cost_estimate=cost(fields * cells * 60, fields * cells * 12),
        name="inner",
    )(b, pot, zup, zdown)

    devices = quads * py * pz
    image, partial = pl.pallas_call(
        functools.partial(main_kernel, owned),
        out_shape=(part, shaped(devices, LANES)),
        in_specs=[VMEM] * 17,
        out_specs=(VMEM,) * 2,
        scratch_shapes=[
            pltpu.VMEM((2, reach, 16, nz), jnp.float32),
            pltpu.VMEM((LANES, nz), jnp.float32),
            pltpu.VMEM((8 * srcs, nz), jnp.float32),
            pltpu.VMEM((fields, owned, ny, nz), jnp.float32),
            pltpu.VMEM((fields, owned * REACH, nz), jnp.float32),
            pltpu.VMEM((fields * reach * REACH, nz), jnp.float32),
        ],
        compiler_params=small(12),
        name="main",
    )(b, pot, inner, below, above, zup, zdown, zbelow, zabove, *weights)

    total = lax.all_to_all(partial, ("quad", "py", "pz"), 0, 0)

    table = jnp.asarray(phase_table())
    row = lax.broadcasted_iota(jnp.int32, table.shape, 0)
    table = radius * table + jnp.where(row == 0, center - MIDDLE, 0.0)
    return pl.pallas_call(
        output_kernel,
        out_shape=shaped(MOMS, 2, srcs, owned, ny, nz),
        in_specs=[VMEM] * 4,
        out_specs=HBM,
        scratch_shapes=[
            pltpu.VMEM((4 * MOMS, 8, LANES), jnp.float32),
            pltpu.VMEM((srcs, MOMS, 2, owned, ny, nz), jnp.float32),
            pltpu.SemaphoreType.DMA((srcs, MOMS)),
        ],
        compiler_params=small(12),
        name="output",
    )(total, table, b, image)


def solution(mesh):
    in_specs = (P(None, None, "py", "pz"), P(None, None, "py", "pz"), P(None, "py", "pz"), P(), P())
    out_specs = P(None, None, None, "quad", "py", "pz")
    return jax.shard_map(
        per_device, mesh=mesh, in_specs=in_specs, out_specs=out_specs, check_vma=False
    )
```

```python
import functools
import math

import jax
import jax.numpy as jnp
import numpy as np
from jax import lax
from jax.experimental import pallas as pl
from jax.experimental.pallas import tpu as pltpu
from jax.sharding import PartitionSpec as P


QPTS = 8
MOMS = 4
REACH = 4
LANES = 128

stencil_weights = (-205.0 / 72.0, 8.0 / 5.0, -1.0 / 5.0, 8.0 / 315.0, -1.0 / 560.0)
DIAG = -1.5 * stencil_weights[0]
MIDDLE = 5.25
SIDE = tuple(-0.5 * w for w in stencil_weights)


def band(shape, offset, signs, scale=1.0):
    step = offset + lax.broadcasted_iota(jnp.int32, shape, 0) - lax.broadcasted_iota(jnp.int32, shape, 1)
    out = jnp.zeros(shape, jnp.float32)
    for k in range(1, REACH + 1):
        for sign in signs:
            out = jnp.where(step == sign * k, scale * SIDE[k], out)
    return out


def split(value):
    high = value.astype(jnp.bfloat16)
    return high, (value - high.astype(jnp.float32)).astype(jnp.bfloat16)


def wide_left(value):
    high, low = split(value)
    return jnp.concatenate([high, low, high], axis=1)


def wide_right(value):
    high, low = split(value)
    return jnp.concatenate([high, high, low], axis=0)


def mul(left, right):
    return lax.dot_general(left, right, (((1,), (0,)), ((), ())), preferred_element_type=jnp.float32)


def gather_edges(gathered, f, value):
    lane = lax.broadcasted_iota(jnp.int32, value.shape, 1)
    moved = pltpu.roll(value, 4 * REACH * f + 2 * REACH, 1)
    return jnp.where(lane // (4 * REACH) == f, moved, gathered)


def load_kernel(
    owned, re_hbm, im_hbm, pot_hbm, b_ref, pot_ref, up_ref, down_ref, far_ref, zup_ref, zdown_ref, pick_ref, sems
):
    fields, cx, ny, nz = b_ref.shape
    srcs = fields // 2
    parts = cx // owned
    reach = up_ref.shape[0] // (fields * REACH)
    first = lax.axis_index("quad")
    copies = []
    for f in range(fields + 1):
        source = pot_hbm if f == fields else (re_hbm, im_hbm)[f // srcs].at[f % srcs]
        target = pot_ref if f == fields else b_ref.at[f]
        group = []
        for j in range(parts):
            at = pl.multiple_of(lax.rem(first + j, parts) * owned, owned)
            group.append(
                pltpu.make_async_copy(
                    source.at[pl.ds(at, owned)], target.at[pl.ds(j * owned, owned)], sems.at[f, j]
                )
            )
        copies.append(group)
    for group in copies:
        for copy in group:
            copy.start()
    shape = (2 * nz, nz)
    layer = lax.broadcasted_iota(jnp.int32, shape, 0) % nz
    lane = lax.broadcasted_iota(jnp.int32, shape, 1)
    spot = lax.rem(layer + 2 * REACH, nz)
    for f in range(fields):
        chosen = (spot < 4 * REACH) & (lane == spot + 4 * REACH * f)
        pick_ref[f] = jnp.where(chosen, 1.0, 0.0).astype(jnp.bfloat16)
    for f in range(fields):
        for copy in copies[f]:
            copy.wait()
        for x in range(reach):
            at = (f * reach + x) * REACH
            up_ref[at : at + REACH, :] = b_ref[f, x, ny - REACH : ny, :]
            down_ref[at : at + REACH, :] = b_ref[f, x, 0:REACH, :]
        for x in range(owned):
            at = (f * owned + x) * REACH
            far_ref[at : at + REACH, :] = b_ref[f, x, REACH : 2 * REACH, :]
    for copy in copies[fields]:
        copy.wait()
    pot_ref[...] = pot_ref[...] + (DIAG - MIDDLE)
    for x in range(owned):
        at = (fields * owned + x) * REACH
        far_ref[at : at + REACH, :] = pot_ref[x, 0:REACH, :]
    turned = pltpu.roll(pot_ref[...].reshape(cx * ny, nz), 2 * REACH, 1).T
    rows = fields * REACH
    after = rows + rows // 2
    zup_ref[after : after + REACH, :] = turned[REACH : 2 * REACH]
    zup_ref[after + REACH : after + 2 * REACH, :] = turned[0:REACH]
    zdown_ref[after : after + 2 * REACH, :] = turned[2 * REACH : 4 * REACH]
    pieces = [split(b_ref[f].reshape(cx * ny, nz)) for f in range(fields)]
    wide = jnp.concatenate([half for pair in pieces for half in pair], axis=1)
    turned = mul(wide, pick_ref[...].reshape(2 * fields * nz, nz)).T
    for f in range(fields):
        at = 4 * REACH * f
        low, high = f * REACH, (f + 1) * REACH
        zup_ref[low:high, :] = turned[at + REACH : at + 2 * REACH]
        zdown_ref[low:high, :] = turned[at + 2 * REACH : at + 3 * REACH]
        side, spot = f // srcs * LANES, rows + f % srcs * REACH
        lanes = slice(side, side + LANES)
        zup_ref[spot : spot + REACH, lanes] = turned[at : at + REACH, 0:LANES]
        zdown_ref[spot : spot + REACH, lanes] = turned[at + 3 * REACH : at + 4 * REACH, 0:LANES]


def phase_table():
    lane = np.arange(LANES)
    angle = 2.0 * math.pi * (lane % QPTS + 0.5) / QPTS
    rows = [np.cos(angle), np.sin(angle)]
    for k in range(1, MOMS + 1):
        rows.append(np.where(lane < QPTS, np.cos(k * angle), 0.0) / QPTS)
        rows.append(np.where(lane < QPTS, np.sin(k * angle), 0.0) / QPTS)
    rows += [np.zeros(LANES)] * (-len(rows) % 8)
    return np.stack(rows).astype(np.float32)


def links(row_at, col_at, row_field, col_field):
    step = jnp.abs(row_at - col_at)
    out = jnp.zeros(step.shape, jnp.float32)
    for k in range(1, REACH + 1):
        out = jnp.where((step == k) & (row_field == col_field), SIDE[k], out)
    return out


def layer_of(index, starts, rows):
    layer = jnp.full(index.shape, 1 << 20, jnp.int32)
    for n, start in enumerate(starts):
        layer = jnp.where(index // rows == n, start + index % REACH, layer)
    return layer, index % rows // REACH


def around(value, ny):
    y = lax.broadcasted_iota(jnp.int32, value.shape, 1) % ny
    width = value.shape[1]
    out = jnp.zeros(value.shape, jnp.float32)
    for k in range(1, REACH + 1):
        sides = jnp.where(y >= ny - k, pltpu.roll(value, ny - k, 1), 0.0)
        sides = sides + jnp.where(y < k, pltpu.roll(value, width + k - ny, 1), 0.0)
        out = out + SIDE[k] * sides
    return out


def inner_kernel(
    owned,
    b_ref,
    pot_ref,
    zup_ref,
    zdown_ref,
    out_ref,
    both_ref,
    half_ref,
    beyond_ref,
    back_ref,
    fix_ref,
    pairs_ref,
    edges_ref,
    base_ref,
    pad_ref,
):
    fields, cx, ny, nz = b_ref.shape
    srcs = fields // 2
    reach = out_ref.shape[1]
    rows = fields * REACH
    both_ref[...] = wide_right(band((nz, nz), 0, (1, -1)))
    half_ref[...] = wide_right(band((nz, nz), 0, (1,), 2.0))
    for f in range(fields):
        own = b_ref[f, 0:reach].reshape(reach * ny, nz)
        out_ref[f] = mul(wide_left(own), both_ref[...]).reshape(reach, ny, nz)
    zero = jnp.zeros((reach, 8, nz), jnp.float32)
    pad_ref[:, 0:8, :] = zero
    pad_ref[:, 8 + ny : 16 + ny, :] = zero

    def field(f, _):
        pad_ref[:, 8 : 8 + ny, :] = b_ref[f, 0:reach]
        for x in range(reach):
            total = out_ref[f, x] + pot_ref[x] * b_ref[f, x]
            for k in range(1, REACH + 1):
                sides = b_ref[f, (x + k) % cx] + b_ref[f, (x - k) % cx]
                sides = sides + pad_ref[x, 8 + k : 8 + k + ny, :]
                sides = sides + pad_ref[x, 8 - k : 8 - k + ny, :]
                total = total + SIDE[k] * sides
            out_ref[f, x] = total
        return 0

    lax.fori_loop(0, fields, field, 0)

    shape = (owned * ny, reach * ny)
    to = lax.broadcasted_iota(jnp.int32, shape, 0)
    of = lax.broadcasted_iota(jnp.int32, shape, 1)
    planes, row_steps = of // ny - to // ny, of % ny - to % ny
    pairs = jnp.zeros(shape, jnp.float32)
    for k in range(1, REACH + 1):
        hit = ((planes == k) & (row_steps == 0)) | ((planes == 0) & (row_steps == k))
        pairs = jnp.where(hit, 2.0 * SIDE[k], pairs)
    pairs_ref[...] = wide_left(pairs)

    shape = (2 * rows, 8 * rows)
    row_at, row_field = layer_of(lax.broadcasted_iota(jnp.int32, shape, 0), (-REACH, nz), rows)
    starts = (0, nz - REACH, -REACH, -2 * REACH, nz, nz + REACH)
    col_at, col_field = layer_of(lax.broadcasted_iota(jnp.int32, shape, 1), starts, rows)
    beyond_ref[...] = wide_left(links(row_at, col_at, row_field, col_field))
    shape = (4 * rows, 4 * rows)
    row = lax.broadcasted_iota(jnp.int32, shape, 0)
    col = lax.broadcasted_iota(jnp.int32, shape, 1)
    row_at, row_field = layer_of(row % (2 * rows), (0, nz - REACH), rows)
    col_at, col_field = layer_of(col % (2 * rows), (-REACH, nz), rows)
    same = row // (2 * rows) == col // (2 * rows)
    back_ref[...] = wide_left(jnp.where(same, links(row_at, col_at, row_field, col_field), 0.0))
    shape = (2 * rows, nz)
    layer, owner = layer_of(lax.broadcasted_iota(jnp.int32, shape, 0), (-REACH, nz), rows)
    cell = lax.broadcasted_iota(jnp.int32, shape, 1)
    for f in range(fields):
        fix_ref[f] = wide_right(links(layer, cell, owner, f))
    lane = lax.broadcasted_iota(jnp.int32, (2 * rows, LANES), 1)
    weight = jnp.where(lane < owned * ny, jnp.where(lane % ny >= ny // 2, 3.0, 1.0), 0.0)
    edges = jnp.concatenate([zdown_ref[0:rows, 0:LANES], zup_ref[0:rows, 0:LANES]], axis=0)
    edges_ref[...] = around(edges, ny) * weight
    for s in range(srcs):
        re = im = jnp.zeros((ny, nz), jnp.float32)
        for x in range(owned):
            br, bi = b_ref[s, x], b_ref[srcs + s, x]
            re = re + (br * br - bi * bi)
            im = im + br * bi
        base_ref[s : s + 1, :] = fold(re)
        base_ref[srcs + s : srcs + s + 1, :] = fold(2.0 * im)


def fold(value):
    return jnp.sum(value, axis=0, keepdims=True)


def product(left, right):
    return left[0] * right[0] - left[1] * right[1], left[0] * right[1] + left[1] * right[0]


def main_kernel(
    owned,
    b_ref,
    pot_ref,
    inner_ref,
    below_ref,
    above_ref,
    zup_ref,
    zdown_ref,
    zbelow_ref,
    zabove_ref,
    half_ref,
    beyond_ref,
    back_ref,
    fix_ref,
    pairs_ref,
    edges_ref,
    base_ref,
    h_ref,
    acc_ref,
    pad_ref,
    edge_ref,
    step_ref,
):
    fields, reach, ny, nz = inner_ref.shape
    cx = b_ref.shape[1]
    srcs = fields // 2
    rows = fields * REACH
    after = rows + rows // 2

    outer = jnp.concatenate([zbelow_ref[0:rows], zabove_ref[0:rows]], axis=0)
    high = outer.astype(jnp.bfloat16).astype(jnp.float32)
    wide = jnp.concatenate([high, outer - high, high], axis=0).T[0 : reach * ny].astype(jnp.bfloat16)
    near = outer[:, 0:LANES]

    def second(ref):
        return [ref[rows:after, 0:LANES], ref[rows:after, LANES : 2 * LANES]]

    stack = jnp.concatenate(
        [zdown_ref[0:rows, 0:LANES], zup_ref[0:rows, 0:LANES], near[0:rows]]
        + second(zbelow_ref)
        + [near[rows : 2 * rows]]
        + second(zabove_ref)
        + [near],
        axis=0,
    )
    image = mul(beyond_ref[...], wide_right(stack))
    for f in range(fields):
        h_ref[f] = mul(wide, fix_ref[f]).reshape(reach, ny, nz)
    zero = jnp.zeros((reach, 16, nz), jnp.float32)
    pad_ref[0] = zero
    pad_ref[1] = zero
    edge_ref[...] = jnp.zeros(edge_ref.shape, jnp.float32)

    def border(f):
        for x in range(reach):
            at = (f * reach + x) * REACH
            pad_ref[0, x, 8 - REACH : 8, :] = below_ref[at : at + REACH, :]
            pad_ref[1, x, 8 : 8 + REACH, :] = above_ref[at : at + REACH, :]
        for x in range(reach):
            low = SIDE[1] * pad_ref[0, x, 7:15, :]
            high = SIDE[1] * pad_ref[1, x, 1:9, :]
            for k in range(2, REACH + 1):
                low = low + SIDE[k] * pad_ref[0, x, 8 - k : 16 - k, :]
                high = high + SIDE[k] * pad_ref[1, x, k : 8 + k, :]
            total = h_ref[f, x] + inner_ref[f, x]
            middle = [total[8 : ny - 8]] if ny > 16 else []
            first, last = total[0:8] + low, total[ny - 8 : ny] + high
            h_ref[f, x] = jnp.concatenate([first] + middle + [last], axis=0)
            if x < owned:
                u = jnp.concatenate([first + low] + middle + [last + 3.0 * high], axis=0)
                spot = pl.ds(x * ny, ny)
                edge_ref[spot, :] = gather_edges(edge_ref[spot, :], f, u)

    cuts = [fields * n // 4 for n in range(5)]
    for f in range(cuts[0], cuts[1]):
        border(f)
    local = jnp.concatenate(
        [zbelow_ref[after : after + REACH, 0:LANES]] * fields
        + [zabove_ref[after : after + REACH, 0:LANES]] * fields,
        axis=0,
    )
    image = image + local * near
    y = lax.broadcasted_iota(jnp.int32, (2 * rows, LANES), 1) % ny
    width = cx * ny
    for k in range(1, REACH + 1):
        sides = pltpu.roll(outer, ny * k, 1) + pltpu.roll(outer, width - ny * k, 1)
        sides = sides[:, 0:LANES] + jnp.where(y >= k, pltpu.roll(near, k, 1), 0.0)
        sides = sides + jnp.where(y < ny - k, pltpu.roll(near, LANES - k, 1), 0.0)
        image = image + SIDE[k] * sides
    for f in range(cuts[1], cuts[2]):
        border(f)
    reached = mul(back_ref[...], wide_right(jnp.concatenate([image, near], axis=0)))
    for f in range(cuts[2], cuts[3]):
        border(f)
    turned = around(reached[2 * rows : 4 * rows], ny)
    for f in range(cuts[3], cuts[4]):
        border(f)

    for s in range(srcs):
        values = [h_ref[f].reshape(reach * ny, nz) for f in (s, srcs + s)]
        along = mul(pairs_ref[...], jnp.concatenate([wide_right(v) for v in values], axis=1))
        for part in range(2):
            f = part * srcs + s
            own = values[part][0 : owned * ny]
            step = mul(wide_left(own), half_ref[...]) + along[:, part * nz : (part + 1) * nz]
            step_ref[f] = step.reshape(owned, ny, nz)
    for s in range(srcs):
        total = [jnp.zeros((ny, nz), jnp.float32) for _ in range(6)]
        for x in range(owned):
            local = pot_ref[x]
            b = (b_ref[s, x], b_ref[srcs + s, x])
            h = (h_ref[s, x], h_ref[srcs + s, x])
            g = [step_ref[part * srcs + s, x] + local * h[part] for part in range(2)]
            squares = (h[0] * h[0] - h[1] * h[1], h[0] * h[1])
            terms = product(b, h) + squares + product(h, g)
            total = [t + v for t, v in zip(total, terms)]
        for i in range(2, 8):
            value = fold(total[i - 2])
            if i == 5:
                value = 2.0 * value
            acc_ref[i * srcs + s : i * srcs + s + 1, :] = value

    acc_ref[0 : 2 * srcs, :] = base_ref[...]
    gathered = edge_ref[...].T
    part = rows // 2
    both = [0.0, 0.0]
    for side in range(2):
        at = (1 - side) * REACH + REACH
        u = jnp.concatenate(
            [gathered[4 * REACH * f + at : 4 * REACH * f + at + REACH] for f in range(fields)], axis=0
        )
        base = side * rows
        for left, right in ((u, reached), (edges_ref[base : base + rows], turned)):
            terms = product(
                (left[0:part], left[part:rows]), (right[base : base + part], right[base + part : base + rows])
            )
            both = [t + v for t, v in zip(both, terms)]
    for c in range(2):
        for s in range(srcs):
            at = (6 + c) * srcs + s
            acc_ref[at : at + 1, :] = acc_ref[at : at + 1, :] + fold(both[c][s * REACH : (s + 1) * REACH])


def tail_kernel(owned, b_ref, h_ref, above_ref, more_ref, both_ref, sums_ref, out_ref, acc_ref, far_ref, pull_ref):
    fields, reach, ny, nz = h_ref.shape
    srcs = fields // 2
    for f in range(fields):
        at = f * reach * REACH
        far_ref[f] = mul(wide_left(above_ref[at : at + owned * REACH, :]), both_ref[...])

    quad_row = lax.broadcasted_iota(jnp.int32, (8, nz), 0) % REACH
    early = lax.broadcasted_iota(jnp.int32, (8, nz), 0) < REACH

    def top(ref, f, x):
        return jnp.where(early, pltpu.roll(ref[f, x, ny - 8 : ny, :], REACH, 0), ref[f, x + 1, ny - 8 : ny, :])

    def lowered(lower, upper, k):
        if k == REACH:
            return lower
        return jnp.where(quad_row >= k, pltpu.roll(upper, k, 0), pltpu.roll(lower, REACH + k, 0))

    def raised(lower, upper, k):
        if k == REACH:
            return upper
        return jnp.where(quad_row < REACH - k, pltpu.roll(lower, 8 - k, 0), pltpu.roll(upper, REACH - k, 0))

    for f in range(fields):
        for x in range(0, reach, 2):
            own = top(h_ref, f, x)
            pull = SIDE[REACH] * own
            for k in range(1, REACH):
                pull = pull + SIDE[k] * jnp.where(quad_row < k, pltpu.roll(own, REACH + k, 0), 0.0)
            at = (f * reach + x) * REACH
            pull_ref[at : at + 8, :] = pull

    acc_ref[...] = sums_ref[...]
    for s in range(srcs):
        cross = [jnp.zeros((8, nz), jnp.float32) for _ in range(2)]
        for x in range(0, owned, 2):
            at = (fields * owned + x) * REACH
            local = more_ref[at : at + 8, :]
            left, right, first, pulls = [], [], [], []
            for part in range(2):
                f = part * srcs + s
                at = (f * reach + x) * REACH
                own = top(b_ref, f, x)
                first_layers = above_ref[at : at + 8, :]
                start = (f * owned + x) * REACH
                more = more_ref[start : start + 8, :]
                value = far_ref[f, x * REACH : x * REACH + 8, :] + local * first_layers
                pull = 0.0
                for k in range(1, REACH + 1):
                    sides = above_ref[at + k * REACH : at + k * REACH + 8, :]
                    sides = sides + raised(first_layers, more, k) + lowered(own, first_layers, k)
                    value = value + SIDE[k] * sides
                    pull = pull + SIDE[k] * pull_ref[at + k * REACH : at + k * REACH + 8, :]
                left.append(pull_ref[at : at + 8, :])
                right.append(value)
                first.append(first_layers)
                pulls.append(pull)
            for c, (one, two) in enumerate(zip(product(left, right), product(first, pulls))):
                cross[c] = cross[c] + (one + two)
        for c in range(2):
            at = (6 + c) * srcs + s
            acc_ref[at : at + 1, :] = acc_ref[at : at + 1, :] + 2.0 * fold(cross[c])

    column = jnp.sum(acc_ref[...], axis=1, keepdims=True)
    row = lax.broadcasted_iota(jnp.int32, acc_ref.shape, 0)
    lane = lax.broadcasted_iota(jnp.int32, acc_ref.shape, 1)
    out_ref[...] = jnp.broadcast_to(fold(jnp.where(row == lane, column, 0.0)), out_ref.shape)


def complex_mul(left, right):
    return (left[0] * right[0] - left[1] * right[1], left[0] * right[1] + left[1] * right[0])


def complex_div(left, right):
    norm_sq = right[0] * right[0] + right[1] * right[1]
    return (
        (left[0] * right[0] + left[1] * right[1]) / norm_sq,
        (left[1] * right[0] - left[0] * right[1]) / norm_sq,
    )


def output_kernel(tot_ref, table_ref, b_ref, h_ref, out_hbm, coef_ref, buf_ref, sems):
    fields, _, ny, nz = b_ref.shape
    srcs = fields // 2
    planes = buf_ref.shape[3]
    shape = (srcs, LANES)
    wide = jnp.broadcast_to(fold(tot_ref[...]), (8 * srcs, LANES))
    row = lax.broadcasted_iota(jnp.int32, wide.shape, 0)
    lane = lax.broadcasted_iota(jnp.int32, wide.shape, 1)
    wide = jnp.broadcast_to(jnp.sum(jnp.where(row == lane, wide, 0.0), axis=1, keepdims=True), wide.shape)
    nu = [
        (wide[2 * k * srcs : (2 * k + 1) * srcs], wide[(2 * k + 1) * srcs : (2 * k + 2) * srcs])
        for k in range(4)
    ]
    zeta = (
        jnp.broadcast_to(table_ref[0:1, :], shape),
        jnp.broadcast_to(table_ref[1:2, :], shape),
    )
    scaled = complex_mul(zeta, nu[0])
    alpha_first = complex_div(nu[0], (scaled[0] - nu[1][0], scaled[1] - nu[1][1]))
    mean = complex_div(nu[1], nu[0])
    t = complex_mul(mean, nu[1])
    spread2 = (nu[2][0] - t[0], nu[2][1] - t[1])
    t = complex_mul(mean, (nu[2][0] + spread2[0], nu[2][1] + spread2[1]))
    spread3 = (nu[3][0] - t[0], nu[3][1] - t[1])
    square = complex_mul(alpha_first, alpha_first)
    rho_next = complex_mul(square, spread2)
    beta = complex_div(rho_next, nu[0])
    first_part = complex_mul(zeta, rho_next)
    second = complex_mul(square, spread3)
    third = complex_div(complex_mul(beta, rho_next), alpha_first)
    alpha_next = complex_div(
        rho_next, (first_part[0] - second[0] - third[0], first_part[1] - second[1] - third[1])
    )
    t = complex_mul(alpha_first, mean)
    carried = complex_mul(alpha_next, (beta[0] - t[0], beta[1] - t[1]))
    on_source = (alpha_first[0] + carried[0], alpha_first[1] + carried[1])
    on_image = complex_mul(alpha_next, alpha_first)
    for k in range(MOMS):
        weight = (
            jnp.broadcast_to(table_ref[2 + 2 * k : 3 + 2 * k, :], shape),
            jnp.broadcast_to(table_ref[3 + 2 * k : 4 + 2 * k, :], shape),
        )
        for n, value in enumerate((on_source, on_image)):
            both = complex_mul(weight, value)
            for c in range(2):
                column = jnp.sum(both[c], axis=1, keepdims=True)
                coef_ref[4 * k + 2 * n + c, 0:srcs, :] = jnp.broadcast_to(column, shape)

    copies = []
    for s in range(srcs):
        for k in range(MOMS):
            c = [
                jnp.broadcast_to(coef_ref[4 * k + n, s : s + 1, :], (ny, nz)) for n in range(4)
            ]
            for x in range(planes):
                br, bi = b_ref[s, x], b_ref[srcs + s, x]
                hr, hi = h_ref[s, x], h_ref[srcs + s, x]
                buf_ref[s, k, 0, x] = c[0] * br - c[1] * bi + (c[2] * hr - c[3] * hi)
                buf_ref[s, k, 1, x] = c[0] * bi + c[1] * br + (c[2] * hi + c[3] * hr)
            copy = pltpu.make_async_copy(buf_ref.at[s, k], out_hbm.at[k, :, s], sems.at[s, k])
            copy.start()
            copies.append(copy)
    for copy in copies:
        copy.wait()


def ring(count, step):
    return [(i, (i + step) % count) for i in range(count)]


def shift(value, axis, step):
    return lax.ppermute(value, axis, ring(lax.axis_size(axis), step))


ANY = pl.BlockSpec(memory_space=pl.ANY)
HBM = pl.BlockSpec(memory_space=pltpu.HBM)
VMEM = pl.BlockSpec(memory_space=pltpu.VMEM)
SMEM = pl.BlockSpec(memory_space=pltpu.SMEM)


def shaped(*dims):
    return jax.ShapeDtypeStruct(dims, jnp.float32)


def small(mib):
    return pltpu.CompilerParams(vmem_limit_bytes=mib << 20)


def cost(flops, nbytes):
    return pl.CostEstimate(flops=flops, bytes_accessed=nbytes, transcendentals=0)


def per_device(source_real, source_imag, potential, center, radius):
    srcs, cx, ny, nz = source_real.shape
    fields = 2 * srcs
    py, pz, quads = lax.axis_size("py"), lax.axis_size("pz"), lax.axis_size("quad")
    owned = cx // quads
    reach = min(cx, owned + REACH)
    cells = reach * ny * nz
    rows = fields * REACH

    source_real, source_imag, potential = (
        pltpu.with_memory_space_constraint(a, pltpu.HBM)
        for a in (source_real, source_imag, potential)
    )
    part = shaped(fields, reach, ny, nz)
    flat = shaped(rows + rows // 2 + 2 * REACH, cx * ny)
    b, pot, up, down, far, zup, zdown = pl.pallas_call(
        functools.partial(load_kernel, owned),
        out_shape=(
            shaped(fields, cx, ny, nz),
            shaped(cx, ny, nz),
            shaped(fields * reach * REACH, nz),
            shaped(fields * reach * REACH, nz),
            shaped((fields + 1) * owned * REACH, nz),
            flat,
            flat,
        ),
        in_specs=[HBM] * 3,
        out_specs=(VMEM,) * 7,
        scratch_shapes=[
            pltpu.VMEM((fields, 2 * nz, nz), jnp.bfloat16),
            pltpu.SemaphoreType.DMA((fields + 1, quads)),
        ],
        compiler_params=small(8),
        name="load",
    )(source_real, source_imag, potential)
    above = shift(down, "py", -1)
    below = shift(up, "py", 1)
    zabove = shift(zdown, "pz", -1)
    zbelow = shift(zup, "pz", 1)
    more = shift(far, "py", -1)

    half = lambda *dims: jax.ShapeDtypeStruct(dims, jnp.bfloat16)
    inner, *weights = pl.pallas_call(
        functools.partial(inner_kernel, owned),
        out_shape=(
            part,
            half(3 * nz, nz),
            half(3 * nz, nz),
            half(2 * rows, 24 * rows),
            half(4 * rows, 12 * rows),
            half(fields, 6 * rows, nz),
            half(owned * ny, 3 * reach * ny),
            shaped(2 * rows, LANES),
            shaped(2 * srcs, nz),
        ),
        in_specs=[VMEM] * 4,
        out_specs=(VMEM,) * 9,
        scratch_shapes=[pltpu.VMEM((reach, ny + 16, nz), jnp.float32)],
        compiler_params=small(12),
        cost_estimate=cost(fields * cells * 60, fields * cells * 12),
        name="inner",
    )(b, pot, zup, zdown)

    both, *weights = weights
    image, sums = pl.pallas_call(
        functools.partial(main_kernel, owned),
        out_shape=(part, shaped(8 * srcs, nz)),
        in_specs=[VMEM] * 16,
        out_specs=(VMEM,) * 2,
        scratch_shapes=[
            pltpu.VMEM((2, reach, 16, nz), jnp.float32),
            pltpu.VMEM((LANES, nz), jnp.float32),
            pltpu.VMEM((fields, owned, ny, nz), jnp.float32),
        ],
        compiler_params=small(12),
        cost_estimate=cost(fields * cells * 60, fields * cells * 12),
        name="main",
    )(b, pot, inner, below, above, zup, zdown, zbelow, zabove, *weights)

    partial = pl.pallas_call(
        functools.partial(tail_kernel, owned),
        out_shape=shaped(quads * py * pz, LANES),
        in_specs=[VMEM] * 6,
        out_specs=VMEM,
        scratch_shapes=[
            pltpu.VMEM((8 * srcs, nz), jnp.float32),
            pltpu.VMEM((fields, owned * REACH, nz), jnp.float32),
            pltpu.VMEM((fields * reach * REACH, nz), jnp.float32),
        ],
        compiler_params=small(8),
        name="tail",
    )(b, image, above, more, both, sums)

    total = lax.all_to_all(partial, ("quad", "py", "pz"), 0, 0)

    table = jnp.asarray(phase_table())
    row = lax.broadcasted_iota(jnp.int32, table.shape, 0)
    table = radius * table + jnp.where(row == 0, center - MIDDLE, 0.0)
    return pl.pallas_call(
        output_kernel,
        out_shape=shaped(MOMS, 2, srcs, owned, ny, nz),
        in_specs=[VMEM] * 4,
        out_specs=HBM,
        scratch_shapes=[
            pltpu.VMEM((4 * MOMS, 8, LANES), jnp.float32),
            pltpu.VMEM((srcs, MOMS, 2, owned, ny, nz), jnp.float32),
            pltpu.SemaphoreType.DMA((srcs, MOMS)),
        ],
        compiler_params=small(12),
        name="output",
    )(total, table, b, image)


def solution(mesh):
    in_specs = (P(None, None, "py", "pz"), P(None, None, "py", "pz"), P(None, "py", "pz"), P(), P())
    out_specs = P(None, None, None, "quad", "py", "pz")

    return jax.shard_map(
        per_device, mesh=mesh, in_specs=in_specs, out_specs=out_specs, check_vma=False
    )
```

```python
import functools
import math

import jax
import jax.numpy as jnp
import numpy as np
from jax import lax
from jax.experimental import pallas as pl
from jax.experimental.pallas import tpu as pltpu
from jax.sharding import PartitionSpec as P


QPTS = 8
MOMS = 4
REACH = 4
LANES = 128

stencil_weights = (-205.0 / 72.0, 8.0 / 5.0, -1.0 / 5.0, 8.0 / 315.0, -1.0 / 560.0)
DIAG = -1.5 * stencil_weights[0]
MIDDLE = 5.25
SIDE = tuple(-0.5 * w for w in stencil_weights)


def band(shape, offset, signs, scale=1.0):
    step = offset + lax.broadcasted_iota(jnp.int32, shape, 0) - lax.broadcasted_iota(jnp.int32, shape, 1)
    out = jnp.zeros(shape, jnp.float32)
    for k in range(1, REACH + 1):
        for sign in signs:
            out = jnp.where(step == sign * k, scale * SIDE[k], out)
    return out


def split(value):
    high = value.astype(jnp.bfloat16)
    return high, (value - high.astype(jnp.float32)).astype(jnp.bfloat16)


def wide_left(value):
    high, low = split(value)
    return jnp.concatenate([high, low, high], axis=1)


def wide_right(value):
    high, low = split(value)
    return jnp.concatenate([high, high, low], axis=0)


def mul(left, right):
    return lax.dot_general(left, right, (((1,), (0,)), ((), ())), preferred_element_type=jnp.float32)


def gather_edges(gathered, f, value):
    lane = lax.broadcasted_iota(jnp.int32, value.shape, 1)
    moved = pltpu.roll(value, 4 * REACH * f + 2 * REACH, 1)
    return jnp.where(lane // (4 * REACH) == f, moved, gathered)


def load_kernel(
    owned, re_hbm, im_hbm, pot_hbm, b_ref, pot_ref, up_ref, down_ref, far_ref, zup_ref, zdown_ref, pick_ref, sems
):
    fields, cx, ny, nz = b_ref.shape
    srcs = fields // 2
    parts = cx // owned
    reach = up_ref.shape[0] // (fields * REACH)
    first = lax.axis_index("quad")
    copies = []
    for n, (source, target) in enumerate(
        ((pot_hbm, pot_ref), (re_hbm, b_ref.at[pl.ds(0, srcs)]), (im_hbm, b_ref.at[pl.ds(srcs, srcs)]))
    ):
        group = []
        for j in range(parts):
            at = pl.multiple_of(lax.rem(first + j, parts) * owned, owned)
            spot = pl.ds(j * owned, owned)
            if n == 0:
                ends = source.at[pl.ds(at, owned)], target.at[spot]
            else:
                ends = source.at[:, pl.ds(at, owned)], target.at[:, spot]
            group.append(pltpu.make_async_copy(*ends, sems.at[n, j]))
        copies.append(group)
    for group in copies:
        for copy in group:
            copy.start()
    shape = (2 * nz, nz)
    layer = lax.broadcasted_iota(jnp.int32, shape, 0) % nz
    lane = lax.broadcasted_iota(jnp.int32, shape, 1)
    spot = lax.rem(layer + 2 * REACH, nz)
    for f in range(fields):
        chosen = (spot < 4 * REACH) & (lane == spot + 4 * REACH * f)
        pick_ref[f] = jnp.where(chosen, 1.0, 0.0).astype(jnp.bfloat16)
    for f in range(fields):
        if f % srcs == 0:
            for copy in copies[1 + f // srcs]:
                copy.wait()
        for x in range(reach):
            at = (f * reach + x) * REACH
            up_ref[at : at + REACH, :] = b_ref[f, x, ny - REACH : ny, :]
            down_ref[at : at + REACH, :] = b_ref[f, x, 0:REACH, :]
        for x in range(owned):
            at = (f * owned + x) * REACH
            far_ref[at : at + REACH, :] = b_ref[f, x, REACH : 2 * REACH, :]
    for copy in copies[0]:
        copy.wait()
    pot_ref[...] = pot_ref[...] + (DIAG - MIDDLE)
    for x in range(owned):
        at = (fields * owned + x) * REACH
        far_ref[at : at + REACH, :] = pot_ref[x, 0:REACH, :]
    turned = pltpu.roll(pot_ref[...].reshape(cx * ny, nz), 2 * REACH, 1).T
    rows = fields * REACH
    after = rows + rows // 2
    zup_ref[after : after + REACH, :] = turned[REACH : 2 * REACH]
    zup_ref[after + REACH : after + 2 * REACH, :] = turned[0:REACH]
    zdown_ref[after : after + 2 * REACH, :] = turned[2 * REACH : 4 * REACH]
    pieces = [split(b_ref[f].reshape(cx * ny, nz)) for f in range(fields)]
    wide = jnp.concatenate([half for pair in pieces for half in pair], axis=1)
    turned = mul(wide, pick_ref[...].reshape(2 * fields * nz, nz)).T
    for f in range(fields):
        at = 4 * REACH * f
        low, high = f * REACH, (f + 1) * REACH
        zup_ref[low:high, :] = turned[at + REACH : at + 2 * REACH]
        zdown_ref[low:high, :] = turned[at + 2 * REACH : at + 3 * REACH]
        side, spot = f // srcs * LANES, rows + f % srcs * REACH
        lanes = slice(side, side + LANES)
        zup_ref[spot : spot + REACH, lanes] = turned[at : at + REACH, 0:LANES]
        zdown_ref[spot : spot + REACH, lanes] = turned[at + 3 * REACH : at + 4 * REACH, 0:LANES]


def phase_table():
    lane = np.arange(LANES)
    angle = 2.0 * math.pi * (lane % QPTS + 0.5) / QPTS
    rows = [np.cos(angle), np.sin(angle)]
    for k in range(1, MOMS + 1):
        rows.append(np.where(lane < QPTS, np.cos(k * angle), 0.0) / QPTS)
        rows.append(np.where(lane < QPTS, np.sin(k * angle), 0.0) / QPTS)
    rows += [np.zeros(LANES)] * (-len(rows) % 8)
    return np.stack(rows).astype(np.float32)


def links(row_at, col_at, row_field, col_field):
    step = jnp.abs(row_at - col_at)
    out = jnp.zeros(step.shape, jnp.float32)
    for k in range(1, REACH + 1):
        out = jnp.where((step == k) & (row_field == col_field), SIDE[k], out)
    return out


def layer_of(index, starts, rows):
    layer = jnp.full(index.shape, 1 << 20, jnp.int32)
    for n, start in enumerate(starts):
        layer = jnp.where(index // rows == n, start + index % REACH, layer)
    return layer, index % rows // REACH


def around(value, ny):
    y = lax.broadcasted_iota(jnp.int32, value.shape, 1) % ny
    width = value.shape[1]
    out = jnp.zeros(value.shape, jnp.float32)
    for k in range(1, REACH + 1):
        sides = jnp.where(y >= ny - k, pltpu.roll(value, ny - k, 1), 0.0)
        sides = sides + jnp.where(y < k, pltpu.roll(value, width + k - ny, 1), 0.0)
        out = out + SIDE[k] * sides
    return out


def inner_kernel(
    owned,
    b_ref,
    pot_ref,
    zup_ref,
    zdown_ref,
    out_ref,
    both_ref,
    half_ref,
    beyond_ref,
    back_ref,
    fix_ref,
    pairs_ref,
    edges_ref,
    base_ref,
    pad_ref,
):
    fields, cx, ny, nz = b_ref.shape
    srcs = fields // 2
    reach = out_ref.shape[1]
    rows = fields * REACH
    both_ref[...] = wide_right(band((nz, nz), 0, (1, -1)))
    half_ref[...] = wide_right(band((nz, nz), 0, (1,), 2.0))
    for f in range(fields):
        own = b_ref[f, 0:reach].reshape(reach * ny, nz)
        out_ref[f] = mul(wide_left(own), both_ref[...]).reshape(reach, ny, nz)
    zero = jnp.zeros((reach, 8, nz), jnp.float32)
    pad_ref[:, 0:8, :] = zero
    pad_ref[:, 8 + ny : 16 + ny, :] = zero

    def field(f, _):
        pad_ref[:, 8 : 8 + ny, :] = b_ref[f, 0:reach]
        for x in range(reach):
            total = out_ref[f, x] + pot_ref[x] * b_ref[f, x]
            for k in range(1, REACH + 1):
                sides = b_ref[f, (x + k) % cx] + b_ref[f, (x - k) % cx]
                sides = sides + pad_ref[x, 8 + k : 8 + k + ny, :]
                sides = sides + pad_ref[x, 8 - k : 8 - k + ny, :]
                total = total + SIDE[k] * sides
            out_ref[f, x] = total
        return 0

    lax.fori_loop(0, fields, field, 0)

    shape = (owned * ny, reach * ny)
    to = lax.broadcasted_iota(jnp.int32, shape, 0)
    of = lax.broadcasted_iota(jnp.int32, shape, 1)
    planes, row_steps = of // ny - to // ny, of % ny - to % ny
    pairs = jnp.zeros(shape, jnp.float32)
    for k in range(1, REACH + 1):
        hit = ((planes == k) & (row_steps == 0)) | ((planes == 0) & (row_steps == k))
        pairs = jnp.where(hit, 2.0 * SIDE[k], pairs)
    pairs_ref[...] = wide_left(pairs)

    shape = (2 * rows, 8 * rows)
    row_at, row_field = layer_of(lax.broadcasted_iota(jnp.int32, shape, 0), (-REACH, nz), rows)
    starts = (0, nz - REACH, -REACH, -2 * REACH, nz, nz + REACH)
    col_at, col_field = layer_of(lax.broadcasted_iota(jnp.int32, shape, 1), starts, rows)
    beyond_ref[...] = wide_left(links(row_at, col_at, row_field, col_field))
    shape = (4 * rows, 4 * rows)
    row = lax.broadcasted_iota(jnp.int32, shape, 0)
    col = lax.broadcasted_iota(jnp.int32, shape, 1)
    row_at, row_field = layer_of(row % (2 * rows), (0, nz - REACH), rows)
    col_at, col_field = layer_of(col % (2 * rows), (-REACH, nz), rows)
    same = row // (2 * rows) == col // (2 * rows)
    back_ref[...] = wide_left(jnp.where(same, links(row_at, col_at, row_field, col_field), 0.0))
    shape = (2 * rows, nz)
    layer, owner = layer_of(lax.broadcasted_iota(jnp.int32, shape, 0), (-REACH, nz), rows)
    cell = lax.broadcasted_iota(jnp.int32, shape, 1)
    for f in range(fields):
        fix_ref[f] = wide_right(links(layer, cell, owner, f))
    lane = lax.broadcasted_iota(jnp.int32, (2 * rows, LANES), 1)
    weight = jnp.where(lane < owned * ny, jnp.where(lane % ny >= ny // 2, 3.0, 1.0), 0.0)
    edges = jnp.concatenate([zdown_ref[0:rows, 0:LANES], zup_ref[0:rows, 0:LANES]], axis=0)
    edges_ref[...] = around(edges, ny) * weight
    for s in range(srcs):
        re = im = jnp.zeros((ny, nz), jnp.float32)
        for x in range(owned):
            br, bi = b_ref[s, x], b_ref[srcs + s, x]
            re = re + (br * br - bi * bi)
            im = im + br * bi
        base_ref[s : s + 1, :] = fold(re)
        base_ref[srcs + s : srcs + s + 1, :] = fold(2.0 * im)


def fold(value):
    return jnp.sum(value, axis=0, keepdims=True)


def product(left, right):
    return left[0] * right[0] - left[1] * right[1], left[0] * right[1] + left[1] * right[0]


def main_kernel(
    owned,
    b_ref,
    pot_ref,
    inner_ref,
    below_ref,
    above_ref,
    zup_ref,
    zdown_ref,
    zbelow_ref,
    zabove_ref,
    half_ref,
    beyond_ref,
    back_ref,
    fix_ref,
    pairs_ref,
    edges_ref,
    base_ref,
    h_ref,
    acc_ref,
    pad_ref,
    edge_ref,
    step_ref,
):
    fields, reach, ny, nz = inner_ref.shape
    cx = b_ref.shape[1]
    srcs = fields // 2
    rows = fields * REACH
    after = rows + rows // 2

    outer = jnp.concatenate([zbelow_ref[0:rows], zabove_ref[0:rows]], axis=0)
    high = outer.astype(jnp.bfloat16).astype(jnp.float32)
    wide = jnp.concatenate([high, outer - high, high], axis=0).T[0 : reach * ny].astype(jnp.bfloat16)
    near = outer[:, 0:LANES]

    def second(ref):
        return [ref[rows:after, 0:LANES], ref[rows:after, LANES : 2 * LANES]]

    stack = jnp.concatenate(
        [zdown_ref[0:rows, 0:LANES], zup_ref[0:rows, 0:LANES], near[0:rows]]
        + second(zbelow_ref)
        + [near[rows : 2 * rows]]
        + second(zabove_ref)
        + [near],
        axis=0,
    )
    image = mul(beyond_ref[...], wide_right(stack))
    for f in range(fields):
        h_ref[f] = mul(wide, fix_ref[f]).reshape(reach, ny, nz)
    zero = jnp.zeros((reach, 16, nz), jnp.float32)
    pad_ref[0] = zero
    pad_ref[1] = zero
    edge_ref[...] = jnp.zeros(edge_ref.shape, jnp.float32)

    def border(f):
        for x in range(reach):
            at = (f * reach + x) * REACH
            pad_ref[0, x, 8 - REACH : 8, :] = below_ref[at : at + REACH, :]
            pad_ref[1, x, 8 : 8 + REACH, :] = above_ref[at : at + REACH, :]
        for x in range(reach):
            low = SIDE[1] * pad_ref[0, x, 7:15, :]
            high = SIDE[1] * pad_ref[1, x, 1:9, :]
            for k in range(2, REACH + 1):
                low = low + SIDE[k] * pad_ref[0, x, 8 - k : 16 - k, :]
                high = high + SIDE[k] * pad_ref[1, x, k : 8 + k, :]
            total = h_ref[f, x] + inner_ref[f, x]
            middle = [total[8 : ny - 8]] if ny > 16 else []
            first, last = total[0:8] + low, total[ny - 8 : ny] + high
            h_ref[f, x] = jnp.concatenate([first] + middle + [last], axis=0)
            if x < owned:
                u = jnp.concatenate([first + low] + middle + [last + 3.0 * high], axis=0)
                spot = pl.ds(x * ny, ny)
                edge_ref[spot, :] = gather_edges(edge_ref[spot, :], f, u)

    cuts = [fields * n // 4 for n in range(5)]
    for f in range(cuts[0], cuts[1]):
        border(f)
    local = jnp.concatenate(
        [zbelow_ref[after : after + REACH, 0:LANES]] * fields
        + [zabove_ref[after : after + REACH, 0:LANES]] * fields,
        axis=0,
    )
    image = image + local * near
    y = lax.broadcasted_iota(jnp.int32, (2 * rows, LANES), 1) % ny
    width = cx * ny
    for k in range(1, REACH + 1):
        sides = pltpu.roll(outer, ny * k, 1) + pltpu.roll(outer, width - ny * k, 1)
        sides = sides[:, 0:LANES] + jnp.where(y >= k, pltpu.roll(near, k, 1), 0.0)
        sides = sides + jnp.where(y < ny - k, pltpu.roll(near, LANES - k, 1), 0.0)
        image = image + SIDE[k] * sides
    for f in range(cuts[1], cuts[2]):
        border(f)
    reached = mul(back_ref[...], wide_right(jnp.concatenate([image, near], axis=0)))
    for f in range(cuts[2], cuts[3]):
        border(f)
    turned = around(reached[2 * rows : 4 * rows], ny)
    for f in range(cuts[3], cuts[4]):
        border(f)

    for s in range(srcs):
        values = [h_ref[f].reshape(reach * ny, nz) for f in (s, srcs + s)]
        along = mul(pairs_ref[...], jnp.concatenate([wide_right(v) for v in values], axis=1))
        for part in range(2):
            f = part * srcs + s
            own = values[part][0 : owned * ny]
            step = mul(wide_left(own), half_ref[...]) + along[:, part * nz : (part + 1) * nz]
            step_ref[f] = step.reshape(owned, ny, nz)
    for s in range(srcs):
        total = [jnp.zeros((ny, nz), jnp.float32) for _ in range(6)]
        for x in range(owned):
            local = pot_ref[x]
            b = (b_ref[s, x], b_ref[srcs + s, x])
            h = (h_ref[s, x], h_ref[srcs + s, x])
            g = [step_ref[part * srcs + s, x] + local * h[part] for part in range(2)]
            squares = (h[0] * h[0] - h[1] * h[1], h[0] * h[1])
            terms = product(b, h) + squares + product(h, g)
            total = [t + v for t, v in zip(total, terms)]
        for i in range(2, 8):
            value = fold(total[i - 2])
            if i == 5:
                value = 2.0 * value
            acc_ref[i * srcs + s : i * srcs + s + 1, :] = value

    acc_ref[0 : 2 * srcs, :] = base_ref[...]
    gathered = edge_ref[...].T
    part = rows // 2
    both = [0.0, 0.0]
    for side in range(2):
        at = (1 - side) * REACH + REACH
        u = jnp.concatenate(
            [gathered[4 * REACH * f + at : 4 * REACH * f + at + REACH] for f in range(fields)], axis=0
        )
        base = side * rows
        for left, right in ((u, reached), (edges_ref[base : base + rows], turned)):
            terms = product(
                (left[0:part], left[part:rows]), (right[base : base + part], right[base + part : base + rows])
            )
            both = [t + v for t, v in zip(both, terms)]
    for c in range(2):
        for s in range(srcs):
            at = (6 + c) * srcs + s
            acc_ref[at : at + 1, :] = acc_ref[at : at + 1, :] + fold(both[c][s * REACH : (s + 1) * REACH])


def tail_kernel(owned, b_ref, h_ref, above_ref, more_ref, both_ref, sums_ref, out_ref, acc_ref, far_ref, pull_ref):
    fields, reach, ny, nz = h_ref.shape
    srcs = fields // 2
    for f in range(fields):
        at = f * reach * REACH
        far_ref[f] = mul(wide_left(above_ref[at : at + owned * REACH, :]), both_ref[...])

    quad_row = lax.broadcasted_iota(jnp.int32, (8, nz), 0) % REACH
    early = lax.broadcasted_iota(jnp.int32, (8, nz), 0) < REACH

    def top(ref, f, x):
        return jnp.where(early, pltpu.roll(ref[f, x, ny - 8 : ny, :], REACH, 0), ref[f, x + 1, ny - 8 : ny, :])

    def lowered(lower, upper, k):
        if k == REACH:
            return lower
        return jnp.where(quad_row >= k, pltpu.roll(upper, k, 0), pltpu.roll(lower, REACH + k, 0))

    def raised(lower, upper, k):
        if k == REACH:
            return upper
        return jnp.where(quad_row < REACH - k, pltpu.roll(lower, 8 - k, 0), pltpu.roll(upper, REACH - k, 0))

    for f in range(fields):
        for x in range(0, reach, 2):
            own = top(h_ref, f, x)
            pull = SIDE[REACH] * own
            for k in range(1, REACH):
                pull = pull + SIDE[k] * jnp.where(quad_row < k, pltpu.roll(own, REACH + k, 0), 0.0)
            at = (f * reach + x) * REACH
            pull_ref[at : at + 8, :] = pull

    acc_ref[...] = sums_ref[...]
    for s in range(srcs):
        cross = [jnp.zeros((8, nz), jnp.float32) for _ in range(2)]
        for x in range(0, owned, 2):
            at = (fields * owned + x) * REACH
            local = more_ref[at : at + 8, :]
            left, right, first, pulls = [], [], [], []
            for part in range(2):
                f = part * srcs + s
                at = (f * reach + x) * REACH
                own = top(b_ref, f, x)
                first_layers = above_ref[at : at + 8, :]
                start = (f * owned + x) * REACH
                more = more_ref[start : start + 8, :]
                value = far_ref[f, x * REACH : x * REACH + 8, :] + local * first_layers
                pull = 0.0
                for k in range(1, REACH + 1):
                    sides = above_ref[at + k * REACH : at + k * REACH + 8, :]
                    sides = sides + raised(first_layers, more, k) + lowered(own, first_layers, k)
                    value = value + SIDE[k] * sides
                    pull = pull + SIDE[k] * pull_ref[at + k * REACH : at + k * REACH + 8, :]
                left.append(pull_ref[at : at + 8, :])
                right.append(value)
                first.append(first_layers)
                pulls.append(pull)
            for c, (one, two) in enumerate(zip(product(left, right), product(first, pulls))):
                cross[c] = cross[c] + (one + two)
        for c in range(2):
            at = (6 + c) * srcs + s
            acc_ref[at : at + 1, :] = acc_ref[at : at + 1, :] + 2.0 * fold(cross[c])

    column = jnp.sum(acc_ref[...], axis=1, keepdims=True)
    row = lax.broadcasted_iota(jnp.int32, acc_ref.shape, 0)
    lane = lax.broadcasted_iota(jnp.int32, acc_ref.shape, 1)
    out_ref[...] = jnp.broadcast_to(fold(jnp.where(row == lane, column, 0.0)), out_ref.shape)


def complex_mul(left, right):
    return (left[0] * right[0] - left[1] * right[1], left[0] * right[1] + left[1] * right[0])


def complex_div(left, right):
    norm_sq = right[0] * right[0] + right[1] * right[1]
    return (
        (left[0] * right[0] + left[1] * right[1]) / norm_sq,
        (left[1] * right[0] - left[0] * right[1]) / norm_sq,
    )


def output_kernel(tot_ref, table_ref, b_ref, h_ref, out_hbm, coef_ref, buf_ref, sems):
    fields, _, ny, nz = b_ref.shape
    srcs = fields // 2
    planes = buf_ref.shape[3]
    shape = (srcs, LANES)
    wide = jnp.broadcast_to(fold(tot_ref[...]), (8 * srcs, LANES))
    row = lax.broadcasted_iota(jnp.int32, wide.shape, 0)
    lane = lax.broadcasted_iota(jnp.int32, wide.shape, 1)
    wide = jnp.broadcast_to(jnp.sum(jnp.where(row == lane, wide, 0.0), axis=1, keepdims=True), wide.shape)
    nu = [
        (wide[2 * k * srcs : (2 * k + 1) * srcs], wide[(2 * k + 1) * srcs : (2 * k + 2) * srcs])
        for k in range(4)
    ]
    zeta = (
        jnp.broadcast_to(table_ref[0:1, :], shape),
        jnp.broadcast_to(table_ref[1:2, :], shape),
    )
    scaled = complex_mul(zeta, nu[0])
    alpha_first = complex_div(nu[0], (scaled[0] - nu[1][0], scaled[1] - nu[1][1]))
    mean = complex_div(nu[1], nu[0])
    t = complex_mul(mean, nu[1])
    spread2 = (nu[2][0] - t[0], nu[2][1] - t[1])
    t = complex_mul(mean, (nu[2][0] + spread2[0], nu[2][1] + spread2[1]))
    spread3 = (nu[3][0] - t[0], nu[3][1] - t[1])
    square = complex_mul(alpha_first, alpha_first)
    rho_next = complex_mul(square, spread2)
    beta = complex_div(rho_next, nu[0])
    first_part = complex_mul(zeta, rho_next)
    second = complex_mul(square, spread3)
    third = complex_div(complex_mul(beta, rho_next), alpha_first)
    alpha_next = complex_div(
        rho_next, (first_part[0] - second[0] - third[0], first_part[1] - second[1] - third[1])
    )
    t = complex_mul(alpha_first, mean)
    carried = complex_mul(alpha_next, (beta[0] - t[0], beta[1] - t[1]))
    on_source = (alpha_first[0] + carried[0], alpha_first[1] + carried[1])
    on_image = complex_mul(alpha_next, alpha_first)
    for k in range(MOMS):
        weight = (
            jnp.broadcast_to(table_ref[2 + 2 * k : 3 + 2 * k, :], shape),
            jnp.broadcast_to(table_ref[3 + 2 * k : 4 + 2 * k, :], shape),
        )
        for n, value in enumerate((on_source, on_image)):
            both = complex_mul(weight, value)
            for c in range(2):
                column = jnp.sum(both[c], axis=1, keepdims=True)
                coef_ref[4 * k + 2 * n + c, 0:srcs, :] = jnp.broadcast_to(column, shape)

    copies = []
    for s in range(srcs):
        for k in range(MOMS):
            c = [
                jnp.broadcast_to(coef_ref[4 * k + n, s : s + 1, :], (ny, nz)) for n in range(4)
            ]
            for x in range(planes):
                br, bi = b_ref[s, x], b_ref[srcs + s, x]
                hr, hi = h_ref[s, x], h_ref[srcs + s, x]
                buf_ref[s, k, 0, x] = c[0] * br - c[1] * bi + (c[2] * hr - c[3] * hi)
                buf_ref[s, k, 1, x] = c[0] * bi + c[1] * br + (c[2] * hi + c[3] * hr)
            copy = pltpu.make_async_copy(buf_ref.at[s, k], out_hbm.at[k, :, s], sems.at[s, k])
            copy.start()
            copies.append(copy)
    for copy in copies:
        copy.wait()


def ring(count, step):
    return [(i, (i + step) % count) for i in range(count)]


def shift(value, axis, step):
    return lax.ppermute(value, axis, ring(lax.axis_size(axis), step))


ANY = pl.BlockSpec(memory_space=pl.ANY)
HBM = pl.BlockSpec(memory_space=pltpu.HBM)
VMEM = pl.BlockSpec(memory_space=pltpu.VMEM)
SMEM = pl.BlockSpec(memory_space=pltpu.SMEM)


def shaped(*dims):
    return jax.ShapeDtypeStruct(dims, jnp.float32)


def small(mib):
    return pltpu.CompilerParams(vmem_limit_bytes=mib << 20)


def cost(flops, nbytes):
    return pl.CostEstimate(flops=flops, bytes_accessed=nbytes, transcendentals=0)


def per_device(source_real, source_imag, potential, center, radius):
    srcs, cx, ny, nz = source_real.shape
    fields = 2 * srcs
    py, pz, quads = lax.axis_size("py"), lax.axis_size("pz"), lax.axis_size("quad")
    owned = cx // quads
    reach = min(cx, owned + REACH)
    cells = reach * ny * nz
    rows = fields * REACH

    source_real, source_imag, potential = (
        pltpu.with_memory_space_constraint(a, pltpu.HBM)
        for a in (source_real, source_imag, potential)
    )
    part = shaped(fields, reach, ny, nz)
    flat = shaped(rows + rows // 2 + 2 * REACH, cx * ny)
    b, pot, up, down, far, zup, zdown = pl.pallas_call(
        functools.partial(load_kernel, owned),
        out_shape=(
            shaped(fields, cx, ny, nz),
            shaped(cx, ny, nz),
            shaped(fields * reach * REACH, nz),
            shaped(fields * reach * REACH, nz),
            shaped((fields + 1) * owned * REACH, nz),
            flat,
            flat,
        ),
        in_specs=[HBM] * 3,
        out_specs=(VMEM,) * 7,
        scratch_shapes=[
            pltpu.VMEM((fields, 2 * nz, nz), jnp.bfloat16),
            pltpu.SemaphoreType.DMA((3, quads)),
        ],
        compiler_params=small(8),
        name="load",
    )(source_real, source_imag, potential)
    above = shift(down, "py", -1)
    below = shift(up, "py", 1)
    zabove = shift(zdown, "pz", -1)
    zbelow = shift(zup, "pz", 1)
    more = shift(far, "py", -1)

    half = lambda *dims: jax.ShapeDtypeStruct(dims, jnp.bfloat16)
    inner, *weights = pl.pallas_call(
        functools.partial(inner_kernel, owned),
        out_shape=(
            part,
            half(3 * nz, nz),
            half(3 * nz, nz),
            half(2 * rows, 24 * rows),
            half(4 * rows, 12 * rows),
            half(fields, 6 * rows, nz),
            half(owned * ny, 3 * reach * ny),
            shaped(2 * rows, LANES),
            shaped(2 * srcs, nz),
        ),
        in_specs=[VMEM] * 4,
        out_specs=(VMEM,) * 9,
        scratch_shapes=[pltpu.VMEM((reach, ny + 16, nz), jnp.float32)],
        compiler_params=small(12),
        cost_estimate=cost(fields * cells * 60, fields * cells * 12),
        name="inner",
    )(b, pot, zup, zdown)

    both, *weights = weights
    image, sums = pl.pallas_call(
        functools.partial(main_kernel, owned),
        out_shape=(part, shaped(8 * srcs, nz)),
        in_specs=[VMEM] * 16,
        out_specs=(VMEM,) * 2,
        scratch_shapes=[
            pltpu.VMEM((2, reach, 16, nz), jnp.float32),
            pltpu.VMEM((LANES, nz), jnp.float32),
            pltpu.VMEM((fields, owned, ny, nz), jnp.float32),
        ],
        compiler_params=small(12),
        cost_estimate=cost(fields * cells * 60, fields * cells * 12),
        name="main",
    )(b, pot, inner, below, above, zup, zdown, zbelow, zabove, *weights)

    partial = pl.pallas_call(
        functools.partial(tail_kernel, owned),
        out_shape=shaped(quads * py * pz, LANES),
        in_specs=[VMEM] * 6,
        out_specs=VMEM,
        scratch_shapes=[
            pltpu.VMEM((8 * srcs, nz), jnp.float32),
            pltpu.VMEM((fields, owned * REACH, nz), jnp.float32),
            pltpu.VMEM((fields * reach * REACH, nz), jnp.float32),
        ],
        compiler_params=small(8),
        name="tail",
    )(b, image, above, more, both, sums)

    total = lax.all_to_all(partial, ("quad", "py", "pz"), 0, 0)

    table = jnp.asarray(phase_table())
    row = lax.broadcasted_iota(jnp.int32, table.shape, 0)
    table = radius * table + jnp.where(row == 0, center - MIDDLE, 0.0)
    return pl.pallas_call(
        output_kernel,
        out_shape=shaped(MOMS, 2, srcs, owned, ny, nz),
        in_specs=[VMEM] * 4,
        out_specs=HBM,
        scratch_shapes=[
            pltpu.VMEM((4 * MOMS, 8, LANES), jnp.float32),
            pltpu.VMEM((srcs, MOMS, 2, owned, ny, nz), jnp.float32),
            pltpu.SemaphoreType.DMA((srcs, MOMS)),
        ],
        compiler_params=small(12),
        name="output",
    )(total, table, b, image)


def solution(mesh):
    in_specs = (P(None, None, "py", "pz"), P(None, None, "py", "pz"), P(None, "py", "pz"), P(), P())
    out_specs = P(None, None, None, "quad", "py", "pz")

    return jax.shard_map(
        per_device, mesh=mesh, in_specs=in_specs, out_specs=out_specs, check_vma=False
    )
```

```python
import functools
import math

import jax
import jax.numpy as jnp
import numpy as np
from jax import lax
from jax.experimental import pallas as pl
from jax.experimental.pallas import tpu as pltpu
from jax.sharding import PartitionSpec as P


QPTS = 8
MOMS = 4
REACH = 4
LANES = 128

stencil_weights = (-205.0 / 72.0, 8.0 / 5.0, -1.0 / 5.0, 8.0 / 315.0, -1.0 / 560.0)
DIAG = -1.5 * stencil_weights[0]
MIDDLE = 5.25
SIDE = tuple(-0.5 * w for w in stencil_weights)


def band(shape, offset, signs, scale=1.0):
    step = offset + lax.broadcasted_iota(jnp.int32, shape, 0) - lax.broadcasted_iota(jnp.int32, shape, 1)
    out = jnp.zeros(shape, jnp.float32)
    for k in range(1, REACH + 1):
        for sign in signs:
            out = jnp.where(step == sign * k, scale * SIDE[k], out)
    return out


def split(value):
    high = value.astype(jnp.bfloat16)
    return high, (value - high.astype(jnp.float32)).astype(jnp.bfloat16)


def wide_left(value):
    high, low = split(value)
    return jnp.concatenate([high, low, high], axis=1)


def wide_right(value):
    high, low = split(value)
    return jnp.concatenate([high, high, low], axis=0)


def mul(left, right):
    return lax.dot_general(left, right, (((1,), (0,)), ((), ())), preferred_element_type=jnp.float32)


def gather_edges(gathered, f, value):
    lane = lax.broadcasted_iota(jnp.int32, value.shape, 1)
    moved = pltpu.roll(value, 4 * REACH * f + 2 * REACH, 1)
    return jnp.where(lane // (4 * REACH) == f, moved, gathered)


def load_kernel(
    owned, re_hbm, im_hbm, pot_hbm, b_ref, pot_ref, up_ref, down_ref, far_ref, zup_ref, zdown_ref, pick_ref, sems
):
    fields, cx, ny, nz = b_ref.shape
    srcs = fields // 2
    parts = cx // owned
    reach = up_ref.shape[0] // (fields * REACH)
    first = lax.axis_index("quad")
    copies = []
    for f in range(fields + 1):
        source = pot_hbm if f == fields else (re_hbm, im_hbm)[f // srcs].at[f % srcs]
        target = pot_ref if f == fields else b_ref.at[f]
        group = []
        for j in range(parts):
            at = pl.multiple_of(lax.rem(first + j, parts) * owned, owned)
            group.append(
                pltpu.make_async_copy(
                    source.at[pl.ds(at, owned)], target.at[pl.ds(j * owned, owned)], sems.at[f, j]
                )
            )
        copies.append(group)
    for group in copies:
        for copy in group:
            copy.start()
    shape = (2 * nz, nz)
    layer = lax.broadcasted_iota(jnp.int32, shape, 0) % nz
    lane = lax.broadcasted_iota(jnp.int32, shape, 1)
    spot = lax.rem(layer + 2 * REACH, nz)
    for f in range(fields):
        chosen = (spot < 4 * REACH) & (lane == spot + 4 * REACH * f)
        pick_ref[f] = jnp.where(chosen, 1.0, 0.0).astype(jnp.bfloat16)
    for f in range(fields):
        for copy in copies[f]:
            copy.wait()
        for x in range(reach):
            at = (f * reach + x) * REACH
            up_ref[at : at + REACH, :] = b_ref[f, x, ny - REACH : ny, :]
            down_ref[at : at + REACH, :] = b_ref[f, x, 0:REACH, :]
        for x in range(owned):
            at = (f * owned + x) * REACH
            far_ref[at : at + REACH, :] = b_ref[f, x, REACH : 2 * REACH, :]
    for copy in copies[fields]:
        copy.wait()
    pot_ref[...] = pot_ref[...] + (DIAG - MIDDLE)
    for x in range(owned):
        at = (fields * owned + x) * REACH
        far_ref[at : at + REACH, :] = pot_ref[x, 0:REACH, :]
    turned = pltpu.roll(pot_ref[...].reshape(cx * ny, nz), 2 * REACH, 1).T
    rows = fields * REACH
    after = rows + rows // 2
    zup_ref[after : after + REACH, :] = turned[REACH : 2 * REACH]
    zup_ref[after + REACH : after + 2 * REACH, :] = turned[0:REACH]
    zdown_ref[after : after + 2 * REACH, :] = turned[2 * REACH : 4 * REACH]
    pieces = [split(b_ref[f].reshape(cx * ny, nz)) for f in range(fields)]
    wide = jnp.concatenate([half for pair in pieces for half in pair], axis=1)
    turned = mul(wide, pick_ref[...].reshape(2 * fields * nz, nz)).T
    for f in range(fields):
        at = 4 * REACH * f
        low, high = f * REACH, (f + 1) * REACH
        zup_ref[low:high, :] = turned[at + REACH : at + 2 * REACH]
        zdown_ref[low:high, :] = turned[at + 2 * REACH : at + 3 * REACH]
        side, spot = f // srcs * LANES, rows + f % srcs * REACH
        lanes = slice(side, side + LANES)
        zup_ref[spot : spot + REACH, lanes] = turned[at : at + REACH, 0:LANES]
        zdown_ref[spot : spot + REACH, lanes] = turned[at + 3 * REACH : at + 4 * REACH, 0:LANES]


def phase_table():
    lane = np.arange(LANES)
    angle = 2.0 * math.pi * (lane % QPTS + 0.5) / QPTS
    rows = [np.cos(angle), np.sin(angle)]
    for k in range(1, MOMS + 1):
        rows.append(np.where(lane < QPTS, np.cos(k * angle), 0.0) / QPTS)
        rows.append(np.where(lane < QPTS, np.sin(k * angle), 0.0) / QPTS)
    rows += [np.zeros(LANES)] * (-len(rows) % 8)
    return np.stack(rows).astype(np.float32)


def links(row_at, col_at, row_field, col_field):
    step = jnp.abs(row_at - col_at)
    out = jnp.zeros(step.shape, jnp.float32)
    for k in range(1, REACH + 1):
        out = jnp.where((step == k) & (row_field == col_field), SIDE[k], out)
    return out


def layer_of(index, starts, rows):
    layer = jnp.full(index.shape, 1 << 20, jnp.int32)
    for n, start in enumerate(starts):
        layer = jnp.where(index // rows == n, start + index % REACH, layer)
    return layer, index % rows // REACH


def around(value, ny):
    y = lax.broadcasted_iota(jnp.int32, value.shape, 1) % ny
    width = value.shape[1]
    out = jnp.zeros(value.shape, jnp.float32)
    for k in range(1, REACH + 1):
        sides = jnp.where(y >= ny - k, pltpu.roll(value, ny - k, 1), 0.0)
        sides = sides + jnp.where(y < k, pltpu.roll(value, width + k - ny, 1), 0.0)
        out = out + SIDE[k] * sides
    return out


def places(planes, rows, layers):
    grid = np.meshgrid(np.asarray(planes), np.asarray(rows), np.asarray(layers), indexing="ij")
    return np.stack([g.reshape(-1) for g in grid])


def couple(to, of, up_planes, rows=True):
    step = of[:, None, :] - to[:, :, None]
    out = np.zeros(step.shape[1:])
    for k in range(1, REACH + 1):
        if rows:
            out[(step[0] == 0) & (np.abs(step[1]) == k) & (step[2] == 0)] = SIDE[k]
        out[(step[0] == 0) & (step[1] == 0) & (np.abs(step[2]) == k)] = SIDE[k]
        if up_planes:
            out[(step[0] == k) & (step[1] == 0) & (step[2] == 0)] = SIDE[k]
    return out


def halves(matrix):
    matrix = np.asarray(matrix, np.float32)
    high = matrix.astype(jnp.bfloat16)
    return high, (matrix - high.astype(np.float32)).astype(jnp.bfloat16)


def table_left(matrix):
    high, low = halves(matrix)
    return np.concatenate([high, low, high], axis=1)


def above_tables(owned, reach, ny):
    four = np.arange(REACH)
    over = places(np.arange(reach), ny + four, [0])
    target = places(np.arange(owned), ny + four, [0])
    sources = [
        over,
        places(np.arange(owned), ny + REACH + four, [0]),
        places(np.arange(owned), ny - REACH + four, [0]),
    ]
    image = couple(target, np.concatenate(sources, axis=1), True)
    pull = couple(over, places(np.arange(reach), ny - REACH + four, [0]), False)
    chain = couple(target, over, True, rows=False) @ pull
    return table_left(image), table_left(np.concatenate([pull[: owned * REACH], chain], 0))


def inner_kernel(
    owned,
    b_ref,
    pot_ref,
    zup_ref,
    zdown_ref,
    image_hbm,
    pull_hbm,
    out_ref,
    both_ref,
    half_ref,
    beyond_ref,
    back_ref,
    fix_ref,
    pairs_ref,
    edges_ref,
    base_ref,
    top_ref,
    image_ref,
    pull_ref,
    pad_ref,
    sems,
):
    fields, cx, ny, nz = b_ref.shape
    srcs = fields // 2
    copies = (
        pltpu.make_async_copy(image_hbm, image_ref, sems.at[0]),
        pltpu.make_async_copy(pull_hbm, pull_ref, sems.at[1]),
    )
    for copy in copies:
        copy.start()
    reach = out_ref.shape[1]
    rows = fields * REACH
    both_ref[...] = wide_right(band((nz, nz), 0, (1, -1)))
    half_ref[...] = wide_right(band((nz, nz), 0, (1,), 2.0))
    for f in range(fields):
        own = b_ref[f, 0:reach].reshape(reach * ny, nz)
        out_ref[f] = mul(wide_left(own), both_ref[...]).reshape(reach, ny, nz)
    zero = jnp.zeros((reach, 8, nz), jnp.float32)
    pad_ref[:, 0:8, :] = zero
    pad_ref[:, 8 + ny : 16 + ny, :] = zero

    def field(f, _):
        pad_ref[:, 8 : 8 + ny, :] = b_ref[f, 0:reach]
        for x in range(reach):
            total = out_ref[f, x] + pot_ref[x] * b_ref[f, x]
            for k in range(1, REACH + 1):
                sides = b_ref[f, (x + k) % cx] + b_ref[f, (x - k) % cx]
                sides = sides + pad_ref[x, 8 + k : 8 + k + ny, :]
                sides = sides + pad_ref[x, 8 - k : 8 - k + ny, :]
                total = total + SIDE[k] * sides
            out_ref[f, x] = total
        return 0

    lax.fori_loop(0, fields, field, 0)

    shape = (owned * ny, reach * ny)
    to = lax.broadcasted_iota(jnp.int32, shape, 0)
    of = lax.broadcasted_iota(jnp.int32, shape, 1)
    planes, row_steps = of // ny - to // ny, of % ny - to % ny
    pairs = jnp.zeros(shape, jnp.float32)
    for k in range(1, REACH + 1):
        hit = ((planes == k) & (row_steps == 0)) | ((planes == 0) & (row_steps == k))
        pairs = jnp.where(hit, 2.0 * SIDE[k], pairs)
    pairs_ref[...] = wide_left(pairs)

    shape = (2 * rows, 8 * rows)
    row_at, row_field = layer_of(lax.broadcasted_iota(jnp.int32, shape, 0), (-REACH, nz), rows)
    starts = (0, nz - REACH, -REACH, -2 * REACH, nz, nz + REACH)
    col_at, col_field = layer_of(lax.broadcasted_iota(jnp.int32, shape, 1), starts, rows)
    beyond_ref[...] = wide_left(links(row_at, col_at, row_field, col_field))
    shape = (4 * rows, 4 * rows)
    row = lax.broadcasted_iota(jnp.int32, shape, 0)
    col = lax.broadcasted_iota(jnp.int32, shape, 1)
    row_at, row_field = layer_of(row % (2 * rows), (0, nz - REACH), rows)
    col_at, col_field = layer_of(col % (2 * rows), (-REACH, nz), rows)
    same = row // (2 * rows) == col // (2 * rows)
    back_ref[...] = wide_left(jnp.where(same, links(row_at, col_at, row_field, col_field), 0.0))
    shape = (2 * rows, nz)
    layer, owner = layer_of(lax.broadcasted_iota(jnp.int32, shape, 0), (-REACH, nz), rows)
    cell = lax.broadcasted_iota(jnp.int32, shape, 1)
    for f in range(fields):
        fix_ref[f] = wide_right(links(layer, cell, owner, f))
    lane = lax.broadcasted_iota(jnp.int32, (2 * rows, LANES), 1)
    weight = jnp.where(lane < owned * ny, jnp.where(lane % ny >= ny // 2, 3.0, 1.0), 0.0)
    edges = jnp.concatenate([zdown_ref[0:rows, 0:LANES], zup_ref[0:rows, 0:LANES]], axis=0)
    edges_ref[...] = around(edges, ny) * weight
    for s in range(srcs):
        re = im = jnp.zeros((ny, nz), jnp.float32)
        for x in range(owned):
            br, bi = b_ref[s, x], b_ref[srcs + s, x]
            re = re + (br * br - bi * bi)
            im = im + br * bi
        base_ref[s : s + 1, :] = fold(re)
        base_ref[srcs + s : srcs + s + 1, :] = fold(2.0 * im)
    for f in range(fields):
        for x in range(owned):
            at = (f * owned + x) * REACH
            top_ref[at : at + REACH, :] = b_ref[f, x, ny - REACH : ny, :]
    for copy in copies:
        copy.wait()


def fold(value):
    return jnp.sum(value, axis=0, keepdims=True)


def product(left, right):
    return left[0] * right[0] - left[1] * right[1], left[0] * right[1] + left[1] * right[0]


def main_kernel(
    owned,
    b_ref,
    pot_ref,
    inner_ref,
    below_ref,
    above_ref,
    zup_ref,
    zdown_ref,
    zbelow_ref,
    zabove_ref,
    half_ref,
    beyond_ref,
    back_ref,
    fix_ref,
    pairs_ref,
    edges_ref,
    base_ref,
    h_ref,
    acc_ref,
    last_ref,
    pad_ref,
    edge_ref,
    step_ref,
):
    fields, reach, ny, nz = inner_ref.shape
    cx = b_ref.shape[1]
    srcs = fields // 2
    rows = fields * REACH
    after = rows + rows // 2

    outer = jnp.concatenate([zbelow_ref[0:rows], zabove_ref[0:rows]], axis=0)
    high = outer.astype(jnp.bfloat16).astype(jnp.float32)
    wide = jnp.concatenate([high, outer - high, high], axis=0).T[0 : reach * ny].astype(jnp.bfloat16)
    near = outer[:, 0:LANES]

    def second(ref):
        return [ref[rows:after, 0:LANES], ref[rows:after, LANES : 2 * LANES]]

    stack = jnp.concatenate(
        [zdown_ref[0:rows, 0:LANES], zup_ref[0:rows, 0:LANES], near[0:rows]]
        + second(zbelow_ref)
        + [near[rows : 2 * rows]]
        + second(zabove_ref)
        + [near],
        axis=0,
    )
    image = mul(beyond_ref[...], wide_right(stack))
    for f in range(fields):
        h_ref[f] = mul(wide, fix_ref[f]).reshape(reach, ny, nz)
    zero = jnp.zeros((reach, 16, nz), jnp.float32)
    pad_ref[0] = zero
    pad_ref[1] = zero
    edge_ref[...] = jnp.zeros(edge_ref.shape, jnp.float32)

    def border(f):
        for x in range(reach):
            at = (f * reach + x) * REACH
            pad_ref[0, x, 8 - REACH : 8, :] = below_ref[at : at + REACH, :]
            pad_ref[1, x, 8 : 8 + REACH, :] = above_ref[at : at + REACH, :]
        for x in range(reach):
            low = SIDE[1] * pad_ref[0, x, 7:15, :]
            high = SIDE[1] * pad_ref[1, x, 1:9, :]
            for k in range(2, REACH + 1):
                low = low + SIDE[k] * pad_ref[0, x, 8 - k : 16 - k, :]
                high = high + SIDE[k] * pad_ref[1, x, k : 8 + k, :]
            total = h_ref[f, x] + inner_ref[f, x]
            middle = [total[8 : ny - 8]] if ny > 16 else []
            first, last = total[0:8] + low, total[ny - 8 : ny] + high
            h_ref[f, x] = jnp.concatenate([first] + middle + [last], axis=0)
            at = (f * reach + x) * REACH
            last_ref[at : at + REACH, :] = last[8 - REACH : 8]
            if x < owned:
                u = jnp.concatenate([first + low] + middle + [last + 3.0 * high], axis=0)
                spot = pl.ds(x * ny, ny)
                edge_ref[spot, :] = gather_edges(edge_ref[spot, :], f, u)

    cuts = [fields * n // 4 for n in range(5)]
    for f in range(cuts[0], cuts[1]):
        border(f)
    local = jnp.concatenate(
        [zbelow_ref[after : after + REACH, 0:LANES]] * fields
        + [zabove_ref[after : after + REACH, 0:LANES]] * fields,
        axis=0,
    )
    image = image + local * near
    y = lax.broadcasted_iota(jnp.int32, (2 * rows, LANES), 1) % ny
    width = cx * ny
    for k in range(1, REACH + 1):
        sides = pltpu.roll(outer, ny * k, 1) + pltpu.roll(outer, width - ny * k, 1)
        sides = sides[:, 0:LANES] + jnp.where(y >= k, pltpu.roll(near, k, 1), 0.0)
        sides = sides + jnp.where(y < ny - k, pltpu.roll(near, LANES - k, 1), 0.0)
        image = image + SIDE[k] * sides
    for f in range(cuts[1], cuts[2]):
        border(f)
    reached = mul(back_ref[...], wide_right(jnp.concatenate([image, near], axis=0)))
    for f in range(cuts[2], cuts[3]):
        border(f)
    turned = around(reached[2 * rows : 4 * rows], ny)
    for f in range(cuts[3], cuts[4]):
        border(f)

    for s in range(srcs):
        values = [h_ref[f].reshape(reach * ny, nz) for f in (s, srcs + s)]
        along = mul(pairs_ref[...], jnp.concatenate([wide_right(v) for v in values], axis=1))
        for part in range(2):
            f = part * srcs + s
            own = values[part][0 : owned * ny]
            step = mul(wide_left(own), half_ref[...]) + along[:, part * nz : (part + 1) * nz]
            step_ref[f] = step.reshape(owned, ny, nz)
    for s in range(srcs):
        total = [jnp.zeros((ny, nz), jnp.float32) for _ in range(6)]
        for x in range(owned):
            local = pot_ref[x]
            b = (b_ref[s, x], b_ref[srcs + s, x])
            h = (h_ref[s, x], h_ref[srcs + s, x])
            g = [step_ref[part * srcs + s, x] + local * h[part] for part in range(2)]
            squares = (h[0] * h[0] - h[1] * h[1], h[0] * h[1])
            terms = product(b, h) + squares + product(h, g)
            total = [t + v for t, v in zip(total, terms)]
        for i in range(2, 8):
            value = fold(total[i - 2])
            if i == 5:
                value = 2.0 * value
            acc_ref[i * srcs + s : i * srcs + s + 1, :] = value

    acc_ref[0 : 2 * srcs, :] = base_ref[...]
    gathered = edge_ref[...].T
    part = rows // 2
    both = [0.0, 0.0]
    for side in range(2):
        at = (1 - side) * REACH + REACH
        u = jnp.concatenate(
            [gathered[4 * REACH * f + at : 4 * REACH * f + at + REACH] for f in range(fields)], axis=0
        )
        base = side * rows
        for left, right in ((u, reached), (edges_ref[base : base + rows], turned)):
            terms = product(
                (left[0:part], left[part:rows]), (right[base : base + part], right[base + part : base + rows])
            )
            both = [t + v for t, v in zip(both, terms)]
    for c in range(2):
        for s in range(srcs):
            at = (6 + c) * srcs + s
            acc_ref[at : at + 1, :] = acc_ref[at : at + 1, :] + fold(both[c][s * REACH : (s + 1) * REACH])


def tail_kernel(
    owned,
    above_ref,
    more_ref,
    top_ref,
    last_ref,
    both_ref,
    image_ref,
    pull_ref,
    sums_ref,
    out_ref,
    acc_ref,
):
    cut = owned * REACH
    fields = top_ref.shape[0] // cut
    span = last_ref.shape[0] // fields
    nz = top_ref.shape[1]
    srcs = fields // 2

    def over(f):
        return jnp.concatenate(
            [
                above_ref[f * span : (f + 1) * span, :],
                more_ref[f * cut : (f + 1) * cut, :],
                top_ref[f * cut : (f + 1) * cut, :],
            ],
            axis=0,
        )

    def paired(table_ref, rows_of, s):
        parts = [wide_right(rows_of(part * srcs + s)) for part in range(2)]
        return mul(table_ref[...], jnp.concatenate(parts, axis=1))

    acc_ref[...] = sums_ref[...]
    local = more_ref[fields * cut : (fields + 1) * cut, :]
    for s in range(srcs):
        image = paired(image_ref, over, s)
        pull = paired(pull_ref, lambda f: last_ref[f * span : (f + 1) * span, :], s)
        left, right, first, pulls = [], [], [], []
        for part in range(2):
            at = (part * srcs + s) * span
            lanes = slice(part * nz, (part + 1) * nz)
            close = above_ref[at : at + cut, :]
            right.append(image[:, lanes] + mul(wide_left(close), both_ref[...]) + local * close)
            left.append(pull[0:cut, lanes])
            first.append(close)
            pulls.append(pull[cut : 2 * cut, lanes])
        for c, (one, two) in enumerate(zip(product(left, right), product(first, pulls))):
            at = (6 + c) * srcs + s
            acc_ref[at : at + 1, :] = acc_ref[at : at + 1, :] + 2.0 * fold(one + two)

    column = jnp.sum(acc_ref[...], axis=1, keepdims=True)
    row = lax.broadcasted_iota(jnp.int32, acc_ref.shape, 0)
    lane = lax.broadcasted_iota(jnp.int32, acc_ref.shape, 1)
    out_ref[...] = jnp.broadcast_to(fold(jnp.where(row == lane, column, 0.0)), out_ref.shape)


def complex_mul(left, right):
    return (left[0] * right[0] - left[1] * right[1], left[0] * right[1] + left[1] * right[0])


def complex_div(left, right):
    norm_sq = right[0] * right[0] + right[1] * right[1]
    return (
        (left[0] * right[0] + left[1] * right[1]) / norm_sq,
        (left[1] * right[0] - left[0] * right[1]) / norm_sq,
    )


def output_kernel(tot_ref, table_ref, b_ref, h_ref, out_hbm, coef_ref, buf_ref, sems):
    fields, _, ny, nz = b_ref.shape
    srcs = fields // 2
    planes = buf_ref.shape[3]
    shape = (srcs, LANES)
    wide = jnp.broadcast_to(fold(tot_ref[...]), (8 * srcs, LANES))
    row = lax.broadcasted_iota(jnp.int32, wide.shape, 0)
    lane = lax.broadcasted_iota(jnp.int32, wide.shape, 1)
    wide = jnp.broadcast_to(jnp.sum(jnp.where(row == lane, wide, 0.0), axis=1, keepdims=True), wide.shape)
    nu = [
        (wide[2 * k * srcs : (2 * k + 1) * srcs], wide[(2 * k + 1) * srcs : (2 * k + 2) * srcs])
        for k in range(4)
    ]
    zeta = (
        jnp.broadcast_to(table_ref[0:1, :], shape),
        jnp.broadcast_to(table_ref[1:2, :], shape),
    )
    scaled = complex_mul(zeta, nu[0])
    alpha_first = complex_div(nu[0], (scaled[0] - nu[1][0], scaled[1] - nu[1][1]))
    mean = complex_div(nu[1], nu[0])
    t = complex_mul(mean, nu[1])
    spread2 = (nu[2][0] - t[0], nu[2][1] - t[1])
    t = complex_mul(mean, (nu[2][0] + spread2[0], nu[2][1] + spread2[1]))
    spread3 = (nu[3][0] - t[0], nu[3][1] - t[1])
    square = complex_mul(alpha_first, alpha_first)
    rho_next = complex_mul(square, spread2)
    beta = complex_div(rho_next, nu[0])
    first_part = complex_mul(zeta, rho_next)
    second = complex_mul(square, spread3)
    third = complex_div(complex_mul(beta, rho_next), alpha_first)
    alpha_next = complex_div(
        rho_next, (first_part[0] - second[0] - third[0], first_part[1] - second[1] - third[1])
    )
    t = complex_mul(alpha_first, mean)
    carried = complex_mul(alpha_next, (beta[0] - t[0], beta[1] - t[1]))
    on_source = (alpha_first[0] + carried[0], alpha_first[1] + carried[1])
    on_image = complex_mul(alpha_next, alpha_first)
    for k in range(MOMS):
        weight = (
            jnp.broadcast_to(table_ref[2 + 2 * k : 3 + 2 * k, :], shape),
            jnp.broadcast_to(table_ref[3 + 2 * k : 4 + 2 * k, :], shape),
        )
        for n, value in enumerate((on_source, on_image)):
            both = complex_mul(weight, value)
            for c in range(2):
                column = jnp.sum(both[c], axis=1, keepdims=True)
                coef_ref[4 * k + 2 * n + c, 0:srcs, :] = jnp.broadcast_to(column, shape)

    copies = []
    for s in range(srcs):
        for k in range(MOMS):
            c = [
                jnp.broadcast_to(coef_ref[4 * k + n, s : s + 1, :], (ny, nz)) for n in range(4)
            ]
            for x in range(planes):
                br, bi = b_ref[s, x], b_ref[srcs + s, x]
                hr, hi = h_ref[s, x], h_ref[srcs + s, x]
                buf_ref[s, k, 0, x] = c[0] * br - c[1] * bi + (c[2] * hr - c[3] * hi)
                buf_ref[s, k, 1, x] = c[0] * bi + c[1] * br + (c[2] * hi + c[3] * hr)
            copy = pltpu.make_async_copy(buf_ref.at[s, k], out_hbm.at[k, :, s], sems.at[s, k])
            copy.start()
            copies.append(copy)
    for copy in copies:
        copy.wait()


def ring(count, step):
    return [(i, (i + step) % count) for i in range(count)]


def shift(value, axis, step):
    return lax.ppermute(value, axis, ring(lax.axis_size(axis), step))


ANY = pl.BlockSpec(memory_space=pl.ANY)
HBM = pl.BlockSpec(memory_space=pltpu.HBM)
VMEM = pl.BlockSpec(memory_space=pltpu.VMEM)
SMEM = pl.BlockSpec(memory_space=pltpu.SMEM)


def shaped(*dims):
    return jax.ShapeDtypeStruct(dims, jnp.float32)


def small(mib):
    return pltpu.CompilerParams(vmem_limit_bytes=mib << 20)


def cost(flops, nbytes):
    return pl.CostEstimate(flops=flops, bytes_accessed=nbytes, transcendentals=0)


def per_device(source_real, source_imag, potential, center, radius):
    srcs, cx, ny, nz = source_real.shape
    fields = 2 * srcs
    py, pz, quads = lax.axis_size("py"), lax.axis_size("pz"), lax.axis_size("quad")
    owned = cx // quads
    reach = min(cx, owned + REACH)
    cells = reach * ny * nz
    rows = fields * REACH

    source_real, source_imag, potential = (
        pltpu.with_memory_space_constraint(a, pltpu.HBM)
        for a in (source_real, source_imag, potential)
    )
    part = shaped(fields, reach, ny, nz)
    flat = shaped(rows + rows // 2 + 2 * REACH, cx * ny)
    b, pot, up, down, far, zup, zdown = pl.pallas_call(
        functools.partial(load_kernel, owned),
        out_shape=(
            shaped(fields, cx, ny, nz),
            shaped(cx, ny, nz),
            shaped(fields * reach * REACH, nz),
            shaped(fields * reach * REACH, nz),
            shaped((fields + 1) * owned * REACH, nz),
            flat,
            flat,
        ),
        in_specs=[HBM] * 3,
        out_specs=(VMEM,) * 7,
        scratch_shapes=[
            pltpu.VMEM((fields, 2 * nz, nz), jnp.bfloat16),
            pltpu.SemaphoreType.DMA((fields + 1, quads)),
        ],
        compiler_params=small(8),
        name="load",
    )(source_real, source_imag, potential)
    above = shift(down, "py", -1)
    below = shift(up, "py", 1)
    zabove = shift(zdown, "pz", -1)
    zbelow = shift(zup, "pz", 1)
    more = shift(far, "py", -1)

    tables = above_tables(owned, reach, ny)
    half = lambda *dims: jax.ShapeDtypeStruct(dims, jnp.bfloat16)
    inner, *weights = pl.pallas_call(
        functools.partial(inner_kernel, owned),
        out_shape=(
            part,
            half(3 * nz, nz),
            half(3 * nz, nz),
            half(2 * rows, 24 * rows),
            half(4 * rows, 12 * rows),
            half(fields, 6 * rows, nz),
            half(owned * ny, 3 * reach * ny),
            shaped(2 * rows, LANES),
            shaped(2 * srcs, nz),
            shaped(fields * owned * REACH, nz),
            *(jax.ShapeDtypeStruct(t.shape, t.dtype) for t in tables),
        ),
        in_specs=[VMEM] * 4 + [HBM] * 2,
        out_specs=(VMEM,) * 12,
        scratch_shapes=[
            pltpu.VMEM((reach, ny + 16, nz), jnp.float32),
            pltpu.SemaphoreType.DMA((2,)),
        ],
        compiler_params=small(12),
        cost_estimate=cost(fields * cells * 60, fields * cells * 12),
        name="inner",
    )(b, pot, zup, zdown, *(pltpu.with_memory_space_constraint(jnp.asarray(t), pltpu.HBM) for t in tables))

    both, *weights, top, image_table, pull_table = weights
    image, sums, last = pl.pallas_call(
        functools.partial(main_kernel, owned),
        out_shape=(part, shaped(8 * srcs, nz), shaped(fields * reach * REACH, nz)),
        in_specs=[VMEM] * 16,
        out_specs=(VMEM,) * 3,
        scratch_shapes=[
            pltpu.VMEM((2, reach, 16, nz), jnp.float32),
            pltpu.VMEM((LANES, nz), jnp.float32),
            pltpu.VMEM((fields, owned, ny, nz), jnp.float32),
        ],
        compiler_params=small(12),
        cost_estimate=cost(fields * cells * 60, fields * cells * 12),
        name="main",
    )(b, pot, inner, below, above, zup, zdown, zbelow, zabove, *weights)

    partial = pl.pallas_call(
        functools.partial(tail_kernel, owned),
        out_shape=shaped(quads * py * pz, LANES),
        in_specs=[VMEM] * 8,
        out_specs=VMEM,
        scratch_shapes=[pltpu.VMEM((8 * srcs, nz), jnp.float32)],
        compiler_params=small(8),
        name="tail",
    )(above, more, top, last, both, image_table, pull_table, sums)

    total = lax.all_to_all(partial, ("quad", "py", "pz"), 0, 0)

    table = jnp.asarray(phase_table())
    row = lax.broadcasted_iota(jnp.int32, table.shape, 0)
    table = radius * table + jnp.where(row == 0, center - MIDDLE, 0.0)
    return pl.pallas_call(
        output_kernel,
        out_shape=shaped(MOMS, 2, srcs, owned, ny, nz),
        in_specs=[VMEM] * 4,
        out_specs=HBM,
        scratch_shapes=[
            pltpu.VMEM((4 * MOMS, 8, LANES), jnp.float32),
            pltpu.VMEM((srcs, MOMS, 2, owned, ny, nz), jnp.float32),
            pltpu.SemaphoreType.DMA((srcs, MOMS)),
        ],
        compiler_params=small(12),
        name="output",
    )(total, table, b, image)


def solution(mesh):
    in_specs = (P(None, None, "py", "pz"), P(None, None, "py", "pz"), P(None, "py", "pz"), P(), P())
    out_specs = P(None, None, None, "quad", "py", "pz")

    return jax.shard_map(
        per_device, mesh=mesh, in_specs=in_specs, out_specs=out_specs, check_vma=False
    )
```
